32 devices in a mesh: dp: 8 (over z, y), mp: 4 (over x, core).
Axes of the slice: x: 2, y: 2, z: 4, core: 2. Of those that a mesh axis runs over, the one named last changes fastest.
Arguments:
- tokens: bfloat16 [16384, 1024], P(('dp', 'mp')), may hold values from -6 to 6
- memory: bfloat16 [16384, 1024], P(('dp', 'mp')), may hold values from -6 to 6
- cotangent: bfloat16 [16384, 1024], P(('dp', 'mp')), may hold values from -6 to 6
- target_lengths: int32 [16], P('dp'), may hold values from 1 to 1024, as said below
- memory_lengths: int32 [16], P('dp'), may hold values from 1 to 1024, as said below
- self_inputs: bfloat16 [3, 1024, 1024], P(None, None, 'mp'), may hold values from -0.176776695 to 0.176776695
- self_output: bfloat16 [1024, 1024], P('mp'), may hold values from -2 to 2
- cross_query: bfloat16 [1024, 1024], P(None, 'mp'), may hold values from -0.176776695 to 0.176776695
- cross_memory: bfloat16 [2, 1024, 1024], P(None, None, 'mp'), may hold values from -0.176776695 to 0.176776695
- cross_output: bfloat16 [1024, 1024], P('mp'), may hold values from -2 to 2
- feed_in: bfloat16 [1024, 4096], P(None, 'mp'), may hold values from -0.125 to 0.125
- feed_out: bfloat16 [4096, 1024], P('mp'), may hold values from -0.35355339 to 0.35355339
- proj_bias: bfloat16 [4, 1024], P(None, 'mp'), may hold values from -3 to 3
- feed_bias: bfloat16 [4096], P('mp'), may hold values from -3 to 3
- branch_bias: float32 [3, 1024], replicated, may hold values from -5 to 5
- norm_gain: float32 [3, 1024], replicated, may hold values from 0.25 to 1.75
- norm_shift: float32 [3, 1024], replicated, may hold values from -3 to 3
Outputs:
- block_out: bfloat16 [16384, 1024], P(('dp', 'mp'))
- grad_tokens: bfloat16 [16384, 1024], P(('dp', 'mp'))
- grad_memory: bfloat16 [16384, 1024], P(('dp', 'mp'))
- grad_self_inputs: float32 [3, 1024, 1024], P(None, None, 'mp')
- grad_self_output: float32 [1024, 1024], P('mp')
- grad_cross_query: float32 [1024, 1024], P(None, 'mp')
- grad_cross_memory: float32 [2, 1024, 1024], P(None, None, 'mp')
- grad_cross_output: float32 [1024, 1024], P('mp')
- grad_feed_in: float32 [1024, 4096], P(None, 'mp')
- grad_feed_out: float32 [4096, 1024], P('mp')
- grad_proj_bias: float32 [4, 1024], P(None, 'mp')
- grad_feed_bias: float32 [4096], P('mp')
- grad_branch_bias: float32 [3, 1024], P(None, 'mp')
- grad_norm_gain: float32 [3, 1024], P(None, 'mp')
- grad_norm_shift: float32 [3, 1024], P(None, 'mp')
The draws below stay inside these ranges and needn't reach their ends.
Inputs may be any that keep to these rules, and one draw needn't show every extreme that they name: `target_lengths`: real target rows of each sequence; rows beyond it are padding whose keys are masked. In every group of 2 sequences on one index of dp, one sequence has exactly 1024 rows. `memory_lengths`: real memory rows of each sequence; in every group of 2 sequences on one index of dp, one has exactly 1024 rows.
All inputs are finite; a program needn't handle non-finite values.
Results may differ from the reference program's by a relative error of at most 0.03.
Values may be sent and summed in bfloat16 or wider, within the bound.
A program may use at most 256 MiB of HBM per device.

```python
import math
import jax
import jax.numpy as jnp
from jax import lax

D = 1024
HEADS = 16
HEAD_DIM = 64
FF = 4096
LEN = 1024
MLEN = 1024
SEQ_GRP = 2
SEQS = 16
TOKENS = 16384
MTOK = 16384


def ragged_lengths(key, longest):
    draw_key, pick_key = jax.random.split(key)
    spread = jax.random.randint(draw_key, (SEQS,), 0, longest)
    lengths = longest - spread * spread // longest
    chosen = jax.random.randint(pick_key, (SEQS // SEQ_GRP,), 0, SEQ_GRP)
    position_in = jnp.arange(SEQS) % SEQ_GRP
    chosen_rows = jnp.repeat(chosen, SEQ_GRP)
    return jnp.where(position_in == chosen_rows, longest, lengths).astype(jnp.int32)


def draw_target_lengths(key, part):
    return ragged_lengths(jax.random.fold_in(key, 11), LEN)


def draw_memory_lengths(key, part):
    return ragged_lengths(jax.random.fold_in(key, 23), MLEN)


def clipped_normal(key, shape, scale, bound):
    values = jax.random.normal(key, shape, jnp.float32) * scale
    return jnp.clip(values, -bound, bound).astype(jnp.bfloat16)


def draw_tokens(key, part):
    return clipped_normal(jax.random.fold_in(key, 31), (TOKENS, D), 1.0, 6.0)


def draw_memory(key, part):
    return clipped_normal(jax.random.fold_in(key, 37), (MTOK, D), 1.0, 6.0)


def weight_draw(key, shape, fan_in):
    scale = fan_in ** (-0.5)
    return clipped_normal(key, shape, scale, 4.0 * scale)


def draw_self_inputs(key, part):
    return weight_draw(jax.random.fold_in(key, 41), (3, D, D), D // 2)


def draw_cross_query(key, part):
    return weight_draw(jax.random.fold_in(key, 43), (D, D), D // 2)


def draw_cross_memory(key, part):
    return weight_draw(jax.random.fold_in(key, 47), (2, D, D), D // 2)


def draw_self_output(key, part):
    return weight_draw(jax.random.fold_in(key, 53), (D, D), max(4, D // 256))


def draw_cross_output(key, part):
    return weight_draw(jax.random.fold_in(key, 59), (D, D), max(4, D // 256))


def draw_feed_in(key, part):
    return weight_draw(jax.random.fold_in(key, 61), (D, FF), D)


def draw_feed_out(key, part):
    return weight_draw(jax.random.fold_in(key, 67), (FF, D), FF // 32)


def block_levels(own_key, extent, cuts, smallest, top_value):
    level = 1.0
    for axis_at, parts in cuts:
        steps = jax.random.uniform(jax.random.fold_in(jax.random.fold_in(own_key, 6), axis_at), (parts,), jnp.float32, smallest / len(cuts), top_value / len(cuts))
        level = level * jnp.repeat(jnp.exp(steps), extent[axis_at] // parts).reshape((-1,) + (1,) * (len(extent) - 1 - axis_at))
    return level


def bell_draw(stream_key, extent, scale, limit, cuts=(), kind=jnp.bfloat16):
    drawn = jax.random.normal(stream_key, extent, jnp.float32) * scale
    if len(cuts) > 0:
        drawn = block_levels(stream_key, extent, cuts, -0.22, 0.18) * drawn
    return jnp.clip(drawn, min=-limit, max=limit).astype(kind)


def setup_inputs(seed: int = 0) -> dict:
    seeds = jax.random.split(jax.random.key(seed), 18)
    tokens = draw_tokens(jax.random.fold_in(seeds[17], 71), 0)
    memory = draw_memory(jax.random.fold_in(seeds[17], 71), 0)
    cotangent = bell_draw(seeds[2], (TOKENS, D), 1.0, 6.0, ((0, 32),))
    target_lengths = draw_target_lengths(jax.random.fold_in(seeds[17], 71), 0)
    memory_lengths = draw_memory_lengths(jax.random.fold_in(seeds[17], 71), 0)
    self_inputs = draw_self_inputs(jax.random.fold_in(seeds[17], 71), 0)
    self_output = draw_self_output(jax.random.fold_in(seeds[17], 71), 0)
    cross_query = draw_cross_query(jax.random.fold_in(seeds[17], 71), 0)
    cross_memory = draw_cross_memory(jax.random.fold_in(seeds[17], 71), 0)
    cross_output = draw_cross_output(jax.random.fold_in(seeds[17], 71), 0)
    feed_in = draw_feed_in(jax.random.fold_in(seeds[17], 71), 0)
    feed_out = draw_feed_out(jax.random.fold_in(seeds[17], 71), 0)
    proj_bias = bell_draw(seeds[12], (4, D), 0.5, 3.0, ((1, 4),))
    feed_bias = bell_draw(seeds[13], (FF,), 0.5, 3.0, ((0, 4),))
    branch_bias = bell_draw(seeds[14], (3, D), 1.0, 5.0, (), jnp.float32)
    norm_gain = jnp.clip(1.0 + 0.15 * jax.random.normal(seeds[15], (3, D), jnp.float32), 0.25, 1.75)
    norm_shift = bell_draw(seeds[16], (3, D), 0.5, 3.0, (), jnp.float32)
    return dict(tokens=tokens, memory=memory, cotangent=cotangent, target_lengths=target_lengths, memory_lengths=memory_lengths, self_inputs=self_inputs, self_output=self_output, cross_query=cross_query, cross_memory=cross_memory, cross_output=cross_output, feed_in=feed_in, feed_out=feed_out, proj_bias=proj_bias, feed_bias=feed_bias, branch_bias=branch_bias, norm_gain=norm_gain, norm_shift=norm_shift)


residual_scale = 300.0 ** 0.25
norm_epsilon = 1e-05
highest = lax.Precision.HIGHEST

@jax.custom_vjp
def low(v):
    return lax.optimization_barrier(v.astype(jnp.bfloat16)).astype(jnp.float32)

@jax.custom_vjp
def low_back(v):
    return v

def low_keep(v):
    return (low(v), None)

def low_pass(kept, grad):
    return (grad,)

def back_keep(v):
    return (v, None)

def back_low(kept, grad):
    return (low(grad),)
low.defvjp(low_keep, low_pass)
low_back.defvjp(back_keep, back_low)

def matmul(left_rows, right_rows):
    return jnp.dot(left_rows, right_rows, precision=highest)

def norm_apply(summed, gain_row, shift_row):
    row_mean = lax.optimization_barrier(jnp.mean(summed, axis=-1, keepdims=True))
    centred = summed - row_mean
    variance = lax.optimization_barrier(jnp.mean(centred * centred, axis=-1, keepdims=True))
    return centred * lax.rsqrt(variance + norm_epsilon) * gain_row + shift_row

def attend_one(queries, key_rows, values, allowed):
    scores = jnp.einsum('qhd,khd->hqk', queries, key_rows, precision=highest) * HEAD_DIM ** (-0.5)
    scores = jnp.where(allowed[None], low_back(scores), -1e+30)
    row_max = lax.optimization_barrier(jnp.max(scores, axis=-1, keepdims=True))
    exp_scores = jnp.exp(scores - row_max)
    attn_prob = exp_scores / lax.optimization_barrier(jnp.sum(exp_scores, axis=-1, keepdims=True))
    return jnp.einsum('hqk,khd->qhd', low(attn_prob), values, precision=highest)

def attend_all(queries, key_rows, values, lengths, causal):
    query_pos = jnp.arange(queries.shape[1], dtype=jnp.int32)[:, None]
    key_pos = jnp.arange(key_rows.shape[1], dtype=jnp.int32)[None, :]

    def one_seq(packed):
        query_blk, key_blk, value_blk, length = packed
        allowed = key_pos < length
        if causal:
            allowed = allowed & (key_pos <= query_pos)
        return attend_one(query_blk, key_blk, value_blk, allowed)
    return lax.map(jax.checkpoint(one_seq), (queries, key_rows, values, lengths))

def layer_forward(params, token_rows, memory_rows, target_part, memory_part):
    self_inputs, self_output, cross_query, cross_memory, cross_output, feed_in, feed_out, proj_bias, feed_bias, branch_bias, norm_gain, norm_shift = params
    seq_count = target_part.shape[0]

    def split_heads(rows, length):
        return rows.reshape(seq_count, length, HEADS, HEAD_DIM)

    def merge_heads(rows):
        return rows.reshape(rows.shape[0] * rows.shape[1], D)
    first_in = low(token_rows)
    queries = low(low_back(matmul(first_in, self_inputs[0]) + proj_bias[0]))
    key_rows = low(low_back(matmul(first_in, self_inputs[1])))
    values = low(low_back(matmul(first_in, self_inputs[2]) + proj_bias[1]))
    mixed_rows = attend_all(split_heads(queries, LEN), split_heads(key_rows, LEN), split_heads(values, LEN), target_part, True)
    mixed_rows = low(low_back(merge_heads(mixed_rows)))
    branch = low_back(matmul(mixed_rows, self_output) + branch_bias[0])
    normed_one = norm_apply(residual_scale * token_rows + branch, norm_gain[0], norm_shift[0])
    second = low(normed_one)
    source = low(memory_rows)
    queries = low(low_back(matmul(second, cross_query) + proj_bias[2]))
    key_rows = low(low_back(matmul(source, cross_memory[0])))
    values = low(low_back(matmul(source, cross_memory[1]) + proj_bias[3]))
    mixed_rows = attend_all(split_heads(queries, LEN), split_heads(key_rows, MLEN), split_heads(values, MLEN), memory_part, False)
    mixed_rows = low(low_back(merge_heads(mixed_rows)))
    branch = low_back(matmul(mixed_rows, cross_output) + branch_bias[1])
    normed_two = norm_apply(residual_scale * normed_one + branch, norm_gain[1], norm_shift[1])
    hidden_pre = low_back(matmul(low(normed_two), feed_in) + feed_bias)
    hidden = low(jax.nn.gelu(hidden_pre, approximate=False))
    branch = low_back(matmul(hidden, feed_out) + branch_bias[2])
    return norm_apply(residual_scale * normed_two + branch, norm_gain[2], norm_shift[2])

def reference(tokens, memory, cotangent, target_lengths, memory_lengths, self_inputs, self_output, cross_query, cross_memory, cross_output, feed_in, feed_out, proj_bias, feed_bias, branch_bias, norm_gain, norm_shift):
    params = tuple((array_in.astype(jnp.float32) for array_in in (self_inputs, self_output, cross_query, cross_memory, cross_output, feed_in, feed_out, proj_bias, feed_bias, branch_bias, norm_gain, norm_shift)))
    per_block = math.gcd(SEQS, max(1, 4096 // LEN))
    blocks = SEQS // per_block
    token_blocks = tokens.astype(jnp.float32).reshape(blocks, per_block * LEN, D)
    memory_blocks = memory.astype(jnp.float32).reshape(blocks, per_block * MLEN, D)
    cot_blocks = cotangent.astype(jnp.float32).reshape(blocks, per_block * LEN, D)
    target_blocks = target_lengths.reshape(blocks, per_block)
    memory_len_blocks = memory_lengths.reshape(blocks, per_block)

    def advance(totals, packed):
        token_rows, memory_rows, cot_rows, target_part, memory_part = packed

        def forward(weights, rows_in, memory_in):
            return layer_forward(weights, rows_in, memory_in, target_part, memory_part)
        result, backward = jax.vjp(forward, params, token_rows, memory_rows)
        grad_params, grad_rows, grad_source = backward(cot_rows)
        totals = jax.tree.map(jnp.add, totals, grad_params)
        return (totals, (result.astype(jnp.bfloat16), grad_rows.astype(jnp.bfloat16), grad_source.astype(jnp.bfloat16)))
    zero_grads = jax.tree.map(jnp.zeros_like, params)
    totals, stacked = lax.scan(advance, zero_grads, (token_blocks, memory_blocks, cot_blocks, target_blocks, memory_len_blocks))
    outputs, grad_rows, grad_source = stacked
    return (outputs.reshape(TOKENS, D), grad_rows.reshape(TOKENS, D), grad_source.reshape(MTOK, D), totals[0], totals[1], totals[2], totals[3], totals[4], totals[5], totals[6], totals[7], totals[8], totals[9], totals[10], totals[11])
```

```python
import functools

import jax, jax.numpy as jnp
from jax import lax
from jax.experimental import pallas as pl
from jax.experimental.pallas import tpu as pltpu
from jax.sharding import Mesh
from jax.sharding import PartitionSpec as P

HEAD = 64
NEG = -1e30

def _nt(a, b):
    return lax.dot_general(a, b, (((1,), (1,)), ((), ())), preferred_element_type=jnp.float32)

def _nn(a, b):
    return lax.dot_general(a, b, (((1,), (0,)), ((), ())), preferred_element_type=jnp.float32)

def _lanes(rows):
    return lax.broadcasted_iota(jnp.int32, (rows, 128), 1)

def _put(base, lane, pairs):
    for at, val in pairs:
        base = jnp.where(lane == at, val, base)
    return base

def fwd_kernel(len_ref, q_ref, k_ref, v_ref, o_ref, lse_ref, *, causal, bq):
    p = pl.program_id(0)
    rows, keys = q_ref.shape[0], k_ref.shape[0]
    length = len_ref[0]
    kl = _lanes(keys)
    kpos = lax.broadcasted_iota(jnp.int32, (keys, 128), 0)
    kbias = jnp.where(kpos < length, 0.0, NEG)
    k2 = k_ref[...].astype(jnp.float32)
    v2 = v_ref[...].astype(jnp.float32)
    ql = _lanes(bq)
    heads = []
    for h in range(2):
        mine = (kl // HEAD) == h
        other = HEAD * (1 - h)
        kh = jnp.where(mine, k2, jnp.where(kl == other, kbias, 0.0)).astype(jnp.bfloat16)
        vh = jnp.where(mine, v2, jnp.where(kl == other, 1.0, 0.0)).astype(jnp.bfloat16)
        heads.append((kh, vh))
    for i in range(rows // bq):
        q2 = q_ref[pl.ds(i * bq, bq), :].astype(jnp.float32) * (HEAD ** -0.5)
        out = jnp.zeros((bq, 128), jnp.float32)
        lse_all = lse_ref[pl.ds(i * bq, bq), :]
        for h in range(2):
            kh, vh = heads[h]
            mine = (ql // HEAD) == h
            other = HEAD * (1 - h)
            qh = jnp.where(mine, q2, jnp.where(ql == other, 1.0, 0.0)).astype(jnp.bfloat16)
            if causal:
                lo = i * bq
                sd = _nt(qh, kh[lo:lo + bq])
                r = lax.broadcasted_iota(jnp.int32, (bq, bq), 0)
                c = lax.broadcasted_iota(jnp.int32, (bq, bq), 1)
                sd = jnp.where(c <= r, sd, NEG)
                m = jnp.max(sd, axis=1, keepdims=True)
                if lo:
                    sl = _nt(qh, kh[:lo])
                    m = jnp.maximum(m, jnp.max(sl, axis=1, keepdims=True))
                    acc = _nn(jnp.exp(sl - m).astype(jnp.bfloat16), vh[:lo])
                    acc += _nn(jnp.exp(sd - m).astype(jnp.bfloat16), vh[lo:lo + bq])
                else:
                    acc = _nn(jnp.exp(sd - m).astype(jnp.bfloat16), vh[:bq])
            else:
                s = _nt(qh, kh)
                m = jnp.max(s, axis=1, keepdims=True)
                acc = _nn(jnp.exp(s - m).astype(jnp.bfloat16), vh)
            total = jnp.sum(jnp.where(ql == other, acc, 0.0), axis=1, keepdims=True)
            out = jnp.where(mine, acc / total, out)
            lse_all = jnp.where(ql == 2 * p + h, m + jnp.log(total), lse_all)
        o_ref[pl.ds(i * bq, bq), :] = out.astype(jnp.bfloat16)
        lse_ref[pl.ds(i * bq, bq), :] = lse_all

def attn_fwd(length, q, k, v, causal, bq=256):
    rows, cols = q.shape
    keys = k.shape[0]
    pairs = cols // 128
    el = pairs * 2 * rows * keys
    return pl.pallas_call(
        functools.partial(fwd_kernel, causal=causal, bq=bq),
        out_shape=(jax.ShapeDtypeStruct((rows, cols), jnp.bfloat16), jax.ShapeDtypeStruct((rows, 128), jnp.float32)),
        grid_spec=pltpu.PrefetchScalarGridSpec(
            num_scalar_prefetch=1, grid=(pairs,),
            in_specs=[pl.BlockSpec((rows, 128), lambda p, n: (0, p)), pl.BlockSpec((keys, 128), lambda p, n: (0, p)), pl.BlockSpec((keys, 128), lambda p, n: (0, p))],
            out_specs=[pl.BlockSpec((rows, 128), lambda p, n: (0, p)), pl.BlockSpec((rows, 128), lambda p, n: (0, 0))],
        ),
        compiler_params=pltpu.CompilerParams(dimension_semantics=("arbitrary",), vmem_limit_bytes=40 << 20),
        cost_estimate=pl.CostEstimate(flops=16 * el * 64, bytes_accessed=8 * rows * cols, transcendentals=el),
        name="attend_forward",
    )(length, q, k, v)

def split3(x):
    a = x.astype(jnp.bfloat16).astype(jnp.float32)
    b = (x - a).astype(jnp.bfloat16).astype(jnp.float32)
    return a, b, x - a - b

def bwd_kernel(len_ref, q_ref, k_ref, v_ref, o_ref, g_ref, lse_ref, dq_ref, dk_ref, dv_ref, dka, dva, *, causal, bq):
    p = pl.program_id(0)
    rows, keys = q_ref.shape[0], k_ref.shape[0]
    length = len_ref[0]
    kl = _lanes(keys)
    kpos = lax.broadcasted_iota(jnp.int32, (keys, 128), 0)
    kbias = jnp.where(kpos < length, 0.0, NEG)
    k2 = k_ref[...].astype(jnp.float32)
    v2 = v_ref[...].astype(jnp.float32)
    ql = _lanes(bq)
    heads = []
    for h in range(2):
        mine = (kl // HEAD) == h
        other = HEAD * (1 - h)
        ones = (kl > other) & (kl < other + 4)
        kh = jnp.where(mine, k2, jnp.where(kl == other, kbias, jnp.where(ones, 1.0, 0.0))).astype(jnp.bfloat16)
        vh = jnp.where(mine, v2, jnp.where(ones, 1.0, 0.0)).astype(jnp.bfloat16)
        heads.append((kh, vh, kh.T))
    for i in reversed(range(rows // bq)):
        at = pl.ds(i * bq, bq)
        q2 = q_ref[at, :].astype(jnp.float32) * (HEAD ** -0.5)
        g2 = g_ref[at, :].astype(jnp.float32)
        go = g2 * o_ref[at, :].astype(jnp.float32)
        lse_all = lse_ref[at, :]
        dqt = []
        for h in range(2):
            kh, vh, kt = heads[h]
            mine = (ql // HEAD) == h
            other = HEAD * (1 - h)
            lse = jnp.sum(jnp.where(ql == 2 * p + h, lse_all, 0.0), axis=1, keepdims=True)
            delta = jnp.sum(jnp.where(mine, go, 0.0), axis=1, keepdims=True)
            la, lb, lc = split3(-lse)
            da, db, dc = split3(-delta)
            qh = _put(jnp.where(mine, q2, 0.0), ql, ((other, 1.0), (other + 1, la), (other + 2, lb), (other + 3, lc))).astype(jnp.bfloat16)
            gh = _put(jnp.where(mine, g2, 0.0), ql, ((other + 1, da), (other + 2, db), (other + 3, dc))).astype(jnp.bfloat16)
            hi = (i + 1) * bq if causal else keys
            st = _nt(kh[:hi], qh)
            if causal:
                kr = lax.broadcasted_iota(jnp.int32, (hi, bq), 0)
                qc = lax.broadcasted_iota(jnp.int32, (hi, bq), 1) + i * bq
                pt = jnp.where(kr <= qc, jnp.exp(st), 0.0)
            else:
                pt = jnp.exp(st)
            dst = (pt * _nt(vh[:hi], gh)).astype(jnp.bfloat16)
            dvn = _nn(pt.astype(jnp.bfloat16), gh)
            dkn = _nn(dst, qh)
            if i == rows // bq - 1:
                dva[h, :hi] = dvn
                dka[h, :hi] = dkn
            else:
                dva[h, :hi] += dvn
                dka[h, :hi] += dkn
            dqt.append(_nn(kt[:, :hi], dst))
        dq = jnp.concatenate([dqt[0][:HEAD], dqt[1][HEAD:]], axis=0).T
        dq_ref[at, :] = (dq * (HEAD ** -0.5)).astype(jnp.bfloat16)
    first = kl < HEAD
    dk_ref[...] = jnp.where(first, dka[0], dka[1]).astype(jnp.bfloat16)
    dv_ref[...] = jnp.where(first, dva[0], dva[1]).astype(jnp.bfloat16)

def attn_bwd(length, q, k, v, o, g, lse, causal, bq=256):
    rows, cols = q.shape
    keys = k.shape[0]
    pairs = cols // 128
    el = pairs * 2 * rows * keys
    qs = pl.BlockSpec((rows, 128), lambda p, n: (0, p))
    ks = pl.BlockSpec((keys, 128), lambda p, n: (0, p))
    return pl.pallas_call(
        functools.partial(bwd_kernel, causal=causal, bq=bq),
        out_shape=(jax.ShapeDtypeStruct((rows, cols), jnp.bfloat16), jax.ShapeDtypeStruct((keys, cols), jnp.bfloat16), jax.ShapeDtypeStruct((keys, cols), jnp.bfloat16)),
        grid_spec=pltpu.PrefetchScalarGridSpec(
            num_scalar_prefetch=1, grid=(pairs,),
            in_specs=[qs, ks, ks, qs, qs, pl.BlockSpec((rows, 128), lambda p, n: (0, 0))],
            out_specs=[qs, ks, ks],
            scratch_shapes=[pltpu.VMEM((2, keys, 128), jnp.float32), pltpu.VMEM((2, keys, 128), jnp.float32)],
        ),
        compiler_params=pltpu.CompilerParams(dimension_semantics=("arbitrary",), vmem_limit_bytes=48 << 20),
        cost_estimate=pl.CostEstimate(flops=40 * el * 64, bytes_accessed=16 * rows * cols, transcendentals=el),
        name="attend_backward",
    )(length, q, k, v, o, g, lse)

residual_scale = 300.0**0.25
norm_epsilon = 1e-05
LOW = jnp.bfloat16
F32 = jnp.float32


def tn(rows, grads):
    return lax.dot_general(rows, grads, (((0,), (0,)), ((), ())), preferred_element_type=F32)


def gelu_exact(pre_rows):
    return jax.nn.gelu(pre_rows, approximate=False)


def gelu_backward(pre_rows, grad_rows):
    unused, pullback = jax.vjp(gelu_exact, pre_rows)
    return pullback(grad_rows)[0]


def norm_forward(summed, gain_row, shift_row):
    row_mean = jnp.mean(summed, axis=-1, keepdims=True)
    centred = summed - row_mean
    variance = jnp.mean(centred * centred, axis=-1, keepdims=True)
    inverse = lax.rsqrt(variance + norm_epsilon)
    unit_rows = centred * inverse
    return unit_rows * gain_row + shift_row, unit_rows, inverse


def norm_backward(grad_out, unit_rows, inverse, gain_row):
    grad_unit = grad_out * gain_row
    first_mean = jnp.mean(grad_unit, axis=-1, keepdims=True)
    second_mean = jnp.mean(grad_unit * unit_rows, axis=-1, keepdims=True)
    return inverse * (grad_unit - first_mean - unit_rows * second_mean)


def layer(sizes, tokens, memory, cotangent, target_lengths, memory_lengths, self_inputs, self_output, cross_query, cross_memory, cross_output, feed_in, feed_out, proj_bias, feed_bias, branch_bias, norm_gain, norm_shift):
    zn, yn, gn, cn = sizes
    seq = lax.axis_index("g")
    core = lax.axis_index("c")
    width = self_output.shape[0]
    joined = width % 128 != 0

    def swap(rows):
        return lax.ppermute(rows, "c", [(0, 1), (1, 0)])

    def gather_rows(rows):
        if cn != 2:
            return lax.all_gather(rows, "c", axis=0, tiled=True)
        got = swap(rows)
        return jnp.where(core == 0, jnp.concatenate([rows, got]), jnp.concatenate([got, rows]))

    def sum_all(part):
        part = part.astype(LOW)
        if cn != 2:
            return lax.psum(part, "c").astype(F32)
        return part.astype(F32) + swap(part).astype(F32)

    def own_rows(rows):
        size = rows.shape[0] // cn
        return lax.dynamic_slice_in_dim(rows, core * size, size, 0)

    def sum_own(part):
        if cn != 2:
            return lax.psum_scatter(part.astype(LOW), "c", scatter_dimension=0, tiled=True).astype(F32)
        size = part.shape[0] // 2
        got = swap(lax.dynamic_slice_in_dim(part, (1 - core) * size, size, 0).astype(LOW))
        return lax.dynamic_slice_in_dim(part, core * size, size, 0) + got.astype(F32)

    def spread(shard, axis):
        every = [shard] + [lax.ppermute(shard, "g", [((i + k) % gn, i) for i in range(gn)]) for k in range(1, gn)]
        return [jnp.concatenate(every, axis=axis)] if joined else every

    def collect(parts, axis):
        if joined:
            parts = jnp.split(parts[0], gn, axis=axis)
        total = parts[0]
        for k in range(1, gn):
            total = total + lax.ppermute(parts[k].astype(LOW), "g", [(i, (i + k) % gn) for i in range(gn)]).astype(F32)
        return lax.psum(total.astype(LOW), ("z", "y")).astype(F32)

    target_length = lax.dynamic_slice_in_dim(target_lengths, seq, 1, 0)
    memory_length = lax.dynamic_slice_in_dim(memory_lengths, seq, 1, 0)

    token_all = gather_rows(tokens)
    w_self = spread(self_inputs, 2)
    b_proj = spread(proj_bias, 1)
    w_self_out = spread(self_output, 0)
    memory_all = gather_rows(memory)
    w_cross_mem = spread(cross_memory, 2)
    w_cross_q = spread(cross_query, 1)
    w_cross_out = spread(cross_output, 0)
    w_in = spread(feed_in, 1)
    b_in = spread(feed_bias, 0)
    w_out = spread(feed_out, 0)
    cot_all = gather_rows(cotangent)
    shards = range(len(w_self))

    self_q = [(_nn(token_all, w_self[s][0]) + b_proj[s][0]).astype(LOW) for s in shards]
    self_k = [_nn(token_all, w_self[s][1]).astype(LOW) for s in shards]
    self_v = [(_nn(token_all, w_self[s][2]) + b_proj[s][1]).astype(LOW) for s in shards]
    self_mixed, self_lse = zip(*[attn_fwd(target_length, self_q[s], self_k[s], self_v[s], True) for s in shards])
    cross_k = [_nn(memory_all, w_cross_mem[s][0]).astype(LOW) for s in shards]
    cross_v = [(_nn(memory_all, w_cross_mem[s][1]) + b_proj[s][3]).astype(LOW) for s in shards]
    branch_one = sum_all(sum(_nn(self_mixed[s], w_self_out[s]) for s in shards)) + branch_bias[0]
    normed_one, unit_one, inverse_one = norm_forward(residual_scale * token_all.astype(F32) + branch_one, norm_gain[0], norm_shift[0])
    second = normed_one.astype(LOW)
    cross_q = [(_nn(second, w_cross_q[s]) + b_proj[s][2]).astype(LOW) for s in shards]
    cross_mixed, cross_lse = zip(*[attn_fwd(memory_length, cross_q[s], cross_k[s], cross_v[s], False) for s in shards])
    branch_two = sum_all(sum(_nn(cross_mixed[s], w_cross_out[s]) for s in shards)) + branch_bias[1]
    normed_two, unit_two, inverse_two = norm_forward(residual_scale * normed_one + branch_two, norm_gain[1], norm_shift[1])
    third = normed_two.astype(LOW)
    hidden_pre = [_nn(third, w_in[s]) + b_in[s].astype(F32) for s in shards]
    hidden = [gelu_exact(hidden_pre[s]).astype(LOW) for s in shards]
    branch_three = sum_all(sum(_nn(hidden[s], w_out[s]) for s in shards)) + branch_bias[2]
    normed_three, unit_three, inverse_three = norm_forward(residual_scale * normed_two + branch_three, norm_gain[2], norm_shift[2])
    block_out = own_rows(normed_three.astype(LOW))

    cot = cot_all.astype(F32)
    grad_three = norm_backward(cot, unit_three, inverse_three, norm_gain[2])
    low_three = grad_three.astype(LOW)
    grad_hidden = [_nt(low_three, w_out[s]) for s in shards]
    grad_feed_out = collect([tn(hidden[s], low_three) for s in shards], 0)
    grad_pre = [gelu_backward(hidden_pre[s], grad_hidden[s]).astype(LOW) for s in shards]
    grad_feed_in = collect([tn(third, grad_pre[s]) for s in shards], 1)
    grad_normed_two = residual_scale * grad_three + sum_all(sum(_nt(grad_pre[s], w_in[s]) for s in shards))
    grad_two = norm_backward(grad_normed_two, unit_two, inverse_two, norm_gain[1])
    low_two = grad_two.astype(LOW)
    grad_cross_mixed = [_nt(low_two, w_cross_out[s]).astype(LOW) for s in shards]
    grad_cross_output = collect([tn(cross_mixed[s], low_two) for s in shards], 0)
    cross_dq, cross_dk, cross_dv = zip(*[attn_bwd(memory_length, cross_q[s], cross_k[s], cross_v[s], cross_mixed[s], grad_cross_mixed[s], cross_lse[s], False) for s in shards])
    grad_normed_one = residual_scale * grad_two + sum_all(sum(_nt(cross_dq[s], w_cross_q[s]) for s in shards))
    grad_cross_query = collect([tn(second, cross_dq[s]) for s in shards], 1)
    grad_cross_memory = collect([jnp.stack([tn(memory_all, cross_dk[s]), tn(memory_all, cross_dv[s])]) for s in shards], 2)
    grad_memory = sum_own(sum(_nt(cross_dk[s], w_cross_mem[s][0]) + _nt(cross_dv[s], w_cross_mem[s][1]) for s in shards)).astype(LOW)
    grad_one = norm_backward(grad_normed_one, unit_one, inverse_one, norm_gain[0])
    low_one = grad_one.astype(LOW)
    grad_self_mixed = [_nt(low_one, w_self_out[s]).astype(LOW) for s in shards]
    grad_self_output = collect([tn(self_mixed[s], low_one) for s in shards], 0)
    self_dq, self_dk, self_dv = zip(*[attn_bwd(target_length, self_q[s], self_k[s], self_v[s], self_mixed[s], grad_self_mixed[s], self_lse[s], True) for s in shards])
    grad_self_inputs = collect([jnp.stack([tn(token_all, self_dq[s]), tn(token_all, self_dk[s]), tn(token_all, self_dv[s])]) for s in shards], 2)
    token_part = sum(_nt(self_dq[s], w_self[s][0]) + _nt(self_dk[s], w_self[s][1]) + _nt(self_dv[s], w_self[s][2]) for s in shards)
    grad_tokens = (residual_scale * own_rows(grad_one) + sum_own(token_part)).astype(LOW)

    def sums(rows):
        return jnp.sum(rows.astype(F32), axis=0)

    proj_sums = collect([jnp.stack([sums(self_dq[s]), sums(self_dv[s]), sums(cross_dq[s]), sums(cross_dv[s])]) for s in shards], 1)
    feed_sums = collect([sums(grad_pre[s]) for s in shards], 0)
    terms = jnp.stack([sums(low_one), sums(low_two), sums(low_three), sums(grad_normed_one * unit_one), sums(grad_normed_two * unit_two), sums(cot * unit_three), sums(grad_normed_one), sums(grad_normed_two), sums(cot)])
    terms = lax.psum(terms.astype(LOW), ("z", "y", "g")).astype(F32)
    terms = lax.dynamic_slice_in_dim(terms, (seq * cn + core) * width, width, 1)
    return (block_out, grad_tokens, grad_memory, grad_self_inputs, grad_self_output, grad_cross_query, grad_cross_memory, grad_cross_output, grad_feed_in, grad_feed_out, proj_sums, feed_sums, terms[0:3], terms[3:6], terms[6:9])


def solution(mesh):
    dp, mp = mesh.shape["dp"], mesh.shape["mp"]

    def whole(*args):
        yn = 2 if dp % 2 == 0 else 1
        gn = args[3].shape[0] // dp
        sizes = (dp // yn, yn, gn, mp // gn)
        fine = Mesh(mesh.devices.reshape(sizes), ("z", "y", "g", "c"))
        d, m = ("z", "y"), ("g", "c")
        rows, wide, tall = P(d + m, None), P(None, m), P(m, None)
        stack = P(None, None, m)
        in_specs = (rows, rows, rows, P(d), P(d), stack, tall, wide, stack, tall, wide, tall, wide, P(m), P(), P(), P())
        out_specs = (rows, rows, rows, stack, tall, wide, stack, tall, wide, tall, wide, P(m), wide, wide, wide)
        return jax.shard_map(functools.partial(layer, sizes), mesh=fine, in_specs=in_specs, out_specs=out_specs, check_vma=False)(*args)

    return whole
```

```python
import functools

import jax, jax.numpy as jnp
from jax import lax
from jax.experimental import pallas as pl
from jax.experimental.pallas import tpu as pltpu
from jax.sharding import Mesh
from jax.sharding import PartitionSpec as P

HEAD = 64
NEG = -1e30

def _nt(a, b):
    return lax.dot_general(a, b, (((1,), (1,)), ((), ())), preferred_element_type=jnp.float32)

def _nn(a, b):
    return lax.dot_general(a, b, (((1,), (0,)), ((), ())), preferred_element_type=jnp.float32)

def _lanes(rows):
    return lax.broadcasted_iota(jnp.int32, (rows, 128), 1)

def _put(base, lane, pairs):
    for at, val in pairs:
        base = jnp.where(lane == at, val, base)
    return base

def fwd_kernel(len_ref, q_ref, k_ref, v_ref, o_ref, lse_ref, *, causal, bq):
    p = pl.program_id(0)
    rows, keys = q_ref.shape[0], k_ref.shape[0]
    length = len_ref[0]
    kl = _lanes(keys)
    kpos = lax.broadcasted_iota(jnp.int32, (keys, 128), 0)
    kbias = jnp.where(kpos < length, 0.0, NEG)
    k2 = k_ref[...].astype(jnp.float32)
    v2 = v_ref[...].astype(jnp.float32)
    ql = _lanes(bq)
    heads = []
    for h in range(2):
        mine = (kl // HEAD) == h
        other = HEAD * (1 - h)
        kh = jnp.where(mine, k2, jnp.where(kl == other, kbias, 0.0)).astype(jnp.bfloat16)
        vh = jnp.where(mine, v2, jnp.where(kl == other, 1.0, 0.0)).astype(jnp.bfloat16)
        heads.append((kh, vh))
    for i in range(rows // bq):
        q2 = q_ref[pl.ds(i * bq, bq), :].astype(jnp.float32) * (HEAD ** -0.5)
        out = jnp.zeros((bq, 128), jnp.float32)
        lse_all = lse_ref[pl.ds(i * bq, bq), :]
        for h in range(2):
            kh, vh = heads[h]
            mine = (ql // HEAD) == h
            other = HEAD * (1 - h)
            qh = jnp.where(mine, q2, jnp.where(ql == other, 1.0, 0.0)).astype(jnp.bfloat16)
            if causal:
                lo = i * bq
                sd = _nt(qh, kh[lo:lo + bq])
                r = lax.broadcasted_iota(jnp.int32, (bq, bq), 0)
                c = lax.broadcasted_iota(jnp.int32, (bq, bq), 1)
                sd = jnp.where(c <= r, sd, NEG)
                m = jnp.max(sd, axis=1, keepdims=True)
                if lo:
                    sl = _nt(qh, kh[:lo])
                    m = jnp.maximum(m, jnp.max(sl, axis=1, keepdims=True))
                    acc = _nn(jnp.exp(sl - m).astype(jnp.bfloat16), vh[:lo])
                    acc += _nn(jnp.exp(sd - m).astype(jnp.bfloat16), vh[lo:lo + bq])
                else:
                    acc = _nn(jnp.exp(sd - m).astype(jnp.bfloat16), vh[:bq])
            else:
                s = _nt(qh, kh)
                m = jnp.max(s, axis=1, keepdims=True)
                acc = _nn(jnp.exp(s - m).astype(jnp.bfloat16), vh)
            total = jnp.sum(jnp.where(ql == other, acc, 0.0), axis=1, keepdims=True)
            out = jnp.where(mine, acc / total, out)
            lse_all = jnp.where(ql == 2 * p + h, m + jnp.log(total), lse_all)
        o_ref[pl.ds(i * bq, bq), :] = out.astype(jnp.bfloat16)
        lse_ref[pl.ds(i * bq, bq), :] = lse_all

def attn_fwd(length, q, k, v, causal, bq=256):
    rows, cols = q.shape
    keys = k.shape[0]
    pairs = cols // 128
    el = pairs * 2 * rows * keys
    return pl.pallas_call(
        functools.partial(fwd_kernel, causal=causal, bq=bq),
        out_shape=(jax.ShapeDtypeStruct((rows, cols), jnp.bfloat16), jax.ShapeDtypeStruct((rows, 128), jnp.float32)),
        grid_spec=pltpu.PrefetchScalarGridSpec(
            num_scalar_prefetch=1, grid=(pairs,),
            in_specs=[pl.BlockSpec((rows, 128), lambda p, n: (0, p)), pl.BlockSpec((keys, 128), lambda p, n: (0, p)), pl.BlockSpec((keys, 128), lambda p, n: (0, p))],
            out_specs=[pl.BlockSpec((rows, 128), lambda p, n: (0, p)), pl.BlockSpec((rows, 128), lambda p, n: (0, 0))],
        ),
        compiler_params=pltpu.CompilerParams(dimension_semantics=("arbitrary",), vmem_limit_bytes=40 << 20),
        cost_estimate=pl.CostEstimate(flops=16 * el * 64, bytes_accessed=8 * rows * cols, transcendentals=el),
        name="attend_forward",
    )(length, q, k, v)

def split3(x):
    a = x.astype(jnp.bfloat16).astype(jnp.float32)
    b = (x - a).astype(jnp.bfloat16).astype(jnp.float32)
    return a, b, x - a - b

def bwd_kernel(len_ref, q_ref, k_ref, v_ref, o_ref, g_ref, lse_ref, dq_ref, dk_ref, dv_ref, dka, dva, *, causal, bq):
    p = pl.program_id(0)
    rows, keys = q_ref.shape[0], k_ref.shape[0]
    length = len_ref[0]
    kl = _lanes(keys)
    kpos = lax.broadcasted_iota(jnp.int32, (keys, 128), 0)
    kbias = jnp.where(kpos < length, 0.0, NEG)
    k2 = k_ref[...].astype(jnp.float32)
    v2 = v_ref[...].astype(jnp.float32)
    ql = _lanes(bq)
    heads = []
    for h in range(2):
        mine = (kl // HEAD) == h
        other = HEAD * (1 - h)
        ones = (kl > other) & (kl < other + 4)
        kh = jnp.where(mine, k2, jnp.where(kl == other, kbias, jnp.where(ones, 1.0, 0.0))).astype(jnp.bfloat16)
        vh = jnp.where(mine, v2, jnp.where(ones, 1.0, 0.0)).astype(jnp.bfloat16)
        heads.append((kh, vh, kh.T))
    for i in reversed(range(rows // bq)):
        at = pl.ds(i * bq, bq)
        q2 = q_ref[at, :].astype(jnp.float32) * (HEAD ** -0.5)
        g2 = g_ref[at, :].astype(jnp.float32)
        go = g2 * o_ref[at, :].astype(jnp.float32)
        lse_all = lse_ref[at, :]
        dqt = []
        for h in range(2):
            kh, vh, kt = heads[h]
            mine = (ql // HEAD) == h
            other = HEAD * (1 - h)
            lse = jnp.sum(jnp.where(ql == 2 * p + h, lse_all, 0.0), axis=1, keepdims=True)
            delta = jnp.sum(jnp.where(mine, go, 0.0), axis=1, keepdims=True)
            la, lb, lc = split3(-lse)
            da, db, dc = split3(-delta)
            qh = _put(jnp.where(mine, q2, 0.0), ql, ((other, 1.0), (other + 1, la), (other + 2, lb), (other + 3, lc))).astype(jnp.bfloat16)
            gh = _put(jnp.where(mine, g2, 0.0), ql, ((other + 1, da), (other + 2, db), (other + 3, dc))).astype(jnp.bfloat16)
            hi = (i + 1) * bq if causal else keys
            st = _nt(kh[:hi], qh)
            if causal:
                kr = lax.broadcasted_iota(jnp.int32, (hi, bq), 0)
                qc = lax.broadcasted_iota(jnp.int32, (hi, bq), 1) + i * bq
                pt = jnp.where(kr <= qc, jnp.exp(st), 0.0)
            else:
                pt = jnp.exp(st)
            dst = (pt * _nt(vh[:hi], gh)).astype(jnp.bfloat16)
            dvn = _nn(pt.astype(jnp.bfloat16), gh)
            dkn = _nn(dst, qh)
            if i == rows // bq - 1:
                dva[h, :hi] = dvn
                dka[h, :hi] = dkn
            else:
                dva[h, :hi] += dvn
                dka[h, :hi] += dkn
            dqt.append(_nn(kt[:, :hi], dst))
        dq = jnp.concatenate([dqt[0][:HEAD], dqt[1][HEAD:]], axis=0).T
        dq_ref[at, :] = (dq * (HEAD ** -0.5)).astype(jnp.bfloat16)
    first = kl < HEAD
    dk_ref[...] = jnp.where(first, dka[0], dka[1]).astype(jnp.bfloat16)
    dv_ref[...] = jnp.where(first, dva[0], dva[1]).astype(jnp.bfloat16)

def attn_bwd(length, q, k, v, o, g, lse, causal, bq=256):
    rows, cols = q.shape
    keys = k.shape[0]
    pairs = cols // 128
    el = pairs * 2 * rows * keys
    qs = pl.BlockSpec((rows, 128), lambda p, n: (0, p))
    ks = pl.BlockSpec((keys, 128), lambda p, n: (0, p))
    return pl.pallas_call(
        functools.partial(bwd_kernel, causal=causal, bq=bq),
        out_shape=(jax.ShapeDtypeStruct((rows, cols), jnp.bfloat16), jax.ShapeDtypeStruct((keys, cols), jnp.bfloat16), jax.ShapeDtypeStruct((keys, cols), jnp.bfloat16)),
        grid_spec=pltpu.PrefetchScalarGridSpec(
            num_scalar_prefetch=1, grid=(pairs,),
            in_specs=[qs, ks, ks, qs, qs, pl.BlockSpec((rows, 128), lambda p, n: (0, 0))],
            out_specs=[qs, ks, ks],
            scratch_shapes=[pltpu.VMEM((2, keys, 128), jnp.float32), pltpu.VMEM((2, keys, 128), jnp.float32)],
        ),
        compiler_params=pltpu.CompilerParams(dimension_semantics=("arbitrary",), vmem_limit_bytes=48 << 20),
        cost_estimate=pl.CostEstimate(flops=40 * el * 64, bytes_accessed=16 * rows * cols, transcendentals=el),
        name="attend_backward",
    )(length, q, k, v, o, g, lse)

residual_scale = 300.0**0.25
norm_epsilon = 1e-05
LOW = jnp.bfloat16
F32 = jnp.float32


def tn(rows, grads):
    return lax.dot_general(rows, grads, (((0,), (0,)), ((), ())), preferred_element_type=F32)


def gelu_exact(pre_rows):
    return jax.nn.gelu(pre_rows, approximate=False)


def gelu_backward(pre_rows, grad_rows):
    unused, pullback = jax.vjp(gelu_exact, pre_rows)
    return pullback(grad_rows)[0]


def norm_forward(summed, gain_row, shift_row):
    row_mean = jnp.mean(summed, axis=-1, keepdims=True)
    centred = summed - row_mean
    variance = jnp.mean(centred * centred, axis=-1, keepdims=True)
    inverse = lax.rsqrt(variance + norm_epsilon)
    unit_rows = centred * inverse
    return unit_rows * gain_row + shift_row, unit_rows, inverse


def norm_backward(grad_out, unit_rows, inverse, gain_row):
    grad_unit = grad_out * gain_row
    first_mean = jnp.mean(grad_unit, axis=-1, keepdims=True)
    second_mean = jnp.mean(grad_unit * unit_rows, axis=-1, keepdims=True)
    return inverse * (grad_unit - first_mean - unit_rows * second_mean)


def layer(sizes, tokens, memory, cotangent, target_lengths, memory_lengths, self_inputs, self_output, cross_query, cross_memory, cross_output, feed_in, feed_out, proj_bias, feed_bias, branch_bias, norm_gain, norm_shift):
    zn, yn, gn, cn = sizes
    seq = lax.axis_index("g")
    core = lax.axis_index("c")
    width = self_output.shape[0]
    joined = width % 128 != 0

    def swap(rows):
        return lax.ppermute(rows, "c", [(0, 1), (1, 0)])

    def gather_rows(rows):
        if cn != 2:
            return lax.all_gather(rows, "c", axis=0, tiled=True)
        got = swap(rows)
        return jnp.where(core == 0, jnp.concatenate([rows, got]), jnp.concatenate([got, rows]))

    def sum_all(part):
        part = part.astype(LOW)
        if cn != 2:
            return lax.psum(part, "c").astype(F32)
        return part.astype(F32) + swap(part).astype(F32)

    def own_rows(rows):
        size = rows.shape[0] // cn
        return lax.dynamic_slice_in_dim(rows, core * size, size, 0)

    def sum_own(part):
        if cn != 2:
            return lax.psum_scatter(part.astype(LOW), "c", scatter_dimension=0, tiled=True).astype(F32)
        size = part.shape[0] // 2
        got = swap(lax.dynamic_slice_in_dim(part, (1 - core) * size, size, 0).astype(LOW))
        return lax.dynamic_slice_in_dim(part, core * size, size, 0) + got.astype(F32)

    def spread(shard, axis):
        every = [shard] + [lax.ppermute(shard, "g", [((i + k) % gn, i) for i in range(gn)]) for k in range(1, gn)]
        return [jnp.concatenate(every, axis=axis)] if joined else every

    def send_home(parts):
        total = parts[0]
        for k in range(1, gn):
            total = total + lax.ppermute(parts[k].astype(LOW), "g", [(i, (i + k) % gn) for i in range(gn)]).astype(F32)
        return total

    steps = [("y", 1, lax.axis_index("y"), yn)] if yn == 2 else []
    steps += [("z", 1 << b, lax.axis_index("z"), zn) for b in range((zn - 1).bit_length())]

    def pairwise(rows, axis, far, size):
        return lax.ppermute(rows, axis, [(i, i ^ far) for i in range(size)])

    def sum_groups(total):
        for axis, far, at, size in steps:
            half = total.shape[0] // 2
            bit = (at // far) % 2
            away = lax.dynamic_slice_in_dim(total, (1 - bit) * half, half, 0).astype(LOW)
            keep = lax.dynamic_slice_in_dim(total, bit * half, half, 0)
            total = keep + pairwise(away, axis, far, size).astype(F32)
        total = total.astype(LOW)
        for axis, far, at, size in reversed(steps):
            got = pairwise(total, axis, far, size)
            total = jnp.where((at // far) % 2 == 0, jnp.concatenate([total, got]), jnp.concatenate([got, total]))
        return total.astype(F32)

    def spread_wide(shard, axis):
        size = shard.shape[0] // (zn * yn)
        at = lax.axis_index("z") * yn + lax.axis_index("y")
        piece = lax.dynamic_slice_in_dim(shard, at * size, size, 0)
        every = [shard]
        for k in range(1, gn):
            got = lax.ppermute(piece, "g", [((i + k) % gn, i) for i in range(gn)])
            every.append(lax.all_gather(got, ("z", "y"), axis=0, tiled=True))
        return [jnp.concatenate(every, axis=axis)] if joined else every

    def parts_of(values, axis):
        return jnp.split(values[0], gn, axis=axis) if joined else values

    target_length = lax.dynamic_slice_in_dim(target_lengths, seq, 1, 0)
    memory_length = lax.dynamic_slice_in_dim(memory_lengths, seq, 1, 0)

    token_all = gather_rows(tokens)
    w_self = spread(self_inputs, 2)
    b_proj = spread(proj_bias, 1)
    w_self_out = spread(self_output, 0)
    memory_all = gather_rows(memory)
    w_cross_mem = spread(cross_memory, 2)
    w_cross_q = spread(cross_query, 1)
    w_cross_out = spread(cross_output, 0)
    w_in = spread_wide(feed_in, 1)
    b_in = spread(feed_bias, 0)
    w_out = spread_wide(feed_out, 0)
    cot_all = gather_rows(cotangent)
    shards = range(len(w_self))

    self_q = [(_nn(token_all, w_self[s][0]) + b_proj[s][0]).astype(LOW) for s in shards]
    self_k = [_nn(token_all, w_self[s][1]).astype(LOW) for s in shards]
    self_v = [(_nn(token_all, w_self[s][2]) + b_proj[s][1]).astype(LOW) for s in shards]
    self_mixed, self_lse = zip(*[attn_fwd(target_length, self_q[s], self_k[s], self_v[s], True) for s in shards])
    cross_k = [_nn(memory_all, w_cross_mem[s][0]).astype(LOW) for s in shards]
    cross_v = [(_nn(memory_all, w_cross_mem[s][1]) + b_proj[s][3]).astype(LOW) for s in shards]
    branch_one = sum_all(sum(_nn(self_mixed[s], w_self_out[s]) for s in shards)) + branch_bias[0]
    normed_one, unit_one, inverse_one = norm_forward(residual_scale * token_all.astype(F32) + branch_one, norm_gain[0], norm_shift[0])
    second = normed_one.astype(LOW)
    cross_q = [(_nn(second, w_cross_q[s]) + b_proj[s][2]).astype(LOW) for s in shards]
    cross_mixed, cross_lse = zip(*[attn_fwd(memory_length, cross_q[s], cross_k[s], cross_v[s], False) for s in shards])
    branch_two = sum_all(sum(_nn(cross_mixed[s], w_cross_out[s]) for s in shards)) + branch_bias[1]
    normed_two, unit_two, inverse_two = norm_forward(residual_scale * normed_one + branch_two, norm_gain[1], norm_shift[1])
    third = normed_two.astype(LOW)
    hidden_pre = [_nn(third, w_in[s]) + b_in[s].astype(F32) for s in shards]
    hidden = [gelu_exact(hidden_pre[s]).astype(LOW) for s in shards]
    branch_three = sum_all(sum(_nn(hidden[s], w_out[s]) for s in shards)) + branch_bias[2]
    normed_three, unit_three, inverse_three = norm_forward(residual_scale * normed_two + branch_three, norm_gain[2], norm_shift[2])
    block_out = own_rows(normed_three.astype(LOW))

    cot = cot_all.astype(F32)
    grad_three = norm_backward(cot, unit_three, inverse_three, norm_gain[2])
    low_three = grad_three.astype(LOW)
    grad_hidden = [_nt(low_three, w_out[s]) for s in shards]
    grad_feed_out = sum_groups(send_home(parts_of([tn(hidden[s], low_three) for s in shards], 0)))
    grad_pre = [gelu_backward(hidden_pre[s], grad_hidden[s]).astype(LOW) for s in shards]
    grad_feed_in = sum_groups(send_home(parts_of([tn(third, grad_pre[s]) for s in shards], 1)))
    grad_normed_two = residual_scale * grad_three + sum_all(sum(_nt(grad_pre[s], w_in[s]) for s in shards))
    grad_two = norm_backward(grad_normed_two, unit_two, inverse_two, norm_gain[1])
    low_two = grad_two.astype(LOW)
    grad_cross_mixed = [_nt(low_two, w_cross_out[s]).astype(LOW) for s in shards]
    cross_out_parts = parts_of([tn(low_two, cross_mixed[s]) for s in shards], 1)
    cross_dq, cross_dk, cross_dv = zip(*[attn_bwd(memory_length, cross_q[s], cross_k[s], cross_v[s], cross_mixed[s], grad_cross_mixed[s], cross_lse[s], False) for s in shards])
    grad_normed_one = residual_scale * grad_two + sum_all(sum(_nt(cross_dq[s], w_cross_q[s]) for s in shards))
    cross_parts = [cross_out_parts, parts_of([tn(second, cross_dq[s]) for s in shards], 1)]
    cross_parts += [parts_of([tn(memory_all, cross_dk[s]) for s in shards], 1), parts_of([tn(memory_all, cross_dv[s]) for s in shards], 1)]
    cross_total = sum_groups(send_home([jnp.concatenate([part[k] for part in cross_parts]) for k in range(gn)]))
    grad_memory = sum_own(sum(_nt(cross_dk[s], w_cross_mem[s][0]) + _nt(cross_dv[s], w_cross_mem[s][1]) for s in shards)).astype(LOW)
    grad_one = norm_backward(grad_normed_one, unit_one, inverse_one, norm_gain[0])
    low_one = grad_one.astype(LOW)
    grad_self_mixed = [_nt(low_one, w_self_out[s]).astype(LOW) for s in shards]
    self_out_parts = parts_of([tn(low_one, self_mixed[s]) for s in shards], 1)
    self_dq, self_dk, self_dv = zip(*[attn_bwd(target_length, self_q[s], self_k[s], self_v[s], self_mixed[s], grad_self_mixed[s], self_lse[s], True) for s in shards])
    token_part = sum(_nt(self_dq[s], w_self[s][0]) + _nt(self_dk[s], w_self[s][1]) + _nt(self_dv[s], w_self[s][2]) for s in shards)
    grad_tokens = (residual_scale * own_rows(grad_one) + sum_own(token_part)).astype(LOW)

    def sums(rows):
        return jnp.sum(rows.astype(F32), axis=0)

    terms = jnp.stack([sums(low_one), sums(low_two), sums(low_three), sums(grad_normed_one * unit_one), sums(grad_normed_two * unit_two), sums(cot * unit_three), sums(grad_normed_one), sums(grad_normed_two), sums(cot)])
    proj_sums = parts_of([jnp.stack([sums(self_dq[s]), sums(self_dv[s]), sums(cross_dq[s]), sums(cross_dv[s])]) for s in shards], 1)
    feed_sums = parts_of([sums(grad_pre[s]) for s in shards], 0)
    self_parts = [self_out_parts] + [parts_of([tn(token_all, grads[s]) for s in shards], 1) for grads in (self_dq, self_dk, self_dv)]
    packed = []
    for k in range(gn):
        small = lax.dynamic_slice_in_dim(terms, ((seq + k) % gn * cn + core) * width, width, 1)
        small = jnp.concatenate([small, proj_sums[k], feed_sums[k].reshape(-1, width)])
        small = jnp.pad(small, ((0, 16 * zn * yn - small.shape[0]), (0, 0)))
        packed.append(jnp.concatenate([part[k] for part in self_parts] + [small]))
    self_total = sum_groups(send_home(packed))
    model = tokens.shape[1]
    take = lambda rows, at: lax.slice_in_dim(rows, at * model, (at + 1) * model)
    small = self_total[4 * model:]
    grad_self_inputs = jnp.stack([take(self_total, 1), take(self_total, 2), take(self_total, 3)])
    grad_cross_memory = jnp.stack([take(cross_total, 2), take(cross_total, 3)])
    feed_rows = feed_bias.shape[0] // width
    return (block_out, grad_tokens, grad_memory, grad_self_inputs, take(self_total, 0).T, take(cross_total, 1), grad_cross_memory, take(cross_total, 0).T, grad_feed_in, grad_feed_out, small[9:13], small[13:13 + feed_rows].reshape(-1), small[0:3], small[3:6], small[6:9])


def solution(mesh):
    dp, mp = mesh.shape["dp"], mesh.shape["mp"]

    def whole(*args):
        yn = 2 if dp % 2 == 0 else 1
        gn = args[3].shape[0] // dp
        sizes = (dp // yn, yn, gn, mp // gn)
        fine = Mesh(mesh.devices.reshape(sizes), ("z", "y", "g", "c"))
        d, m = ("z", "y"), ("g", "c")
        rows, wide, tall = P(d + m, None), P(None, m), P(m, None)
        stack = P(None, None, m)
        in_specs = (rows, rows, rows, P(d), P(d), stack, tall, wide, stack, tall, wide, tall, wide, P(m), P(), P(), P())
        out_specs = (rows, rows, rows, stack, tall, wide, stack, tall, wide, tall, wide, P(m), wide, wide, wide)
        return jax.shard_map(functools.partial(layer, sizes), mesh=fine, in_specs=in_specs, out_specs=out_specs, check_vma=False)(*args)

    return whole
```

```python
import functools

import jax, jax.numpy as jnp
from jax import lax
from jax.experimental import pallas as pl
from jax.experimental.pallas import tpu as pltpu
from jax.sharding import Mesh
from jax.sharding import PartitionSpec as P

HEAD = 64
NEG = -1e30

def _nt(a, b):
    return lax.dot_general(a, b, (((1,), (1,)), ((), ())), preferred_element_type=jnp.float32)

def _nn(a, b):
    return lax.dot_general(a, b, (((1,), (0,)), ((), ())), preferred_element_type=jnp.float32)

def _lanes(rows):
    return lax.broadcasted_iota(jnp.int32, (rows, 128), 1)

def _put(base, lane, pairs):
    for at, val in pairs:
        base = jnp.where(lane == at, val, base)
    return base

def fwd_kernel(len_ref, q_ref, k_ref, v_ref, o_ref, lse_ref, *, causal, bq):
    p = pl.program_id(0)
    rows, keys = q_ref.shape[0], k_ref.shape[0]
    length = len_ref[0]
    kl = _lanes(keys)
    kpos = lax.broadcasted_iota(jnp.int32, (keys, 128), 0)
    kbias = jnp.where(kpos < length, 0.0, NEG)
    k2 = k_ref[...].astype(jnp.float32)
    v2 = v_ref[...].astype(jnp.float32)
    ql = _lanes(bq)
    heads = []
    for h in range(2):
        mine = (kl // HEAD) == h
        other = HEAD * (1 - h)
        kh = jnp.where(mine, k2, jnp.where(kl == other, kbias, 0.0)).astype(jnp.bfloat16)
        vh = jnp.where(mine, v2, jnp.where(kl == other, 1.0, 0.0)).astype(jnp.bfloat16)
        heads.append((kh, vh))
    for i in range(rows // bq):
        q2 = q_ref[pl.ds(i * bq, bq), :].astype(jnp.float32) * (HEAD ** -0.5)
        out = jnp.zeros((bq, 128), jnp.float32)
        lse_all = lse_ref[pl.ds(i * bq, bq), :]
        for h in range(2):
            kh, vh = heads[h]
            mine = (ql // HEAD) == h
            other = HEAD * (1 - h)
            qh = jnp.where(mine, q2, jnp.where(ql == other, 1.0, 0.0)).astype(jnp.bfloat16)
            if causal:
                lo = i * bq
                sd = _nt(qh, kh[lo:lo + bq])
                r = lax.broadcasted_iota(jnp.int32, (bq, bq), 0)
                c = lax.broadcasted_iota(jnp.int32, (bq, bq), 1)
                sd = jnp.where(c <= r, sd, NEG)
                m = jnp.max(sd, axis=1, keepdims=True)
                if lo:
                    sl = _nt(qh, kh[:lo])
                    m = jnp.maximum(m, jnp.max(sl, axis=1, keepdims=True))
                    acc = _nn(jnp.exp(sl - m).astype(jnp.bfloat16), vh[:lo])
                    acc += _nn(jnp.exp(sd - m).astype(jnp.bfloat16), vh[lo:lo + bq])
                else:
                    acc = _nn(jnp.exp(sd - m).astype(jnp.bfloat16), vh[:bq])
            else:
                s = _nt(qh, kh)
                m = jnp.max(s, axis=1, keepdims=True)
                acc = _nn(jnp.exp(s - m).astype(jnp.bfloat16), vh)
            total = jnp.sum(jnp.where(ql == other, acc, 0.0), axis=1, keepdims=True)
            out = jnp.where(mine, acc / total, out)
            lse_all = jnp.where(ql == 2 * p + h, m + jnp.log(total), lse_all)
        o_ref[pl.ds(i * bq, bq), :] = out.astype(jnp.bfloat16)
        lse_ref[pl.ds(i * bq, bq), :] = lse_all

def attn_fwd(length, q, k, v, causal, bq=256):
    rows, cols = q.shape
    keys = k.shape[0]
    pairs = cols // 128
    el = pairs * 2 * rows * keys
    return pl.pallas_call(
        functools.partial(fwd_kernel, causal=causal, bq=bq),
        out_shape=(jax.ShapeDtypeStruct((rows, cols), jnp.bfloat16), jax.ShapeDtypeStruct((rows, 128), jnp.float32)),
        grid_spec=pltpu.PrefetchScalarGridSpec(
            num_scalar_prefetch=1, grid=(pairs,),
            in_specs=[pl.BlockSpec((rows, 128), lambda p, n: (0, p)), pl.BlockSpec((keys, 128), lambda p, n: (0, p)), pl.BlockSpec((keys, 128), lambda p, n: (0, p))],
            out_specs=[pl.BlockSpec((rows, 128), lambda p, n: (0, p)), pl.BlockSpec((rows, 128), lambda p, n: (0, 0))],
        ),
        compiler_params=pltpu.CompilerParams(dimension_semantics=("arbitrary",), vmem_limit_bytes=40 << 20),
        cost_estimate=pl.CostEstimate(flops=16 * el * 64, bytes_accessed=8 * rows * cols, transcendentals=el),
        name="attend_forward",
    )(length, q, k, v)

def split3(x):
    a = x.astype(jnp.bfloat16).astype(jnp.float32)
    b = (x - a).astype(jnp.bfloat16).astype(jnp.float32)
    return a, b, x - a - b

def bwd_kernel(len_ref, q_ref, k_ref, v_ref, o_ref, g_ref, lse_ref, dq_ref, dk_ref, dv_ref, dka, dva, *, causal, bq):
    p = pl.program_id(0)
    rows, keys = q_ref.shape[0], k_ref.shape[0]
    length = len_ref[0]
    kl = _lanes(keys)
    kpos = lax.broadcasted_iota(jnp.int32, (keys, 128), 0)
    kbias = jnp.where(kpos < length, 0.0, NEG)
    k2 = k_ref[...].astype(jnp.float32)
    v2 = v_ref[...].astype(jnp.float32)
    ql = _lanes(bq)
    heads = []
    for h in range(2):
        mine = (kl // HEAD) == h
        other = HEAD * (1 - h)
        ones = (kl > other) & (kl < other + 4)
        kh = jnp.where(mine, k2, jnp.where(kl == other, kbias, jnp.where(ones, 1.0, 0.0))).astype(jnp.bfloat16)
        vh = jnp.where(mine, v2, jnp.where(ones, 1.0, 0.0)).astype(jnp.bfloat16)
        heads.append((kh, vh, kh.T))
    for i in reversed(range(rows // bq)):
        at = pl.ds(i * bq, bq)
        q2 = q_ref[at, :].astype(jnp.float32) * (HEAD ** -0.5)
        g2 = g_ref[at, :].astype(jnp.float32)
        go = g2 * o_ref[at, :].astype(jnp.float32)
        lse_all = lse_ref[at, :]
        dqt = []
        for h in range(2):
            kh, vh, kt = heads[h]
            mine = (ql // HEAD) == h
            other = HEAD * (1 - h)
            lse = jnp.sum(jnp.where(ql == 2 * p + h, lse_all, 0.0), axis=1, keepdims=True)
            delta = jnp.sum(jnp.where(mine, go, 0.0), axis=1, keepdims=True)
            la, lb, lc = split3(-lse)
            da, db, dc = split3(-delta)
            qh = _put(jnp.where(mine, q2, 0.0), ql, ((other, 1.0), (other + 1, la), (other + 2, lb), (other + 3, lc))).astype(jnp.bfloat16)
            gh = _put(jnp.where(mine, g2, 0.0), ql, ((other + 1, da), (other + 2, db), (other + 3, dc))).astype(jnp.bfloat16)
            hi = (i + 1) * bq if causal else keys
            st = _nt(kh[:hi], qh)
            if causal:
                kr = lax.broadcasted_iota(jnp.int32, (hi, bq), 0)
                qc = lax.broadcasted_iota(jnp.int32, (hi, bq), 1) + i * bq
                pt = jnp.where(kr <= qc, jnp.exp(st), 0.0)
            else:
                pt = jnp.exp(st)
            dst = (pt * _nt(vh[:hi], gh)).astype(jnp.bfloat16)
            dvn = _nn(pt.astype(jnp.bfloat16), gh)
            dkn = _nn(dst, qh)
            if i == rows // bq - 1:
                dva[h, :hi] = dvn
                dka[h, :hi] = dkn
            else:
                dva[h, :hi] += dvn
                dka[h, :hi] += dkn
            dqt.append(_nn(kt[:, :hi], dst))
        dq = jnp.concatenate([dqt[0][:HEAD], dqt[1][HEAD:]], axis=0).T
        dq_ref[at, :] = (dq * (HEAD ** -0.5)).astype(jnp.bfloat16)
    first = kl < HEAD
    dk_ref[...] = jnp.where(first, dka[0], dka[1]).astype(jnp.bfloat16)
    dv_ref[...] = jnp.where(first, dva[0], dva[1]).astype(jnp.bfloat16)

def attn_bwd(length, q, k, v, o, g, lse, causal, bq=256):
    rows, cols = q.shape
    keys = k.shape[0]
    pairs = cols // 128
    el = pairs * 2 * rows * keys
    qs = pl.BlockSpec((rows, 128), lambda p, n: (0, p))
    ks = pl.BlockSpec((keys, 128), lambda p, n: (0, p))
    return pl.pallas_call(
        functools.partial(bwd_kernel, causal=causal, bq=bq),
        out_shape=(jax.ShapeDtypeStruct((rows, cols), jnp.bfloat16), jax.ShapeDtypeStruct((keys, cols), jnp.bfloat16), jax.ShapeDtypeStruct((keys, cols), jnp.bfloat16)),
        grid_spec=pltpu.PrefetchScalarGridSpec(
            num_scalar_prefetch=1, grid=(pairs,),
            in_specs=[qs, ks, ks, qs, qs, pl.BlockSpec((rows, 128), lambda p, n: (0, 0))],
            out_specs=[qs, ks, ks],
            scratch_shapes=[pltpu.VMEM((2, keys, 128), jnp.float32), pltpu.VMEM((2, keys, 128), jnp.float32)],
        ),
        compiler_params=pltpu.CompilerParams(dimension_semantics=("arbitrary",), vmem_limit_bytes=48 << 20),
        cost_estimate=pl.CostEstimate(flops=40 * el * 64, bytes_accessed=16 * rows * cols, transcendentals=el),
        name="attend_backward",
    )(length, q, k, v, o, g, lse)

CHUNK = 512
SPAN = 256


def reduce_kernel(spots, count, results, *refs):
    own, other, out, rest = refs[:count], refs[count : 2 * count], refs[2 * count : 2 * count + results], refs[2 * count + results :]
    held, ysum, zgot, full, mine, load, store, xs, xr, ys, yr, zs, zr, bs, br, es, er = rest
    seq, ya, za = lax.axis_index("g"), lax.axis_index("y"), lax.axis_index("z")
    peers = {1: za + 1 - 2 * (za % 2), 2: (za + 2) % 4, 3: 3 - za}
    total = len(spots)

    def remote(src, dst, send, recv, where):
        return pltpu.make_async_remote_copy(src_ref=src, dst_ref=dst, send_sem=send, recv_sem=recv, device_id=where, device_id_type=pl.DeviceIdType.MESH)

    def block(at, size):
        return pl.ds(pl.multiple_of(at * size, size), size)

    def x_copy(k):
        a, r, c, n, o, q = spots[k]
        return remote(other[a].at[pl.ds(r, n), pl.ds(c, SPAN)], held.at[k, pl.ds(0, n)], xs.at[k], xr.at[k], {"g": 1 - seq})

    def own_copy(k):
        a, r, c, n, o, q = spots[k]
        return pltpu.make_async_copy(own[a].at[pl.ds(r, n), pl.ds(c, SPAN)], mine.at[k % 4, pl.ds(0, n)], load.at[k % 4])

    def y_copy(k):
        h = spots[k][3] // 2
        return remote(held.at[k, block(1 - ya, h)], ysum.at[k, pl.ds(0, h)], ys.at[k], yr.at[k], {"y": 1 - ya})

    def z_copy(k, d):
        p = spots[k][3] // 8
        return remote(ysum.at[k, block(peers[d], p)], zgot.at[k, d - 1, pl.ds(0, p)], zs.at[k, d - 1], zr.at[k, d - 1], {"z": peers[d]})

    def zb_copy(k, d):
        rows = full.at[k, block(ya * 4 + za, spots[k][3] // 8)]
        return remote(rows, rows, bs.at[k, d - 1], br.at[k, d - 1], {"z": peers[d]})

    def yb_copy(k):
        rows = full.at[k, block(ya, spots[k][3] // 2)]
        return remote(rows, rows, es.at[k], er.at[k], {"y": 1 - ya})

    def out_copy(k):
        a, r, c, n, o, q = spots[k]
        return pltpu.make_async_copy(full.at[k, pl.ds(0, n)], out[o].at[pl.ds(q, n), pl.ds(c, SPAN)], store.at[k])

    def to_y(k):
        n = spots[k][3]
        own_copy(k).wait()
        x_copy(k).wait_recv()
        held[k, :n] = held[k, :n] + mine[k % 4, :n]
        y_copy(k).start()

    def to_z(k):
        h = spots[k][3] // 2
        y_copy(k).wait_recv()
        ysum[k, :h] = ysum[k, :h] + held[k, block(ya, h)]
        for d in (1, 2, 3):
            z_copy(k, d).start()

    def back_z(k):
        p = spots[k][3] // 8
        for d in (1, 2, 3):
            z_copy(k, d).wait_recv()
        rows = ysum[k, block(za, p)].astype(F32)
        for d in (1, 2, 3):
            rows = rows + zgot[k, d - 1, :p].astype(F32)
        full[k, block(ya * 4 + za, p)] = rows.astype(LOW)
        for d in (1, 2, 3):
            zb_copy(k, d).start()

    def back_y(k):
        for d in (1, 2, 3):
            zb_copy(k, d).wait_recv()
        yb_copy(k).start()

    def finish(k):
        yb_copy(k).wait_recv()
        out_copy(k).start()

    barrier = pltpu.get_barrier_semaphore()
    everyone = [{"g": 1 - seq}, {"y": 1 - ya}] + [{"z": peers[d]} for d in (1, 2, 3)]
    for where in everyone:
        pl.semaphore_signal(barrier, inc=1, device_id=where, device_id_type=pl.DeviceIdType.MESH)
    for k in range(3):
        own_copy(k).start()
    pl.semaphore_wait(barrier, len(everyone))
    stages = (to_y, to_z, back_z, back_y, finish)
    ahead = 3
    for k in range(min(ahead, total)):
        x_copy(k).start()
    for step in range(total + len(stages) - 1):
        if step + ahead < total:
            x_copy(step + ahead).start()
        for at, stage in enumerate(stages):
            if 0 <= step - at < total:
                stage(step - at)
        if step + 3 < total:
            own_copy(step + 3).start()
    for k in range(total):
        x_copy(k).wait_send()
        y_copy(k).wait_send()
        yb_copy(k).wait_send()
        out_copy(k).wait()
        for d in (1, 2, 3):
            z_copy(k, d).wait_send()
            zb_copy(k, d).wait_send()


def reduce_all(pairs, places, results):
    spots = []
    for a, (part, unused) in enumerate(pairs):
        rows, cols = part.shape
        size = min(CHUNK, rows)
        for r in range(0, rows, size):
            for c in range(0, cols, SPAN):
                spots.append((a, r, c, size, places[a][0], places[a][1] + r))
    count, total = len(pairs), len(spots)
    most = max(s[3] for s in spots)
    any_space = pl.BlockSpec(memory_space=pl.ANY)
    dma = pltpu.SemaphoreType.DMA
    size = sum(own.size for own, unused in pairs)
    return pl.pallas_call(
        functools.partial(reduce_kernel, tuple(spots), count, len(results)),
        out_shape=[jax.ShapeDtypeStruct(shape, LOW) for shape in results],
        in_specs=[any_space] * (2 * count),
        out_specs=[any_space] * len(results),
        scratch_shapes=[
            pltpu.VMEM((total, most, SPAN), LOW),
            pltpu.VMEM((total, most // 2, SPAN), LOW),
            pltpu.VMEM((total, 3, most // 8, SPAN), LOW),
            pltpu.VMEM((total, most, SPAN), LOW),
            pltpu.VMEM((4, most, SPAN), LOW),
            dma((4,)), dma((total,)),
            dma((total,)), dma((total,)), dma((total,)), dma((total,)),
            dma((total, 3)), dma((total, 3)), dma((total, 3)), dma((total, 3)),
            dma((total,)), dma((total,)),
        ],
        compiler_params=pltpu.CompilerParams(collective_id=0, has_side_effects=True, vmem_limit_bytes=48 << 20),
        cost_estimate=pl.CostEstimate(flops=4 * size, bytes_accessed=400 * size, transcendentals=0),
        name="reduce_gradients",
    )(*[p[0] for p in pairs], *[p[1] for p in pairs])


residual_scale = 300.0**0.25
norm_epsilon = 1e-05
LOW = jnp.bfloat16
F32 = jnp.float32


def tn(rows, grads):
    return lax.dot_general(rows, grads, (((0,), (0,)), ((), ())), preferred_element_type=F32)


def gelu_exact(pre_rows):
    return jax.nn.gelu(pre_rows, approximate=False)


def gelu_backward(pre_rows, grad_rows):
    unused, pullback = jax.vjp(gelu_exact, pre_rows)
    return pullback(grad_rows)[0]


def norm_forward(summed, gain_row, shift_row):
    row_mean = jnp.mean(summed, axis=-1, keepdims=True)
    centred = summed - row_mean
    variance = jnp.mean(centred * centred, axis=-1, keepdims=True)
    inverse = lax.rsqrt(variance + norm_epsilon)
    unit_rows = centred * inverse
    return unit_rows * gain_row + shift_row, unit_rows, inverse


def norm_backward(grad_out, unit_rows, inverse, gain_row):
    grad_unit = grad_out * gain_row
    first_mean = jnp.mean(grad_unit, axis=-1, keepdims=True)
    second_mean = jnp.mean(grad_unit * unit_rows, axis=-1, keepdims=True)
    return inverse * (grad_unit - first_mean - unit_rows * second_mean)


def layer(sizes, tokens, memory, cotangent, target_lengths, memory_lengths, self_inputs, self_output, cross_query, cross_memory, cross_output, feed_in, feed_out, proj_bias, feed_bias, branch_bias, norm_gain, norm_shift):
    zn, yn, gn, cn = sizes
    seq = lax.axis_index("g")
    core = lax.axis_index("c")
    width = self_output.shape[0]
    joined = width % 128 != 0

    def swap(rows):
        return lax.ppermute(rows, "c", [(0, 1), (1, 0)])

    def gather_rows(rows):
        if cn != 2:
            return lax.all_gather(rows, "c", axis=0, tiled=True)
        got = swap(rows)
        return jnp.where(core == 0, jnp.concatenate([rows, got]), jnp.concatenate([got, rows]))

    def sum_all(part):
        part = part.astype(LOW)
        if cn != 2:
            return lax.psum(part, "c").astype(F32)
        return part.astype(F32) + swap(part).astype(F32)

    def own_rows(rows):
        size = rows.shape[0] // cn
        return lax.dynamic_slice_in_dim(rows, core * size, size, 0)

    def sum_own(part):
        if cn != 2:
            return lax.psum_scatter(part.astype(LOW), "c", scatter_dimension=0, tiled=True).astype(F32)
        size = part.shape[0] // 2
        got = swap(lax.dynamic_slice_in_dim(part, (1 - core) * size, size, 0).astype(LOW))
        return lax.dynamic_slice_in_dim(part, core * size, size, 0) + got.astype(F32)

    def spread(shard, axis):
        every = [shard] + [lax.ppermute(shard, "g", [((i + k) % gn, i) for i in range(gn)]) for k in range(1, gn)]
        return [jnp.concatenate(every, axis=axis)] if joined else every

    def send_home(parts):
        total = parts[0]
        for k in range(1, gn):
            total = total + lax.ppermute(parts[k].astype(LOW), "g", [(i, (i + k) % gn) for i in range(gn)]).astype(F32)
        return total

    steps = [("y", 1, lax.axis_index("y"), yn)] if yn == 2 else []
    steps += [("z", 1 << b, lax.axis_index("z"), zn) for b in range((zn - 1).bit_length())]

    def pairwise(rows, axis, far, size):
        return lax.ppermute(rows, axis, [(i, i ^ far) for i in range(size)])

    def sum_groups(total):
        for axis, far, at, size in steps:
            half = total.shape[0] // 2
            bit = (at // far) % 2
            away = lax.dynamic_slice_in_dim(total, (1 - bit) * half, half, 0).astype(LOW)
            keep = lax.dynamic_slice_in_dim(total, bit * half, half, 0)
            total = keep + pairwise(away, axis, far, size).astype(F32)
        total = total.astype(LOW)
        for axis, far, at, size in reversed(steps):
            got = pairwise(total, axis, far, size)
            total = jnp.where((at // far) % 2 == 0, jnp.concatenate([total, got]), jnp.concatenate([got, total]))
        return total.astype(F32)

    def spread_wide(shard, axis):
        size = shard.shape[0] // (zn * yn)
        at = lax.axis_index("z") * yn + lax.axis_index("y")
        piece = lax.dynamic_slice_in_dim(shard, at * size, size, 0)
        every = [shard]
        for k in range(1, gn):
            got = lax.ppermute(piece, "g", [((i + k) % gn, i) for i in range(gn)])
            every.append(lax.all_gather(got, ("z", "y"), axis=0, tiled=True))
        return [jnp.concatenate(every, axis=axis)] if joined else every

    def parts_of(values, axis):
        return jnp.split(values[0], gn, axis=axis) if joined else values

    target_length = lax.dynamic_slice_in_dim(target_lengths, seq, 1, 0)
    memory_length = lax.dynamic_slice_in_dim(memory_lengths, seq, 1, 0)

    token_all = gather_rows(tokens)
    w_self = spread(self_inputs, 2)
    b_proj = spread(proj_bias, 1)
    w_self_out = spread(self_output, 0)
    memory_all = gather_rows(memory)
    w_cross_mem = spread(cross_memory, 2)
    w_cross_q = spread(cross_query, 1)
    w_cross_out = spread(cross_output, 0)
    w_in = spread_wide(feed_in, 1)
    b_in = spread(feed_bias, 0)
    w_out = spread_wide(feed_out, 0)
    cot_all = gather_rows(cotangent)
    shards = range(len(w_self))

    self_q = [(_nn(token_all, w_self[s][0]) + b_proj[s][0]).astype(LOW) for s in shards]
    self_k = [_nn(token_all, w_self[s][1]).astype(LOW) for s in shards]
    self_v = [(_nn(token_all, w_self[s][2]) + b_proj[s][1]).astype(LOW) for s in shards]
    self_mixed, self_lse = zip(*[attn_fwd(target_length, self_q[s], self_k[s], self_v[s], True) for s in shards])
    cross_k = [_nn(memory_all, w_cross_mem[s][0]).astype(LOW) for s in shards]
    cross_v = [(_nn(memory_all, w_cross_mem[s][1]) + b_proj[s][3]).astype(LOW) for s in shards]
    branch_one = sum_all(sum(_nn(self_mixed[s], w_self_out[s]) for s in shards)) + branch_bias[0]
    normed_one, unit_one, inverse_one = norm_forward(residual_scale * token_all.astype(F32) + branch_one, norm_gain[0], norm_shift[0])
    second = normed_one.astype(LOW)
    cross_q = [(_nn(second, w_cross_q[s]) + b_proj[s][2]).astype(LOW) for s in shards]
    cross_mixed, cross_lse = zip(*[attn_fwd(memory_length, cross_q[s], cross_k[s], cross_v[s], False) for s in shards])
    branch_two = sum_all(sum(_nn(cross_mixed[s], w_cross_out[s]) for s in shards)) + branch_bias[1]
    normed_two, unit_two, inverse_two = norm_forward(residual_scale * normed_one + branch_two, norm_gain[1], norm_shift[1])
    third = normed_two.astype(LOW)
    hidden_pre = [_nn(third, w_in[s]) + b_in[s].astype(F32) for s in shards]
    hidden = [gelu_exact(hidden_pre[s]).astype(LOW) for s in shards]
    branch_three = sum_all(sum(_nn(hidden[s], w_out[s]) for s in shards)) + branch_bias[2]
    normed_three, unit_three, inverse_three = norm_forward(residual_scale * normed_two + branch_three, norm_gain[2], norm_shift[2])
    block_out = own_rows(normed_three.astype(LOW))

    cot = cot_all.astype(F32)
    grad_three = norm_backward(cot, unit_three, inverse_three, norm_gain[2])
    low_three = grad_three.astype(LOW)
    grad_hidden = [_nt(low_three, w_out[s]) for s in shards]
    feed_out_parts = parts_of([tn(hidden[s], low_three) for s in shards], 0)
    grad_pre = [gelu_backward(hidden_pre[s], grad_hidden[s]).astype(LOW) for s in shards]
    feed_in_parts = parts_of([tn(third, grad_pre[s]) for s in shards], 1)
    grad_normed_two = residual_scale * grad_three + sum_all(sum(_nt(grad_pre[s], w_in[s]) for s in shards))
    grad_two = norm_backward(grad_normed_two, unit_two, inverse_two, norm_gain[1])
    low_two = grad_two.astype(LOW)
    grad_cross_mixed = [_nt(low_two, w_cross_out[s]).astype(LOW) for s in shards]
    cross_out_parts = parts_of([tn(cross_mixed[s], low_two) for s in shards], 0)
    cross_dq, cross_dk, cross_dv = zip(*[attn_bwd(memory_length, cross_q[s], cross_k[s], cross_v[s], cross_mixed[s], grad_cross_mixed[s], cross_lse[s], False) for s in shards])
    grad_normed_one = residual_scale * grad_two + sum_all(sum(_nt(cross_dq[s], w_cross_q[s]) for s in shards))
    cross_parts = [parts_of([tn(second, cross_dq[s]) for s in shards], 1), parts_of([tn(memory_all, cross_dk[s]) for s in shards], 1), parts_of([tn(memory_all, cross_dv[s]) for s in shards], 1)]
    grad_memory = sum_own(sum(_nt(cross_dk[s], w_cross_mem[s][0]) + _nt(cross_dv[s], w_cross_mem[s][1]) for s in shards)).astype(LOW)
    grad_one = norm_backward(grad_normed_one, unit_one, inverse_one, norm_gain[0])
    low_one = grad_one.astype(LOW)
    grad_self_mixed = [_nt(low_one, w_self_out[s]).astype(LOW) for s in shards]
    self_out_parts = parts_of([tn(self_mixed[s], low_one) for s in shards], 0)
    self_dq, self_dk, self_dv = zip(*[attn_bwd(target_length, self_q[s], self_k[s], self_v[s], self_mixed[s], grad_self_mixed[s], self_lse[s], True) for s in shards])
    token_part = sum(_nt(self_dq[s], w_self[s][0]) + _nt(self_dk[s], w_self[s][1]) + _nt(self_dv[s], w_self[s][2]) for s in shards)
    grad_tokens = (residual_scale * own_rows(grad_one) + sum_own(token_part)).astype(LOW)

    def sums(rows):
        return jnp.sum(rows.astype(F32), axis=0)

    terms = jnp.stack([sums(low_one), sums(low_two), sums(low_three), sums(grad_normed_one * unit_one), sums(grad_normed_two * unit_two), sums(cot * unit_three), sums(grad_normed_one), sums(grad_normed_two), sums(cot)])
    proj_sums = parts_of([jnp.stack([sums(self_dq[s]), sums(self_dv[s]), sums(cross_dq[s]), sums(cross_dv[s])]) for s in shards], 1)
    feed_sums = parts_of([sums(grad_pre[s]) for s in shards], 0)
    self_parts = [parts_of([tn(token_all, grads[s]) for s in shards], 1) for grads in (self_dq, self_dk, self_dv)]
    smalls = []
    for k in range(gn):
        small = lax.dynamic_slice_in_dim(terms, ((seq + k) % gn * cn + core) * width, width, 1)
        small = jnp.concatenate([small, proj_sums[k], feed_sums[k].reshape(-1, width)])
        smalls.append(jnp.pad(small, ((0, 16 * zn * yn - small.shape[0]), (0, 0))))
    model = tokens.shape[1]
    groups = [[feed_out_parts], [feed_in_parts], [cross_out_parts], cross_parts[:1], cross_parts[1:], [self_out_parts], self_parts, [smalls]]
    if (zn, yn, gn, cn, width) == (4, 2, 2, 2, SPAN):
        pairs, places, results = [], [], []
        for at, group in enumerate(groups):
            rows = 0
            for part in group:
                pairs.append((part[0].astype(LOW), part[1].astype(LOW)))
                places.append((at, rows))
                rows += part[0].shape[0]
            results.append((rows, group[0][0].shape[1]))
        sums_low = reduce_all(pairs, places, results)
    else:
        sums_low = [sum_groups(send_home([jnp.concatenate([part[k] for part in group]) for k in range(gn)])) for group in groups]
    feed_out_sum, feed_in_sum, cross_out_sum, cross_q_sum, cross_mem_sum, self_out_sum, self_in_sum, small = [rows.astype(F32) for rows in sums_low]
    feed_rows = feed_bias.shape[0] // width
    return (block_out, grad_tokens, grad_memory, self_in_sum.reshape(3, model, width), self_out_sum, cross_q_sum, cross_mem_sum.reshape(2, model, width), cross_out_sum, feed_in_sum, feed_out_sum, small[9:13], small[13:13 + feed_rows].reshape(-1), small[0:3], small[3:6], small[6:9])


def solution(mesh):
    dp, mp = mesh.shape["dp"], mesh.shape["mp"]

    def whole(*args):
        yn = 2 if dp % 2 == 0 else 1
        gn = args[3].shape[0] // dp
        sizes = (dp // yn, yn, gn, mp // gn)
        fine = Mesh(mesh.devices.reshape(sizes), ("z", "y", "g", "c"))
        d, m = ("z", "y"), ("g", "c")
        rows, wide, tall = P(d + m, None), P(None, m), P(m, None)
        stack = P(None, None, m)
        in_specs = (rows, rows, rows, P(d), P(d), stack, tall, wide, stack, tall, wide, tall, wide, P(m), P(), P(), P())
        out_specs = (rows, rows, rows, stack, tall, wide, stack, tall, wide, tall, wide, P(m), wide, wide, wide)
        return jax.shard_map(functools.partial(layer, sizes), mesh=fine, in_specs=in_specs, out_specs=out_specs, check_vma=False)(*args)

    return whole
```

```python
import functools

import jax, jax.numpy as jnp
from jax import lax
from jax.experimental import pallas as pl
from jax.experimental.pallas import tpu as pltpu
from jax.sharding import Mesh
from jax.sharding import PartitionSpec as P

HEAD = 64
NEG = -1e30

def _nt(a, b):
    return lax.dot_general(a, b, (((1,), (1,)), ((), ())), preferred_element_type=jnp.float32)

def _nn(a, b):
    return lax.dot_general(a, b, (((1,), (0,)), ((), ())), preferred_element_type=jnp.float32)

def _lanes(rows):
    return lax.broadcasted_iota(jnp.int32, (rows, 128), 1)

def _put(base, lane, pairs):
    for at, val in pairs:
        base = jnp.where(lane == at, val, base)
    return base

def fwd_kernel(len_ref, q_ref, k_ref, v_ref, o_ref, lse_ref, *, causal, bq):
    p = pl.program_id(0)
    rows, keys = q_ref.shape[0], k_ref.shape[0]
    length = len_ref[0]
    kl = _lanes(keys)
    kpos = lax.broadcasted_iota(jnp.int32, (keys, 128), 0)
    kbias = jnp.where(kpos < length, 0.0, NEG)
    k2 = k_ref[...].astype(jnp.float32)
    v2 = v_ref[...].astype(jnp.float32)
    ql = _lanes(bq)
    heads = []
    for h in range(2):
        mine = (kl // HEAD) == h
        other = HEAD * (1 - h)
        kh = jnp.where(mine, k2, jnp.where(kl == other, kbias, 0.0)).astype(jnp.bfloat16)
        vh = jnp.where(mine, v2, jnp.where(kl == other, 1.0, 0.0)).astype(jnp.bfloat16)
        heads.append((kh, vh))
    for i in range(rows // bq):
        q2 = q_ref[pl.ds(i * bq, bq), :].astype(jnp.float32) * (HEAD ** -0.5)
        out = jnp.zeros((bq, 128), jnp.float32)
        lse_all = lse_ref[pl.ds(i * bq, bq), :]
        for h in range(2):
            kh, vh = heads[h]
            mine = (ql // HEAD) == h
            other = HEAD * (1 - h)
            qh = jnp.where(mine, q2, jnp.where(ql == other, 1.0, 0.0)).astype(jnp.bfloat16)
            if causal:
                lo = i * bq
                sd = _nt(qh, kh[lo:lo + bq])
                r = lax.broadcasted_iota(jnp.int32, (bq, bq), 0)
                c = lax.broadcasted_iota(jnp.int32, (bq, bq), 1)
                sd = jnp.where(c <= r, sd, NEG)
                m = jnp.max(sd, axis=1, keepdims=True)
                if lo:
                    sl = _nt(qh, kh[:lo])
                    m = jnp.maximum(m, jnp.max(sl, axis=1, keepdims=True))
                    acc = _nn(jnp.exp(sl - m).astype(jnp.bfloat16), vh[:lo])
                    acc += _nn(jnp.exp(sd - m).astype(jnp.bfloat16), vh[lo:lo + bq])
                else:
                    acc = _nn(jnp.exp(sd - m).astype(jnp.bfloat16), vh[:bq])
            else:
                s = _nt(qh, kh)
                m = jnp.max(s, axis=1, keepdims=True)
                acc = _nn(jnp.exp(s - m).astype(jnp.bfloat16), vh)
            total = jnp.sum(jnp.where(ql == other, acc, 0.0), axis=1, keepdims=True)
            out = jnp.where(mine, acc / total, out)
            lse_all = jnp.where(ql == 2 * p + h, m + jnp.log(total), lse_all)
        o_ref[pl.ds(i * bq, bq), :] = out.astype(jnp.bfloat16)
        lse_ref[pl.ds(i * bq, bq), :] = lse_all

def attn_fwd(length, q, k, v, causal, bq=256):
    rows, cols = q.shape
    keys = k.shape[0]
    pairs = cols // 128
    el = pairs * 2 * rows * keys
    return pl.pallas_call(
        functools.partial(fwd_kernel, causal=causal, bq=bq),
        out_shape=(jax.ShapeDtypeStruct((rows, cols), jnp.bfloat16), jax.ShapeDtypeStruct((rows, 128), jnp.float32)),
        grid_spec=pltpu.PrefetchScalarGridSpec(
            num_scalar_prefetch=1, grid=(pairs,),
            in_specs=[pl.BlockSpec((rows, 128), lambda p, n: (0, p)), pl.BlockSpec((keys, 128), lambda p, n: (0, p)), pl.BlockSpec((keys, 128), lambda p, n: (0, p))],
            out_specs=[pl.BlockSpec((rows, 128), lambda p, n: (0, p)), pl.BlockSpec((rows, 128), lambda p, n: (0, 0))],
        ),
        compiler_params=pltpu.CompilerParams(dimension_semantics=("arbitrary",), vmem_limit_bytes=40 << 20),
        cost_estimate=pl.CostEstimate(flops=16 * el * 64, bytes_accessed=8 * rows * cols, transcendentals=el),
        name="attend_forward",
    )(length, q, k, v)

def split3(x):
    a = x.astype(jnp.bfloat16).astype(jnp.float32)
    b = (x - a).astype(jnp.bfloat16).astype(jnp.float32)
    return a, b, x - a - b

def bwd_kernel(len_ref, q_ref, k_ref, v_ref, o_ref, g_ref, lse_ref, dq_ref, dk_ref, dv_ref, dka, dva, *, causal, bq):
    p = pl.program_id(0)
    rows, keys = q_ref.shape[0], k_ref.shape[0]
    length = len_ref[0]
    kl = _lanes(keys)
    kpos = lax.broadcasted_iota(jnp.int32, (keys, 128), 0)
    kbias = jnp.where(kpos < length, 0.0, NEG)
    k2 = k_ref[...].astype(jnp.float32)
    v2 = v_ref[...].astype(jnp.float32)
    ql = _lanes(bq)
    heads = []
    for h in range(2):
        mine = (kl // HEAD) == h
        other = HEAD * (1 - h)
        ones = (kl > other) & (kl < other + 4)
        kh = jnp.where(mine, k2, jnp.where(kl == other, kbias, jnp.where(ones, 1.0, 0.0))).astype(jnp.bfloat16)
        vh = jnp.where(mine, v2, jnp.where(ones, 1.0, 0.0)).astype(jnp.bfloat16)
        heads.append((kh, vh, kh.T))
    for i in reversed(range(rows // bq)):
        at = pl.ds(i * bq, bq)
        q2 = q_ref[at, :].astype(jnp.float32) * (HEAD ** -0.5)
        g2 = g_ref[at, :].astype(jnp.float32)
        go = g2 * o_ref[at, :].astype(jnp.float32)
        lse_all = lse_ref[at, :]
        dqt = []
        for h in range(2):
            kh, vh, kt = heads[h]
            mine = (ql // HEAD) == h
            other = HEAD * (1 - h)
            lse = jnp.sum(jnp.where(ql == 2 * p + h, lse_all, 0.0), axis=1, keepdims=True)
            delta = jnp.sum(jnp.where(mine, go, 0.0), axis=1, keepdims=True)
            la, lb, lc = split3(-lse)
            da, db, dc = split3(-delta)
            qh = _put(jnp.where(mine, q2, 0.0), ql, ((other, 1.0), (other + 1, la), (other + 2, lb), (other + 3, lc))).astype(jnp.bfloat16)
            gh = _put(jnp.where(mine, g2, 0.0), ql, ((other + 1, da), (other + 2, db), (other + 3, dc))).astype(jnp.bfloat16)
            hi = (i + 1) * bq if causal else keys
            st = _nt(kh[:hi], qh)
            if causal:
                kr = lax.broadcasted_iota(jnp.int32, (hi, bq), 0)
                qc = lax.broadcasted_iota(jnp.int32, (hi, bq), 1) + i * bq
                pt = jnp.where(kr <= qc, jnp.exp(st), 0.0)
            else:
                pt = jnp.exp(st)
            dst = (pt * _nt(vh[:hi], gh)).astype(jnp.bfloat16)
            dvn = _nn(pt.astype(jnp.bfloat16), gh)
            dkn = _nn(dst, qh)
            if i == rows // bq - 1:
                dva[h, :hi] = dvn
                dka[h, :hi] = dkn
            else:
                dva[h, :hi] += dvn
                dka[h, :hi] += dkn
            dqt.append(_nn(kt[:, :hi], dst))
        dq = jnp.concatenate([dqt[0][:HEAD], dqt[1][HEAD:]], axis=0).T
        dq_ref[at, :] = (dq * (HEAD ** -0.5)).astype(jnp.bfloat16)
    first = kl < HEAD
    dk_ref[...] = jnp.where(first, dka[0], dka[1]).astype(jnp.bfloat16)
    dv_ref[...] = jnp.where(first, dva[0], dva[1]).astype(jnp.bfloat16)

def attn_bwd(length, q, k, v, o, g, lse, causal, bq=256):
    rows, cols = q.shape
    keys = k.shape[0]
    pairs = cols // 128
    el = pairs * 2 * rows * keys
    qs = pl.BlockSpec((rows, 128), lambda p, n: (0, p))
    ks = pl.BlockSpec((keys, 128), lambda p, n: (0, p))
    return pl.pallas_call(
        functools.partial(bwd_kernel, causal=causal, bq=bq),
        out_shape=(jax.ShapeDtypeStruct((rows, cols), jnp.bfloat16), jax.ShapeDtypeStruct((keys, cols), jnp.bfloat16), jax.ShapeDtypeStruct((keys, cols), jnp.bfloat16)),
        grid_spec=pltpu.PrefetchScalarGridSpec(
            num_scalar_prefetch=1, grid=(pairs,),
            in_specs=[qs, ks, ks, qs, qs, pl.BlockSpec((rows, 128), lambda p, n: (0, 0))],
            out_specs=[qs, ks, ks],
            scratch_shapes=[pltpu.VMEM((2, keys, 128), jnp.float32), pltpu.VMEM((2, keys, 128), jnp.float32)],
        ),
        compiler_params=pltpu.CompilerParams(dimension_semantics=("arbitrary",), vmem_limit_bytes=48 << 20),
        cost_estimate=pl.CostEstimate(flops=40 * el * 64, bytes_accessed=16 * rows * cols, transcendentals=el),
        name="attend_backward",
    )(length, q, k, v, o, g, lse)

CHUNK = 512
SPAN = 256


def reduce_kernel(spots, count, results, *refs):
    own, other, out, rest = refs[:count], refs[count : 2 * count], refs[2 * count : 2 * count + results], refs[2 * count + results :]
    held, ysum, zgot, full, mine, load, store, xs, xr, ys, yr, zs, zr, bs, br, es, er = rest
    seq, ya, za = lax.axis_index("g"), lax.axis_index("y"), lax.axis_index("z")
    peers = {1: za + 1 - 2 * (za % 2), 2: (za + 2) % 4, 3: 3 - za}
    total = len(spots)

    def remote(src, dst, send, recv, where):
        return pltpu.make_async_remote_copy(src_ref=src, dst_ref=dst, send_sem=send, recv_sem=recv, device_id=where, device_id_type=pl.DeviceIdType.MESH)

    def block(at, size):
        return pl.ds(pl.multiple_of(at * size, size), size)

    def x_copy(k):
        a, r, c, n, o, q = spots[k]
        return remote(other[a].at[pl.ds(r, n), pl.ds(c, SPAN)], held.at[k, pl.ds(0, n)], xs.at[k], xr.at[k], {"g": 1 - seq})

    def own_copy(k):
        a, r, c, n, o, q = spots[k]
        return pltpu.make_async_copy(own[a].at[pl.ds(r, n), pl.ds(c, SPAN)], mine.at[k % 4, pl.ds(0, n)], load.at[k % 4])

    def y_copy(k):
        h = spots[k][3] // 2
        return remote(held.at[k, block(1 - ya, h)], ysum.at[k, pl.ds(0, h)], ys.at[k], yr.at[k], {"y": 1 - ya})

    def z_copy(k, d):
        p = spots[k][3] // 8
        return remote(ysum.at[k, block(peers[d], p)], zgot.at[k, d - 1, pl.ds(0, p)], zs.at[k, d - 1], zr.at[k, d - 1], {"z": peers[d]})

    def zb_copy(k, d):
        rows = full.at[k, block(ya * 4 + za, spots[k][3] // 8)]
        return remote(rows, rows, bs.at[k, d - 1], br.at[k, d - 1], {"z": peers[d]})

    def yb_copy(k):
        rows = full.at[k, block(ya, spots[k][3] // 2)]
        return remote(rows, rows, es.at[k], er.at[k], {"y": 1 - ya})

    def out_copy(k):
        a, r, c, n, o, q = spots[k]
        return pltpu.make_async_copy(full.at[k, pl.ds(0, n)], out[o].at[pl.ds(q, n), pl.ds(c, SPAN)], store.at[k])

    def to_y(k):
        n = spots[k][3]
        own_copy(k).wait()
        x_copy(k).wait_recv()
        held[k, :n] = held[k, :n] + mine[k % 4, :n]
        y_copy(k).start()

    def to_z(k):
        h = spots[k][3] // 2
        y_copy(k).wait_recv()
        ysum[k, :h] = ysum[k, :h] + held[k, block(ya, h)]
        for d in (1, 2, 3):
            z_copy(k, d).start()

    def back_z(k):
        p = spots[k][3] // 8
        for d in (1, 2, 3):
            z_copy(k, d).wait_recv()
        rows = ysum[k, block(za, p)].astype(F32)
        for d in (1, 2, 3):
            rows = rows + zgot[k, d - 1, :p].astype(F32)
        full[k, block(ya * 4 + za, p)] = rows.astype(LOW)
        for d in (1, 2, 3):
            zb_copy(k, d).start()

    def back_y(k):
        for d in (1, 2, 3):
            zb_copy(k, d).wait_recv()
        yb_copy(k).start()

    def finish(k):
        yb_copy(k).wait_recv()
        out_copy(k).start()

    barrier = pltpu.get_barrier_semaphore()
    everyone = [{"g": 1 - seq}, {"y": 1 - ya}] + [{"z": peers[d]} for d in (1, 2, 3)]
    for where in everyone:
        pl.semaphore_signal(barrier, inc=1, device_id=where, device_id_type=pl.DeviceIdType.MESH)
    for k in range(3):
        own_copy(k).start()
    pl.semaphore_wait(barrier, len(everyone))
    stages = (to_y, to_z, back_z, back_y, finish)
    ahead = 3
    for k in range(min(ahead, total)):
        x_copy(k).start()
    for step in range(total + len(stages) - 1):
        if step + ahead < total:
            x_copy(step + ahead).start()
        for at, stage in enumerate(stages):
            if 0 <= step - at < total:
                stage(step - at)
        if step + 3 < total:
            own_copy(step + 3).start()
    for k in range(total):
        x_copy(k).wait_send()
        y_copy(k).wait_send()
        yb_copy(k).wait_send()
        out_copy(k).wait()
        for d in (1, 2, 3):
            z_copy(k, d).wait_send()
            zb_copy(k, d).wait_send()


def reduce_all(pairs, places, results):
    spots = []
    for a, (part, unused) in enumerate(pairs):
        rows, cols = part.shape
        size = min(CHUNK, rows)
        for r in range(0, rows, size):
            for c in range(0, cols, SPAN):
                spots.append((a, r, c, size, places[a][0], places[a][1] + r))
    count, total = len(pairs), len(spots)
    most = max(s[3] for s in spots)
    any_space = pl.BlockSpec(memory_space=pl.ANY)
    dma = pltpu.SemaphoreType.DMA
    size = sum(own.size for own, unused in pairs)
    return pl.pallas_call(
        functools.partial(reduce_kernel, tuple(spots), count, len(results)),
        out_shape=[jax.ShapeDtypeStruct(shape, LOW) for shape in results],
        in_specs=[any_space] * (2 * count),
        out_specs=[any_space] * len(results),
        scratch_shapes=[
            pltpu.VMEM((total, most, SPAN), LOW),
            pltpu.VMEM((total, most // 2, SPAN), LOW),
            pltpu.VMEM((total, 3, most // 8, SPAN), LOW),
            pltpu.VMEM((total, most, SPAN), LOW),
            pltpu.VMEM((4, most, SPAN), LOW),
            dma((4,)), dma((total,)),
            dma((total,)), dma((total,)), dma((total,)), dma((total,)),
            dma((total, 3)), dma((total, 3)), dma((total, 3)), dma((total, 3)),
            dma((total,)), dma((total,)),
        ],
        compiler_params=pltpu.CompilerParams(collective_id=0, has_side_effects=True, vmem_limit_bytes=48 << 20),
        cost_estimate=pl.CostEstimate(flops=4 * size, bytes_accessed=400 * size, transcendentals=0),
        name="reduce_gradients",
    )(*[p[0] for p in pairs], *[p[1] for p in pairs])


residual_scale = 300.0**0.25
norm_epsilon = 1e-05
LOW = jnp.bfloat16
F32 = jnp.float32


def tn(rows, grads):
    return lax.dot_general(rows, grads, (((0,), (0,)), ((), ())), preferred_element_type=F32)


def gelu_exact(pre_rows):
    return jax.nn.gelu(pre_rows, approximate=False)


def gelu_backward(pre_rows, grad_rows):
    unused, pullback = jax.vjp(gelu_exact, pre_rows)
    return pullback(grad_rows)[0]


def norm_forward(summed, gain_row, shift_row):
    row_mean = jnp.mean(summed, axis=-1, keepdims=True)
    centred = summed - row_mean
    variance = jnp.mean(centred * centred, axis=-1, keepdims=True)
    inverse = lax.rsqrt(variance + norm_epsilon)
    unit_rows = centred * inverse
    return unit_rows * gain_row + shift_row, unit_rows, inverse


def norm_backward(grad_out, unit_rows, inverse, gain_row):
    grad_unit = grad_out * gain_row
    first_mean = jnp.mean(grad_unit, axis=-1, keepdims=True)
    second_mean = jnp.mean(grad_unit * unit_rows, axis=-1, keepdims=True)
    return inverse * (grad_unit - first_mean - unit_rows * second_mean)


def layer(sizes, tokens, memory, cotangent, target_lengths, memory_lengths, self_inputs, self_output, cross_query, cross_memory, cross_output, feed_in, feed_out, proj_bias, feed_bias, branch_bias, norm_gain, norm_shift):
    zn, yn, gn, cn = sizes
    seq = lax.axis_index("g")
    core = lax.axis_index("c")
    width = self_output.shape[0]
    joined = width % 128 != 0

    def swap(rows):
        return lax.ppermute(rows, "c", [(0, 1), (1, 0)])

    def gather_rows(rows):
        if cn != 2:
            return lax.all_gather(rows, "c", axis=0, tiled=True)
        got = swap(rows)
        return jnp.where(core == 0, jnp.concatenate([rows, got]), jnp.concatenate([got, rows]))

    def sum_all(part):
        part = part.astype(LOW)
        if cn != 2:
            return lax.psum(part, "c").astype(F32)
        return part.astype(F32) + swap(part).astype(F32)

    def own_rows(rows):
        size = rows.shape[0] // cn
        return lax.dynamic_slice_in_dim(rows, core * size, size, 0)

    def sum_own(part):
        if cn != 2:
            return lax.psum_scatter(part.astype(LOW), "c", scatter_dimension=0, tiled=True).astype(F32)
        size = part.shape[0] // 2
        got = swap(lax.dynamic_slice_in_dim(part, (1 - core) * size, size, 0).astype(LOW))
        return lax.dynamic_slice_in_dim(part, core * size, size, 0) + got.astype(F32)

    def spread(shard, axis):
        every = [shard] + [lax.ppermute(shard, "g", [((i + k) % gn, i) for i in range(gn)]) for k in range(1, gn)]
        return [jnp.concatenate(every, axis=axis)] if joined else every

    def send_home(parts):
        total = parts[0]
        for k in range(1, gn):
            total = total + lax.ppermute(parts[k].astype(LOW), "g", [(i, (i + k) % gn) for i in range(gn)]).astype(F32)
        return total

    steps = [("y", 1, lax.axis_index("y"), yn)] if yn == 2 else []
    steps += [("z", 1 << b, lax.axis_index("z"), zn) for b in range((zn - 1).bit_length())]

    def pairwise(rows, axis, far, size):
        return lax.ppermute(rows, axis, [(i, i ^ far) for i in range(size)])

    def sum_groups(total):
        for axis, far, at, size in steps:
            half = total.shape[0] // 2
            bit = (at // far) % 2
            away = lax.dynamic_slice_in_dim(total, (1 - bit) * half, half, 0).astype(LOW)
            keep = lax.dynamic_slice_in_dim(total, bit * half, half, 0)
            total = keep + pairwise(away, axis, far, size).astype(F32)
        total = total.astype(LOW)
        for axis, far, at, size in reversed(steps):
            got = pairwise(total, axis, far, size)
            total = jnp.where((at // far) % 2 == 0, jnp.concatenate([total, got]), jnp.concatenate([got, total]))
        return total.astype(F32)

    def fetch_slices(shards):
        at = lax.axis_index("z") * yn + lax.axis_index("y")
        pieces = [lax.dynamic_slice_in_dim(shard, at * (shard.shape[0] // (zn * yn)), shard.shape[0] // (zn * yn), 0) for shard in shards]
        pieces = [jnp.stack(pieces)] if pieces[0].shape == pieces[1].shape else [piece[None] for piece in pieces]
        return [[lax.ppermute(piece, "g", [((i + k) % gn, i) for i in range(gn)]) for piece in pieces] for k in range(1, gn)]

    def spread_wide(shards, slices):
        every = [[shard] for shard in shards]
        for got in slices:
            whole = [rows for piece in got for rows in lax.all_gather(piece, ("z", "y"), axis=1, tiled=True)]
            for at, rows in enumerate(whole):
                every[at].append(rows)
        return [[jnp.concatenate(part, axis=1 - at)] if joined else part for at, part in enumerate(every)]

    def parts_of(values, axis):
        return jnp.split(values[0], gn, axis=axis) if joined else values

    target_length = lax.dynamic_slice_in_dim(target_lengths, seq, 1, 0)
    memory_length = lax.dynamic_slice_in_dim(memory_lengths, seq, 1, 0)

    def after(value, *needed):
        return lax.optimization_barrier((value,) + needed)[0]

    token_all = gather_rows(tokens)
    biases = spread(jnp.concatenate([proj_bias, feed_bias.reshape(-1, width)]), 1)
    feed_rows = feed_bias.shape[0] // width
    if joined:
        halves = jnp.split(biases[0], gn, axis=1)
        b_in = [jnp.concatenate([part[4:].reshape(-1) for part in halves])]
    else:
        b_in = [part[4:].reshape(-1) for part in biases]
    b_proj = [part[:4] for part in biases]
    slices = fetch_slices((feed_in, feed_out))
    w_self = spread(after(self_inputs, token_all, biases[-1], slices[-1][0]), 2)
    w_in, w_out = spread_wide((feed_in, feed_out), slices)
    self_q, self_k, self_v, self_mixed, self_lse = [], [], [], [], []
    shards = range(len(w_self))
    for s in shards:
        self_q.append((_nn(token_all, w_self[s][0]) + b_proj[s][0]).astype(LOW))
        self_k.append(_nn(token_all, w_self[s][1]).astype(LOW))
        self_v.append((_nn(token_all, w_self[s][2]) + b_proj[s][1]).astype(LOW))
        mixed, lse = attn_fwd(target_length, self_q[s], self_k[s], self_v[s], True)
        self_mixed.append(mixed)
        self_lse.append(lse)
    first = self_mixed[0]
    w_self_out = spread(after(self_output, first), 0)
    memory_all = gather_rows(after(memory, first))
    w_cross_mem = spread(after(cross_memory, first), 2)
    w_cross_q = spread(after(cross_query, first), 1)
    w_cross_out = spread(after(cross_output, first), 0)
    cot_all = gather_rows(after(cotangent, self_mixed[-1]))

    cross_k = [_nn(memory_all, w_cross_mem[s][0]).astype(LOW) for s in shards]
    cross_v = [(_nn(memory_all, w_cross_mem[s][1]) + b_proj[s][3]).astype(LOW) for s in shards]
    branch_one = sum_all(sum(_nn(self_mixed[s], w_self_out[s]) for s in shards)) + branch_bias[0]
    normed_one, unit_one, inverse_one = norm_forward(residual_scale * token_all.astype(F32) + branch_one, norm_gain[0], norm_shift[0])
    second = normed_one.astype(LOW)
    cross_q = [(_nn(second, w_cross_q[s]) + b_proj[s][2]).astype(LOW) for s in shards]
    cross_mixed, cross_lse = zip(*[attn_fwd(memory_length, cross_q[s], cross_k[s], cross_v[s], False) for s in shards])
    branch_two = sum_all(sum(_nn(cross_mixed[s], w_cross_out[s]) for s in shards)) + branch_bias[1]
    normed_two, unit_two, inverse_two = norm_forward(residual_scale * normed_one + branch_two, norm_gain[1], norm_shift[1])
    third = normed_two.astype(LOW)
    hidden_pre = [_nn(third, w_in[s]) + b_in[s].astype(F32) for s in shards]
    hidden = [gelu_exact(hidden_pre[s]).astype(LOW) for s in shards]
    branch_three = sum_all(sum(_nn(hidden[s], w_out[s]) for s in shards)) + branch_bias[2]
    normed_three, unit_three, inverse_three = norm_forward(residual_scale * normed_two + branch_three, norm_gain[2], norm_shift[2])
    block_out = own_rows(normed_three.astype(LOW))

    cot = cot_all.astype(F32)
    grad_three = norm_backward(cot, unit_three, inverse_three, norm_gain[2])
    low_three = grad_three.astype(LOW)
    grad_hidden = [_nt(low_three, w_out[s]) for s in shards]
    feed_out_parts = parts_of([tn(hidden[s], low_three) for s in shards], 0)
    grad_pre = [gelu_backward(hidden_pre[s], grad_hidden[s]).astype(LOW) for s in shards]
    feed_in_parts = parts_of([tn(third, grad_pre[s]) for s in shards], 1)
    feed_out_sum, feed_in_sum = [lax.psum(send_home(part).astype(LOW), ("z", "y")).astype(F32) for part in (feed_out_parts, feed_in_parts)]
    grad_normed_two = residual_scale * grad_three + sum_all(sum(_nt(grad_pre[s], w_in[s]) for s in shards))
    grad_two = norm_backward(grad_normed_two, unit_two, inverse_two, norm_gain[1])
    low_two = grad_two.astype(LOW)
    grad_cross_mixed = [_nt(low_two, w_cross_out[s]).astype(LOW) for s in shards]
    cross_out_parts = parts_of([tn(cross_mixed[s], low_two) for s in shards], 0)
    cross_dq, cross_dk, cross_dv = zip(*[attn_bwd(memory_length, cross_q[s], cross_k[s], cross_v[s], cross_mixed[s], grad_cross_mixed[s], cross_lse[s], False) for s in shards])
    grad_normed_one = residual_scale * grad_two + sum_all(sum(_nt(cross_dq[s], w_cross_q[s]) for s in shards))
    cross_parts = [parts_of([tn(second, cross_dq[s]) for s in shards], 1), parts_of([tn(memory_all, cross_dk[s]) for s in shards], 1), parts_of([tn(memory_all, cross_dv[s]) for s in shards], 1)]
    grad_memory = sum_own(sum(_nt(cross_dk[s], w_cross_mem[s][0]) + _nt(cross_dv[s], w_cross_mem[s][1]) for s in shards)).astype(LOW)
    grad_one = norm_backward(grad_normed_one, unit_one, inverse_one, norm_gain[0])
    low_one = grad_one.astype(LOW)
    grad_self_mixed = [_nt(low_one, w_self_out[s]).astype(LOW) for s in shards]
    self_out_parts = parts_of([tn(self_mixed[s], low_one) for s in shards], 0)
    self_dq, self_dk, self_dv = zip(*[attn_bwd(target_length, self_q[s], self_k[s], self_v[s], self_mixed[s], grad_self_mixed[s], self_lse[s], True) for s in shards])
    token_part = sum(_nt(self_dq[s], w_self[s][0]) + _nt(self_dk[s], w_self[s][1]) + _nt(self_dv[s], w_self[s][2]) for s in shards)
    grad_tokens = (residual_scale * own_rows(grad_one) + sum_own(token_part)).astype(LOW)

    def sums(rows):
        return jnp.sum(rows.astype(F32), axis=0)

    terms = jnp.stack([sums(low_one), sums(low_two), sums(low_three), sums(grad_normed_one * unit_one), sums(grad_normed_two * unit_two), sums(cot * unit_three), sums(grad_normed_one), sums(grad_normed_two), sums(cot)])
    proj_sums = parts_of([jnp.stack([sums(self_dq[s]), sums(self_dv[s]), sums(cross_dq[s]), sums(cross_dv[s])]) for s in shards], 1)
    feed_sums = parts_of([sums(grad_pre[s]) for s in shards], 0)
    self_parts = [parts_of([tn(token_all, grads[s]) for s in shards], 1) for grads in (self_dq, self_dk, self_dv)]
    smalls = []
    for k in range(gn):
        small = lax.dynamic_slice_in_dim(terms, ((seq + k) % gn * cn + core) * width, width, 1)
        small = jnp.concatenate([small, proj_sums[k], feed_sums[k].reshape(-1, width)])
        smalls.append(jnp.pad(small, ((0, 16 * zn * yn - small.shape[0]), (0, 0))))
    model = tokens.shape[1]
    groups = [[cross_out_parts], cross_parts[:1], cross_parts[1:], [self_out_parts], self_parts, [smalls]]
    if (zn, yn, gn, cn, width) == (4, 2, 2, 2, SPAN):
        pairs, places, results = [], [], []
        for at, group in enumerate(groups):
            rows = 0
            for part in group:
                pairs.append((part[0].astype(LOW), part[1].astype(LOW)))
                places.append((at, rows))
                rows += part[0].shape[0]
            results.append((rows, group[0][0].shape[1]))
        sums_low = reduce_all(pairs, places, results)
    else:
        sums_low = [sum_groups(send_home([jnp.concatenate([part[k] for part in group]) for k in range(gn)])) for group in groups]
    cross_out_sum, cross_q_sum, cross_mem_sum, self_out_sum, self_in_sum, small = [rows.astype(F32) for rows in sums_low]
    return (block_out, grad_tokens, grad_memory, self_in_sum.reshape(3, model, width), self_out_sum, cross_q_sum, cross_mem_sum.reshape(2, model, width), cross_out_sum, feed_in_sum, feed_out_sum, small[9:13], small[13:13 + feed_rows].reshape(-1), small[0:3], small[3:6], small[6:9])


def solution(mesh):
    dp, mp = mesh.shape["dp"], mesh.shape["mp"]

    def whole(*args):
        yn = 2 if dp % 2 == 0 else 1
        gn = args[3].shape[0] // dp
        sizes = (dp // yn, yn, gn, mp // gn)
        fine = Mesh(mesh.devices.reshape(sizes), ("z", "y", "g", "c"))
        d, m = ("z", "y"), ("g", "c")
        rows, wide, tall = P(d + m, None), P(None, m), P(m, None)
        stack = P(None, None, m)
        in_specs = (rows, rows, rows, P(d), P(d), stack, tall, wide, stack, tall, wide, tall, wide, P(m), P(), P(), P())
        out_specs = (rows, rows, rows, stack, tall, wide, stack, tall, wide, tall, wide, P(m), wide, wide, wide)
        return jax.shard_map(functools.partial(layer, sizes), mesh=fine, in_specs=in_specs, out_specs=out_specs, check_vma=False)(*args)

    return whole
```

```python
import functools

import jax, jax.numpy as jnp
from jax import lax
from jax.experimental import pallas as pl
from jax.experimental.pallas import tpu as pltpu
from jax.sharding import Mesh
from jax.sharding import PartitionSpec as P

HEAD = 64
NEG = -1e30

def _nt(a, b):
    return lax.dot_general(a, b, (((1,), (1,)), ((), ())), preferred_element_type=jnp.float32)

def _nn(a, b):
    return lax.dot_general(a, b, (((1,), (0,)), ((), ())), preferred_element_type=jnp.float32)

def _lanes(rows):
    return lax.broadcasted_iota(jnp.int32, (rows, 128), 1)

def _put(base, lane, pairs):
    for at, val in pairs:
        base = jnp.where(lane == at, val, base)
    return base

def fwd_kernel(len_ref, q_ref, k_ref, v_ref, o_ref, lse_ref, *, causal, bq):
    p = pl.program_id(0)
    rows, keys = q_ref.shape[0], k_ref.shape[0]
    length = len_ref[0]
    kl = _lanes(keys)
    kpos = lax.broadcasted_iota(jnp.int32, (keys, 128), 0)
    kbias = jnp.where(kpos < length, 0.0, NEG)
    k2 = k_ref[...].astype(jnp.float32)
    v2 = v_ref[...].astype(jnp.float32)
    ql = _lanes(bq)
    heads = []
    for h in range(2):
        mine = (kl // HEAD) == h
        other = HEAD * (1 - h)
        kh = jnp.where(mine, k2, jnp.where(kl == other, kbias, 0.0)).astype(jnp.bfloat16)
        vh = jnp.where(mine, v2, jnp.where(kl == other, 1.0, 0.0)).astype(jnp.bfloat16)
        heads.append((kh, vh))
    for i in range(rows // bq):
        q2 = q_ref[pl.ds(i * bq, bq), :].astype(jnp.float32) * (HEAD ** -0.5)
        out = jnp.zeros((bq, 128), jnp.float32)
        lse_all = lse_ref[pl.ds(i * bq, bq), :]
        for h in range(2):
            kh, vh = heads[h]
            mine = (ql // HEAD) == h
            other = HEAD * (1 - h)
            qh = jnp.where(mine, q2, jnp.where(ql == other, 1.0, 0.0)).astype(jnp.bfloat16)
            if causal:
                lo = i * bq
                sd = _nt(qh, kh[lo:lo + bq])
                r = lax.broadcasted_iota(jnp.int32, (bq, bq), 0)
                c = lax.broadcasted_iota(jnp.int32, (bq, bq), 1)
                sd = jnp.where(c <= r, sd, NEG)
                m = jnp.max(sd, axis=1, keepdims=True)
                if lo:
                    sl = _nt(qh, kh[:lo])
                    m = jnp.maximum(m, jnp.max(sl, axis=1, keepdims=True))
                    acc = _nn(jnp.exp(sl - m).astype(jnp.bfloat16), vh[:lo])
                    acc += _nn(jnp.exp(sd - m).astype(jnp.bfloat16), vh[lo:lo + bq])
                else:
                    acc = _nn(jnp.exp(sd - m).astype(jnp.bfloat16), vh[:bq])
            else:
                s = _nt(qh, kh)
                m = jnp.max(s, axis=1, keepdims=True)
                acc = _nn(jnp.exp(s - m).astype(jnp.bfloat16), vh)
            total = jnp.sum(jnp.where(ql == other, acc, 0.0), axis=1, keepdims=True)
            out = jnp.where(mine, acc / total, out)
            lse_all = jnp.where(ql == 2 * p + h, m + jnp.log(total), lse_all)
        o_ref[pl.ds(i * bq, bq), :] = out.astype(jnp.bfloat16)
        lse_ref[pl.ds(i * bq, bq), :] = lse_all

def attn_fwd(length, q, k, v, causal, bq=256):
    rows, cols = q.shape
    keys = k.shape[0]
    pairs = cols // 128
    el = pairs * 2 * rows * keys
    return pl.pallas_call(
        functools.partial(fwd_kernel, causal=causal, bq=bq),
        out_shape=(jax.ShapeDtypeStruct((rows, cols), jnp.bfloat16), jax.ShapeDtypeStruct((rows, 128), jnp.float32)),
        grid_spec=pltpu.PrefetchScalarGridSpec(
            num_scalar_prefetch=1, grid=(pairs,),
            in_specs=[pl.BlockSpec((rows, 128), lambda p, n: (0, p)), pl.BlockSpec((keys, 128), lambda p, n: (0, p)), pl.BlockSpec((keys, 128), lambda p, n: (0, p))],
            out_specs=[pl.BlockSpec((rows, 128), lambda p, n: (0, p)), pl.BlockSpec((rows, 128), lambda p, n: (0, 0))],
        ),
        compiler_params=pltpu.CompilerParams(dimension_semantics=("arbitrary",), vmem_limit_bytes=40 << 20),
        cost_estimate=pl.CostEstimate(flops=16 * el * 64, bytes_accessed=8 * rows * cols, transcendentals=el),
        name="attend_forward",
    )(length, q, k, v)

def split3(x):
    a = x.astype(jnp.bfloat16).astype(jnp.float32)
    b = (x - a).astype(jnp.bfloat16).astype(jnp.float32)
    return a, b, x - a - b


def key_side(k2, v2, length):
    keys = k2.shape[0]
    kl = _lanes(keys)
    kbias = jnp.where(lax.broadcasted_iota(jnp.int32, (keys, 128), 0) < length, 0.0, NEG)
    k2, v2 = k2.astype(jnp.float32), v2.astype(jnp.float32)
    heads = []
    for h in range(2):
        mine = (kl // HEAD) == h
        other = HEAD * (1 - h)
        ones = (kl > other) & (kl < other + 4)
        kh = jnp.where(mine, k2, jnp.where(kl == other, kbias, jnp.where(ones, 1.0, 0.0))).astype(jnp.bfloat16)
        vh = jnp.where(mine, v2, jnp.where(ones, 1.0, 0.0)).astype(jnp.bfloat16)
        heads.append((kh, vh, kh.T))
    return heads


def query_block(heads, q2, o2, g2, lse_all, pair, i, last, causal, dka, dva):
    bq = q2.shape[0]
    keys = heads[0][0].shape[0]
    ql = _lanes(bq)
    q2 = q2.astype(jnp.float32) * (HEAD ** -0.5)
    g2 = g2.astype(jnp.float32)
    go = g2 * o2.astype(jnp.float32)
    dqt = []
    for h in range(2):
        kh, vh, kt = heads[h]
        mine = (ql // HEAD) == h
        other = HEAD * (1 - h)
        lse = jnp.sum(jnp.where(ql == 2 * pair + h, lse_all, 0.0), axis=1, keepdims=True)
        delta = jnp.sum(jnp.where(mine, go, 0.0), axis=1, keepdims=True)
        la, lb, lc = split3(-lse)
        da, db, dc = split3(-delta)
        qh = _put(jnp.where(mine, q2, 0.0), ql, ((other, 1.0), (other + 1, la), (other + 2, lb), (other + 3, lc))).astype(jnp.bfloat16)
        gh = _put(jnp.where(mine, g2, 0.0), ql, ((other + 1, da), (other + 2, db), (other + 3, dc))).astype(jnp.bfloat16)
        hi = (i + 1) * bq if causal else keys
        st = _nt(kh[:hi], qh)
        if causal:
            kr = lax.broadcasted_iota(jnp.int32, (hi, bq), 0)
            qc = lax.broadcasted_iota(jnp.int32, (hi, bq), 1) + i * bq
            pt = jnp.where(kr <= qc, jnp.exp(st), 0.0)
        else:
            pt = jnp.exp(st)
        dst = (pt * _nt(vh[:hi], gh)).astype(jnp.bfloat16)
        dvn = _nn(pt.astype(jnp.bfloat16), gh)
        dkn = _nn(dst, qh)
        if last:
            dva[h, :hi] = dvn
            dka[h, :hi] = dkn
        else:
            dva[h, :hi] += dvn
            dka[h, :hi] += dkn
        dqt.append(_nn(kt[:, :hi], dst))
    dq = jnp.concatenate([dqt[0][:HEAD], dqt[1][HEAD:]], axis=0).T
    return (dq * (HEAD ** -0.5)).astype(jnp.bfloat16)


def bwd_kernel(len_ref, q_ref, k_ref, v_ref, o_ref, g_ref, lse_ref, dq_ref, dk_ref, dv_ref, dka, dva, *, causal, bq):
    rows, keys = q_ref.shape[0], k_ref.shape[0]
    heads = key_side(k_ref[...], v_ref[...], len_ref[0])
    blocks = rows // bq
    for i in reversed(range(blocks)):
        at = pl.ds(i * bq, bq)
        dq_ref[at, :] = query_block(heads, q_ref[at, :], o_ref[at, :], g_ref[at, :], lse_ref[at, :], pl.program_id(0), i, i == blocks - 1, causal, dka, dva)
    first = _lanes(keys) < HEAD
    dk_ref[...] = jnp.where(first, dka[0], dka[1]).astype(jnp.bfloat16)
    dv_ref[...] = jnp.where(first, dva[0], dva[1]).astype(jnp.bfloat16)

def attn_bwd(length, q, k, v, o, g, lse, causal, bq=256):
    rows, cols = q.shape
    keys = k.shape[0]
    pairs = cols // 128
    el = pairs * 2 * rows * keys
    qs = pl.BlockSpec((rows, 128), lambda p, n: (0, p))
    ks = pl.BlockSpec((keys, 128), lambda p, n: (0, p))
    return pl.pallas_call(
        functools.partial(bwd_kernel, causal=causal, bq=bq),
        out_shape=(jax.ShapeDtypeStruct((rows, cols), jnp.bfloat16), jax.ShapeDtypeStruct((keys, cols), jnp.bfloat16), jax.ShapeDtypeStruct((keys, cols), jnp.bfloat16)),
        grid_spec=pltpu.PrefetchScalarGridSpec(
            num_scalar_prefetch=1, grid=(pairs,),
            in_specs=[qs, ks, ks, qs, qs, pl.BlockSpec((rows, 128), lambda p, n: (0, 0))],
            out_specs=[qs, ks, ks],
            scratch_shapes=[pltpu.VMEM((2, keys, 128), jnp.float32), pltpu.VMEM((2, keys, 128), jnp.float32)],
        ),
        compiler_params=pltpu.CompilerParams(dimension_semantics=("arbitrary",), vmem_limit_bytes=48 << 20),
        cost_estimate=pl.CostEstimate(flops=40 * el * 64, bytes_accessed=16 * rows * cols, transcendentals=el),
        name="attend_backward",
    )(length, q, k, v, o, g, lse)

CHUNK = 512
SPAN = 256


class Pipeline:
    AHEAD = 3

    def __init__(self, total, scratch):
        self.spots, self.total, self.step, self.sent, self.loaded = [], total, 0, 0, 0
        (self.held, self.ysum, self.zgot, self.full, self.mine, self.load, self.store, self.xs, self.xr, self.ys, self.yr, self.zs, self.zr, self.bs, self.br, self.es, self.er) = scratch
        self.seq, self.ya, za = lax.axis_index("g"), lax.axis_index("y"), lax.axis_index("z")
        self.za = za
        self.peers = {1: za + 1 - 2 * (za % 2), 2: (za + 2) % 4, 3: 3 - za}
        self.stages = (self.to_y, self.to_z, self.back_z, self.back_y, self.finish)

    @staticmethod
    def scratch(total, most):
        dma = pltpu.SemaphoreType.DMA
        return [
            pltpu.VMEM((total, most, SPAN), LOW),
            pltpu.VMEM((total, most // 2, SPAN), LOW),
            pltpu.VMEM((total, 3, most // 8, SPAN), LOW),
            pltpu.VMEM((total, most, SPAN), LOW),
            pltpu.VMEM((4, most, SPAN), LOW),
            dma((4,)), dma((total,)),
            dma((total,)), dma((total,)), dma((total,)), dma((total,)),
            dma((total, 3)), dma((total, 3)), dma((total, 3)), dma((total, 3)),
            dma((total,)), dma((total,)),
        ]

    def greet(self, more=()):
        barrier = pltpu.get_barrier_semaphore()
        everyone = [{"g": 1 - self.seq}, {"y": 1 - self.ya}] + [{"z": self.peers[d]} for d in (1, 2, 3)] + list(more)
        for where in everyone:
            pl.semaphore_signal(barrier, inc=1, device_id=where, device_id_type=pl.DeviceIdType.MESH)
        pl.semaphore_wait(barrier, len(everyone))

    def add(self, own, other, out, out_row):
        rows, cols = own.shape
        size = min(CHUNK, rows)
        for r in range(0, rows, size):
            for c in range(0, cols, SPAN):
                self.spots.append((own, other, r, c, size, out, out_row + r))
        self.feed()

    def feed(self):
        while self.sent < min(len(self.spots), self.step + self.AHEAD):
            self.x_copy(self.sent).start()
            self.own_copy(self.sent).start()
            self.sent += 1

    def tick(self, times=1):
        for unused in range(times):
            if self.step >= self.total + len(self.stages) - 1:
                return
            for at, stage in enumerate(self.stages):
                if 0 <= self.step - at < self.total:
                    stage(self.step - at)
            self.step += 1
            self.feed()

    def drain(self):
        assert len(self.spots) == self.total
        self.tick(self.total + len(self.stages))
        for k in range(self.total):
            self.x_copy(k).wait_send()
            self.y_copy(k).wait_send()
            self.yb_copy(k).wait_send()
            self.out_copy(k).wait()
            for d in (1, 2, 3):
                self.z_copy(k, d).wait_send()
                self.zb_copy(k, d).wait_send()

    @staticmethod
    def remote(src, dst, send, recv, where):
        return pltpu.make_async_remote_copy(src_ref=src, dst_ref=dst, send_sem=send, recv_sem=recv, device_id=where, device_id_type=pl.DeviceIdType.MESH)

    @staticmethod
    def block(at, size):
        return pl.ds(pl.multiple_of(at * size, size), size)

    def x_copy(self, k):
        own, other, r, c, n, o, q = self.spots[k]
        return self.remote(other.at[pl.ds(r, n), pl.ds(c, SPAN)], self.held.at[k, pl.ds(0, n)], self.xs.at[k], self.xr.at[k], {"g": 1 - self.seq})

    def own_copy(self, k):
        own, other, r, c, n, o, q = self.spots[k]
        return pltpu.make_async_copy(own.at[pl.ds(r, n), pl.ds(c, SPAN)], self.mine.at[k % 4, pl.ds(0, n)], self.load.at[k % 4])

    def y_copy(self, k):
        h = self.spots[k][4] // 2
        return self.remote(self.held.at[k, self.block(1 - self.ya, h)], self.ysum.at[k, pl.ds(0, h)], self.ys.at[k], self.yr.at[k], {"y": 1 - self.ya})

    def z_copy(self, k, d):
        p = self.spots[k][4] // 8
        return self.remote(self.ysum.at[k, self.block(self.peers[d], p)], self.zgot.at[k, d - 1, pl.ds(0, p)], self.zs.at[k, d - 1], self.zr.at[k, d - 1], {"z": self.peers[d]})

    def zb_copy(self, k, d):
        rows = self.full.at[k, self.block(self.ya * 4 + self.za, self.spots[k][4] // 8)]
        return self.remote(rows, rows, self.bs.at[k, d - 1], self.br.at[k, d - 1], {"z": self.peers[d]})

    def yb_copy(self, k):
        rows = self.full.at[k, self.block(self.ya, self.spots[k][4] // 2)]
        return self.remote(rows, rows, self.es.at[k], self.er.at[k], {"y": 1 - self.ya})

    def out_copy(self, k):
        own, other, r, c, n, o, q = self.spots[k]
        return pltpu.make_async_copy(self.full.at[k, pl.ds(0, n)], o.at[pl.ds(q, n), pl.ds(c, SPAN)], self.store.at[k])

    def to_y(self, k):
        n = self.spots[k][4]
        self.own_copy(k).wait()
        self.x_copy(k).wait_recv()
        self.held[k, :n] = self.held[k, :n] + self.mine[k % 4, :n]
        self.y_copy(k).start()

    def to_z(self, k):
        h = self.spots[k][4] // 2
        self.y_copy(k).wait_recv()
        self.ysum[k, :h] = self.ysum[k, :h] + self.held[k, self.block(self.ya, h)]
        for d in (1, 2, 3):
            self.z_copy(k, d).start()

    def back_z(self, k):
        p = self.spots[k][4] // 8
        for d in (1, 2, 3):
            self.z_copy(k, d).wait_recv()
        rows = self.ysum[k, self.block(self.za, p)].astype(F32)
        for d in (1, 2, 3):
            rows = rows + self.zgot[k, d - 1, :p].astype(F32)
        self.full[k, self.block(self.ya * 4 + self.za, p)] = rows.astype(LOW)
        for d in (1, 2, 3):
            self.zb_copy(k, d).start()

    def back_y(self, k):
        for d in (1, 2, 3):
            self.zb_copy(k, d).wait_recv()
        self.yb_copy(k).start()

    def finish(self, k):
        self.yb_copy(k).wait_recv()
        self.out_copy(k).start()


def spot_count(shapes):
    return sum((rows // min(CHUNK, rows)) * (cols // SPAN) for rows, cols in shapes)


def self_back_kernel(carried, bq, len_ref, low, q0, k0, v0, o0, l0, q1, k1, v1, o1, l1, wo0, wo1, xt, w0, w1, small0, small1, *rest):
    own, other, rest = rest[:carried], rest[carried : 2 * carried], rest[2 * carried :]
    token_out, rest = rest[0], rest[1:]
    outs, rest = rest[: carried + 3], rest[carried + 3 :]
    gm, dq, dk, dv, dka, dva, go_own, go_other, gi_own, gi_other, sm_own, sm_other, part, got, part_send, part_recv = rest[:16]
    core = lax.axis_index("c")
    total = spot_count([ref.shape for ref in own] + [go_own.shape, gi_own.shape, sm_own.shape])
    pipe = Pipeline(total, rest[16:])
    pipe.greet([{"c": 1 - core}])
    for a, b, out in zip(own, other, outs):
        pipe.add(a, b, out, 0)
    shards = ((q0, k0, v0, o0, l0, wo0, w0, go_own, gi_own, sm_own, small0), (q1, k1, v1, o1, l1, wo1, w1, go_other, gi_other, sm_other, small1))
    rows = low.shape[0]
    blocks = rows // bq
    for s, (q, k, v, o, l, wo, w, go, gi, sm, small) in enumerate(shards):
        for c in range(0, low.shape[1], SPAN):
            go[:, c : c + SPAN] = tn(o[...], low[:, c : c + SPAN]).astype(LOW)
        for i in range(blocks):
            at = pl.ds(i * bq, bq)
            gm[s, at, :] = _nt(low[at, :], wo[...]).astype(LOW)
    pipe.add(go_own, go_other, outs[carried], 0)
    for s, (q, k, v, o, l, wo, w, go, gi, sm, small) in enumerate(shards):
        width = q.shape[1]
        for p in range(width // 128):
            cols = pl.ds(p * 128, 128)
            heads = key_side(k[:, cols], v[:, cols], len_ref[0])
            for i in reversed(range(blocks)):
                at = pl.ds(i * bq, bq)
                dq[s, at, cols] = query_block(heads, q[at, cols], o[at, cols], gm[s, at, cols], l[at, :], p, i, i == blocks - 1, True, dka, dva)
            first = _lanes(rows) < HEAD
            dk[s, :, cols] = jnp.where(first, dka[0], dka[1]).astype(LOW)
            dv[s, :, cols] = jnp.where(first, dva[0], dva[1]).astype(LOW)
            pipe.tick()
    for s, (q, k, v, o, l, wo, w, go, gi, sm, small) in enumerate(shards):
        for m, grads in enumerate((dq, dk, dv)):
            for i in range(blocks):
                at = pl.ds(i * bq, bq)
                gi[pl.ds(m * rows + i * bq, bq), :] = _nn(xt[at, :], grads[s]).astype(LOW)
        row = lax.broadcasted_iota(jnp.int32, sm.shape, 0)
        sums = [jnp.sum(grads[s].astype(F32), axis=0, keepdims=True) for grads in (dq, dv)]
        sm[...] = jnp.where(row == 9, sums[0], jnp.where(row == 10, sums[1], small[...])).astype(LOW)
    pipe.add(gi_own, gi_other, outs[carried + 1], 0)
    pipe.add(sm_own, sm_other, outs[carried + 2], 0)
    half = rows // 2
    exchange = Pipeline.remote(part, got, part_send, part_recv, {"c": 1 - core})

    def token_rows(start, size):
        at = pl.ds(pl.multiple_of(start, size), size)
        both = jnp.zeros((size, low.shape[1]), F32)
        for s, w in ((0, w0), (1, w1)):
            for m, grads in enumerate((dq, dk, dv)):
                both = both + _nt(grads[s, at, :], w[m])
        return both

    for i in range(0, half, bq):
        part[pl.ds(i, bq), :] = token_rows((1 - core) * half + i, bq).astype(LOW)
    exchange.start()
    pipe.tick()
    for i in range(0, half, bq):
        token_out[pl.ds(i, bq), :] = token_rows(core * half + i, bq)
    pipe.tick()
    exchange.wait()
    for i in range(0, half, bq):
        token_out[pl.ds(i, bq), :] += got[pl.ds(i, bq), :].astype(F32)
    pipe.drain()


def self_back(length, low, first, second, wo, xt, w, smalls, pairs, places, results, bq=256):
    rows, model = low.shape
    width = wo[0].shape[0]
    carried = len(pairs)
    any_space = pl.BlockSpec(memory_space=pl.ANY)
    vmem = pl.BlockSpec(memory_space=pltpu.VMEM)
    ends = [(width, model), (3 * rows, width), smalls[0].shape]
    total = spot_count([own.shape for own, unused in pairs] + ends)
    low_ram = lambda *shape: pltpu.VMEM(shape, LOW)
    return pl.pallas_call(
        functools.partial(self_back_kernel, carried, bq),
        out_shape=[jax.ShapeDtypeStruct((rows // 2, model), F32)] + [jax.ShapeDtypeStruct(own.shape, LOW) for own, unused in pairs] + [jax.ShapeDtypeStruct(shape, LOW) for shape in ends],
        in_specs=[pl.BlockSpec(memory_space=pltpu.SMEM)] + [vmem] * 18 + [any_space] * (2 * carried),
        out_specs=[vmem] + [any_space] * (carried + 3),
        scratch_shapes=[
            low_ram(2, rows, width), low_ram(2, rows, width), low_ram(2, rows, width), low_ram(2, rows, width),
            pltpu.VMEM((2, rows, 128), F32), pltpu.VMEM((2, rows, 128), F32),
            low_ram(width, model), low_ram(width, model), low_ram(3 * rows, width), low_ram(3 * rows, width),
            low_ram(*smalls[0].shape), low_ram(*smalls[0].shape),
            low_ram(rows // 2, model), low_ram(rows // 2, model), pltpu.SemaphoreType.DMA, pltpu.SemaphoreType.DMA,
        ] + Pipeline.scratch(total, CHUNK),
        compiler_params=pltpu.CompilerParams(collective_id=0, has_side_effects=True, vmem_limit_bytes=58 << 20),
        cost_estimate=pl.CostEstimate(flops=20 * rows * model * width, bytes_accessed=200 << 20, transcendentals=8 * rows * rows),
        name="self_backward",
    )(length, low, *first, *second, *wo, xt, *w, *smalls, *[p[0] for p in pairs], *[p[1] for p in pairs])


residual_scale = 300.0**0.25
norm_epsilon = 1e-05
LOW = jnp.bfloat16
F32 = jnp.float32


def tn(rows, grads):
    return lax.dot_general(rows, grads, (((0,), (0,)), ((), ())), preferred_element_type=F32)


def gelu_exact(pre_rows):
    return jax.nn.gelu(pre_rows, approximate=False)


def gelu_backward(pre_rows, grad_rows):
    unused, pullback = jax.vjp(gelu_exact, pre_rows)
    return pullback(grad_rows)[0]


def norm_forward(summed, gain_row, shift_row):
    row_mean = jnp.mean(summed, axis=-1, keepdims=True)
    centred = summed - row_mean
    variance = jnp.mean(centred * centred, axis=-1, keepdims=True)
    inverse = lax.rsqrt(variance + norm_epsilon)
    unit_rows = centred * inverse
    return unit_rows * gain_row + shift_row, unit_rows, inverse


def norm_backward(grad_out, unit_rows, inverse, gain_row):
    grad_unit = grad_out * gain_row
    first_mean = jnp.mean(grad_unit, axis=-1, keepdims=True)
    second_mean = jnp.mean(grad_unit * unit_rows, axis=-1, keepdims=True)
    return inverse * (grad_unit - first_mean - unit_rows * second_mean)


def layer(sizes, tokens, memory, cotangent, target_lengths, memory_lengths, self_inputs, self_output, cross_query, cross_memory, cross_output, feed_in, feed_out, proj_bias, feed_bias, branch_bias, norm_gain, norm_shift):
    zn, yn, gn, cn = sizes
    seq = lax.axis_index("g")
    core = lax.axis_index("c")
    width = self_output.shape[0]
    joined = width % 128 != 0

    def swap(rows):
        return lax.ppermute(rows, "c", [(0, 1), (1, 0)])

    def gather_rows(rows):
        if cn != 2:
            return lax.all_gather(rows, "c", axis=0, tiled=True)
        got = swap(rows)
        return jnp.where(core == 0, jnp.concatenate([rows, got]), jnp.concatenate([got, rows]))

    def sum_all(part):
        part = part.astype(LOW)
        if cn != 2:
            return lax.psum(part, "c").astype(F32)
        return part.astype(F32) + swap(part).astype(F32)

    def own_rows(rows):
        size = rows.shape[0] // cn
        return lax.dynamic_slice_in_dim(rows, core * size, size, 0)

    def sum_own(part):
        if cn != 2:
            return lax.psum_scatter(part.astype(LOW), "c", scatter_dimension=0, tiled=True).astype(F32)
        size = part.shape[0] // 2
        got = swap(lax.dynamic_slice_in_dim(part, (1 - core) * size, size, 0).astype(LOW))
        return lax.dynamic_slice_in_dim(part, core * size, size, 0) + got.astype(F32)

    def spread(shard, axis):
        every = [shard] + [lax.ppermute(shard, "g", [((i + k) % gn, i) for i in range(gn)]) for k in range(1, gn)]
        return [jnp.concatenate(every, axis=axis)] if joined else every

    def send_home(parts):
        total = parts[0]
        for k in range(1, gn):
            total = total + lax.ppermute(parts[k].astype(LOW), "g", [(i, (i + k) % gn) for i in range(gn)]).astype(F32)
        return total

    steps = [("y", 1, lax.axis_index("y"), yn)] if yn == 2 else []
    steps += [("z", 1 << b, lax.axis_index("z"), zn) for b in range((zn - 1).bit_length())]

    def pairwise(rows, axis, far, size):
        return lax.ppermute(rows, axis, [(i, i ^ far) for i in range(size)])

    def sum_groups(total):
        for axis, far, at, size in steps:
            half = total.shape[0] // 2
            bit = (at // far) % 2
            away = lax.dynamic_slice_in_dim(total, (1 - bit) * half, half, 0).astype(LOW)
            keep = lax.dynamic_slice_in_dim(total, bit * half, half, 0)
            total = keep + pairwise(away, axis, far, size).astype(F32)
        total = total.astype(LOW)
        for axis, far, at, size in reversed(steps):
            got = pairwise(total, axis, far, size)
            total = jnp.where((at // far) % 2 == 0, jnp.concatenate([total, got]), jnp.concatenate([got, total]))
        return total.astype(F32)

    def fetch_slices(shards):
        at = lax.axis_index("z") * yn + lax.axis_index("y")
        pieces = [lax.dynamic_slice_in_dim(shard, at * (shard.shape[0] // (zn * yn)), shard.shape[0] // (zn * yn), 0) for shard in shards]
        pieces = [jnp.stack(pieces)] if pieces[0].shape == pieces[1].shape else [piece[None] for piece in pieces]
        return [[lax.ppermute(piece, "g", [((i + k) % gn, i) for i in range(gn)]) for piece in pieces] for k in range(1, gn)]

    def spread_wide(shards, slices):
        every = [[shard] for shard in shards]
        for got in slices:
            whole = [rows for piece in got for rows in lax.all_gather(piece, ("z", "y"), axis=1, tiled=True)]
            for at, rows in enumerate(whole):
                every[at].append(rows)
        return [[jnp.concatenate(part, axis=1 - at)] if joined else part for at, part in enumerate(every)]

    def parts_of(values, axis):
        return jnp.split(values[0], gn, axis=axis) if joined else values

    target_length = lax.dynamic_slice_in_dim(target_lengths, seq, 1, 0)
    memory_length = lax.dynamic_slice_in_dim(memory_lengths, seq, 1, 0)

    def after(value, *needed):
        return lax.optimization_barrier((value,) + needed)[0]

    token_all = gather_rows(tokens)
    biases = spread(jnp.concatenate([proj_bias, feed_bias.reshape(-1, width)]), 1)
    feed_rows = feed_bias.shape[0] // width
    if joined:
        halves = jnp.split(biases[0], gn, axis=1)
        b_in = [jnp.concatenate([part[4:].reshape(-1) for part in halves])]
    else:
        b_in = [part[4:].reshape(-1) for part in biases]
    b_proj = [part[:4] for part in biases]
    slices = fetch_slices((feed_in, feed_out))
    w_self = spread(after(self_inputs, token_all, biases[-1], slices[-1][0]), 2)
    w_in, w_out = spread_wide((feed_in, feed_out), slices)
    self_q, self_k, self_v, self_mixed, self_lse = [], [], [], [], []
    shards = range(len(w_self))
    for s in shards:
        self_q.append((_nn(token_all, w_self[s][0]) + b_proj[s][0]).astype(LOW))
        self_k.append(_nn(token_all, w_self[s][1]).astype(LOW))
        self_v.append((_nn(token_all, w_self[s][2]) + b_proj[s][1]).astype(LOW))
        mixed, lse = attn_fwd(target_length, self_q[s], self_k[s], self_v[s], True)
        self_mixed.append(mixed)
        self_lse.append(lse)
    first = self_mixed[0]
    w_self_out = spread(after(self_output, first), 0)
    memory_all = gather_rows(after(memory, first))
    w_cross_mem = spread(after(cross_memory, first), 2)
    w_cross_q = spread(after(cross_query, first), 1)
    w_cross_out = spread(after(cross_output, first), 0)
    cot_all = gather_rows(after(cotangent, self_mixed[-1]))

    cross_k = [_nn(memory_all, w_cross_mem[s][0]).astype(LOW) for s in shards]
    cross_v = [(_nn(memory_all, w_cross_mem[s][1]) + b_proj[s][3]).astype(LOW) for s in shards]
    branch_one = sum_all(sum(_nn(self_mixed[s], w_self_out[s]) for s in shards)) + branch_bias[0]
    normed_one, unit_one, inverse_one = norm_forward(residual_scale * token_all.astype(F32) + branch_one, norm_gain[0], norm_shift[0])
    second = normed_one.astype(LOW)
    cross_q = [(_nn(second, w_cross_q[s]) + b_proj[s][2]).astype(LOW) for s in shards]
    cross_mixed, cross_lse = zip(*[attn_fwd(memory_length, cross_q[s], cross_k[s], cross_v[s], False) for s in shards])
    branch_two = sum_all(sum(_nn(cross_mixed[s], w_cross_out[s]) for s in shards)) + branch_bias[1]
    normed_two, unit_two, inverse_two = norm_forward(residual_scale * normed_one + branch_two, norm_gain[1], norm_shift[1])
    third = normed_two.astype(LOW)
    hidden_pre = [_nn(third, w_in[s]) + b_in[s].astype(F32) for s in shards]
    hidden = [gelu_exact(hidden_pre[s]).astype(LOW) for s in shards]
    branch_three = sum_all(sum(_nn(hidden[s], w_out[s]) for s in shards)) + branch_bias[2]
    normed_three, unit_three, inverse_three = norm_forward(residual_scale * normed_two + branch_three, norm_gain[2], norm_shift[2])
    block_out = own_rows(normed_three.astype(LOW))

    cot = cot_all.astype(F32)
    grad_three = norm_backward(cot, unit_three, inverse_three, norm_gain[2])
    low_three = grad_three.astype(LOW)
    grad_hidden = [_nt(low_three, w_out[s]) for s in shards]
    feed_out_parts = parts_of([tn(hidden[s], low_three) for s in shards], 0)
    grad_pre = [gelu_backward(hidden_pre[s], grad_hidden[s]).astype(LOW) for s in shards]
    feed_in_parts = parts_of([tn(third, grad_pre[s]) for s in shards], 1)
    feed_out_sum, feed_in_sum = [lax.psum(send_home(part).astype(LOW), ("z", "y")).astype(F32) for part in (feed_out_parts, feed_in_parts)]
    grad_normed_two = residual_scale * grad_three + sum_all(sum(_nt(grad_pre[s], w_in[s]) for s in shards))
    grad_two = norm_backward(grad_normed_two, unit_two, inverse_two, norm_gain[1])
    low_two = grad_two.astype(LOW)
    grad_cross_mixed = [_nt(low_two, w_cross_out[s]).astype(LOW) for s in shards]
    cross_out_parts = parts_of([tn(cross_mixed[s], low_two) for s in shards], 0)
    cross_dq, cross_dk, cross_dv = zip(*[attn_bwd(memory_length, cross_q[s], cross_k[s], cross_v[s], cross_mixed[s], grad_cross_mixed[s], cross_lse[s], False) for s in shards])
    grad_normed_one = residual_scale * grad_two + sum_all(sum(_nt(cross_dq[s], w_cross_q[s]) for s in shards))
    cross_parts = [parts_of([tn(second, cross_dq[s]) for s in shards], 1), parts_of([tn(memory_all, cross_dk[s]) for s in shards], 1), parts_of([tn(memory_all, cross_dv[s]) for s in shards], 1)]
    grad_memory = sum_own(sum(_nt(cross_dk[s], w_cross_mem[s][0]) + _nt(cross_dv[s], w_cross_mem[s][1]) for s in shards)).astype(LOW)
    grad_one = norm_backward(grad_normed_one, unit_one, inverse_one, norm_gain[0])
    low_one = grad_one.astype(LOW)

    def sums(rows):
        return jnp.sum(rows.astype(F32), axis=0)

    model = tokens.shape[1]
    terms = jnp.stack([sums(low_one), sums(low_two), sums(low_three), sums(grad_normed_one * unit_one), sums(grad_normed_two * unit_two), sums(cot * unit_three), sums(grad_normed_one), sums(grad_normed_two), sums(cot)])
    feed_sums = parts_of([sums(grad_pre[s]) for s in shards], 0)
    groups = [[cross_out_parts], cross_parts[:1], cross_parts[1:]]
    in_kernel = (zn, yn, gn, cn, width, joined) == (4, 2, 2, 2, SPAN, False)
    if not in_kernel:
        grad_self_mixed = [_nt(low_one, w_self_out[s]).astype(LOW) for s in shards]
        self_out_parts = parts_of([tn(self_mixed[s], low_one) for s in shards], 0)
        self_dq, self_dk, self_dv = zip(*[attn_bwd(target_length, self_q[s], self_k[s], self_v[s], self_mixed[s], grad_self_mixed[s], self_lse[s], True) for s in shards])
        token_part = sum_own(sum(_nt(self_dq[s], w_self[s][0]) + _nt(self_dk[s], w_self[s][1]) + _nt(self_dv[s], w_self[s][2]) for s in shards))
        self_sums = parts_of([jnp.stack([sums(self_dq[s]), sums(self_dv[s])]) for s in shards], 1)
    else:
        self_sums = [jnp.zeros((2, width), F32)] * gn
    cross_sums = parts_of([jnp.stack([sums(cross_dq[s]), sums(cross_dv[s])]) for s in shards], 1)
    smalls = []
    for k in range(gn):
        small = lax.dynamic_slice_in_dim(terms, ((seq + k) % gn * cn + core) * width, width, 1)
        small = jnp.concatenate([small, self_sums[k], cross_sums[k], feed_sums[k].reshape(-1, width)])
        smalls.append(jnp.pad(small, ((0, 16 * zn * yn - small.shape[0]), (0, 0))))
    if in_kernel:
        pairs = [(part[0].astype(LOW), part[1].astype(LOW)) for group in groups for part in group]
        per_shard = [(self_q[s], self_k[s], self_v[s], self_mixed[s], self_lse[s]) for s in shards]
        token_part, *sums_low = self_back(target_length, low_one, per_shard[0], per_shard[1], w_self_out, token_all.T, w_self, smalls, pairs, None, None)
        sums_low = [rows.astype(F32) for rows in sums_low]
        cross_out_sum, cross_q_sum, cross_k_sum, cross_v_sum, self_out_sum, self_in_sum, small = sums_low
        cross_mem_sum = jnp.stack([cross_k_sum, cross_v_sum])
    else:
        groups += [[self_out_parts], [parts_of([tn(token_all, grads[s]) for s in shards], 1) for grads in (self_dq, self_dk, self_dv)], [smalls]]
        sums_low = [sum_groups(send_home([jnp.concatenate([part[k] for part in group]) for k in range(gn)])) for group in groups]
        cross_out_sum, cross_q_sum, cross_mem_sum, self_out_sum, self_in_sum, small = [rows.astype(F32) for rows in sums_low]
    grad_tokens = (residual_scale * own_rows(grad_one) + token_part).astype(LOW)
    return (block_out, grad_tokens, grad_memory, self_in_sum.reshape(3, model, width), self_out_sum, cross_q_sum, cross_mem_sum.reshape(2, model, width), cross_out_sum, feed_in_sum, feed_out_sum, small[9:13], small[13:13 + feed_rows].reshape(-1), small[0:3], small[3:6], small[6:9])


def solution(mesh):
    dp, mp = mesh.shape["dp"], mesh.shape["mp"]

    def whole(*args):
        yn = 2 if dp % 2 == 0 else 1
        gn = args[3].shape[0] // dp
        sizes = (dp // yn, yn, gn, mp // gn)
        fine = Mesh(mesh.devices.reshape(sizes), ("z", "y", "g", "c"))
        d, m = ("z", "y"), ("g", "c")
        rows, wide, tall = P(d + m, None), P(None, m), P(m, None)
        stack = P(None, None, m)
        in_specs = (rows, rows, rows, P(d), P(d), stack, tall, wide, stack, tall, wide, tall, wide, P(m), P(), P(), P())
        out_specs = (rows, rows, rows, stack, tall, wide, stack, tall, wide, tall, wide, P(m), wide, wide, wide)
        return jax.shard_map(functools.partial(layer, sizes), mesh=fine, in_specs=in_specs, out_specs=out_specs, check_vma=False)(*args)

    return whole
```

```python
import functools

import jax, jax.numpy as jnp
from jax import lax
from jax.experimental import pallas as pl
from jax.experimental.pallas import tpu as pltpu
from jax.sharding import Mesh
from jax.sharding import PartitionSpec as P

HEAD = 64
NEG = -1e30

def _nt(a, b):
    return lax.dot_general(a, b, (((1,), (1,)), ((), ())), preferred_element_type=jnp.float32)

def _nn(a, b):
    return lax.dot_general(a, b, (((1,), (0,)), ((), ())), preferred_element_type=jnp.float32)

def _lanes(rows):
    return lax.broadcasted_iota(jnp.int32, (rows, 128), 1)

def _put(base, lane, pairs):
    for at, val in pairs:
        base = jnp.where(lane == at, val, base)
    return base

def fwd_kernel(len_ref, q_ref, k_ref, v_ref, o_ref, lse_ref, *, causal, bq):
    p = pl.program_id(0)
    rows, keys = q_ref.shape[0], k_ref.shape[0]
    length = len_ref[0]
    kl = _lanes(keys)
    kpos = lax.broadcasted_iota(jnp.int32, (keys, 128), 0)
    kbias = jnp.where(kpos < length, 0.0, NEG)
    k2 = k_ref[...].astype(jnp.float32)
    v2 = v_ref[...].astype(jnp.float32)
    ql = _lanes(bq)
    heads = []
    for h in range(2):
        mine = (kl // HEAD) == h
        other = HEAD * (1 - h)
        kh = jnp.where(mine, k2, jnp.where(kl == other, kbias, 0.0)).astype(jnp.bfloat16)
        vh = jnp.where(mine, v2, jnp.where(kl == other, 1.0, 0.0)).astype(jnp.bfloat16)
        heads.append((kh, vh))
    for i in range(rows // bq):
        q2 = q_ref[pl.ds(i * bq, bq), :].astype(jnp.float32) * (HEAD ** -0.5)
        out = jnp.zeros((bq, 128), jnp.float32)
        lse_all = lse_ref[pl.ds(i * bq, bq), :]
        for h in range(2):
            kh, vh = heads[h]
            mine = (ql // HEAD) == h
            other = HEAD * (1 - h)
            qh = jnp.where(mine, q2, jnp.where(ql == other, 1.0, 0.0)).astype(jnp.bfloat16)
            if causal:
                lo = i * bq
                sd = _nt(qh, kh[lo:lo + bq])
                r = lax.broadcasted_iota(jnp.int32, (bq, bq), 0)
                c = lax.broadcasted_iota(jnp.int32, (bq, bq), 1)
                sd = jnp.where(c <= r, sd, NEG)
                m = jnp.max(sd, axis=1, keepdims=True)
                if lo:
                    sl = _nt(qh, kh[:lo])
                    m = jnp.maximum(m, jnp.max(sl, axis=1, keepdims=True))
                    acc = _nn(jnp.exp(sl - m).astype(jnp.bfloat16), vh[:lo])
                    acc += _nn(jnp.exp(sd - m).astype(jnp.bfloat16), vh[lo:lo + bq])
                else:
                    acc = _nn(jnp.exp(sd - m).astype(jnp.bfloat16), vh[:bq])
            else:
                s = _nt(qh, kh)
                m = jnp.max(s, axis=1, keepdims=True)
                acc = _nn(jnp.exp(s - m).astype(jnp.bfloat16), vh)
            total = jnp.sum(jnp.where(ql == other, acc, 0.0), axis=1, keepdims=True)
            out = jnp.where(mine, acc / total, out)
            lse_all = jnp.where(ql == 2 * p + h, m + jnp.log(total), lse_all)
        o_ref[pl.ds(i * bq, bq), :] = out.astype(jnp.bfloat16)
        lse_ref[pl.ds(i * bq, bq), :] = lse_all

def attn_fwd(length, q, k, v, causal, bq=256):
    rows, cols = q.shape
    keys = k.shape[0]
    pairs = cols // 128
    el = pairs * 2 * rows * keys
    return pl.pallas_call(
        functools.partial(fwd_kernel, causal=causal, bq=bq),
        out_shape=(jax.ShapeDtypeStruct((rows, cols), jnp.bfloat16), jax.ShapeDtypeStruct((rows, 128), jnp.float32)),
        grid_spec=pltpu.PrefetchScalarGridSpec(
            num_scalar_prefetch=1, grid=(pairs,),
            in_specs=[pl.BlockSpec((rows, 128), lambda p, n: (0, p)), pl.BlockSpec((keys, 128), lambda p, n: (0, p)), pl.BlockSpec((keys, 128), lambda p, n: (0, p))],
            out_specs=[pl.BlockSpec((rows, 128), lambda p, n: (0, p)), pl.BlockSpec((rows, 128), lambda p, n: (0, 0))],
        ),
        compiler_params=pltpu.CompilerParams(dimension_semantics=("arbitrary",), vmem_limit_bytes=40 << 20),
        cost_estimate=pl.CostEstimate(flops=16 * el * 64, bytes_accessed=8 * rows * cols, transcendentals=el),
        name="attend_forward",
    )(length, q, k, v)

def split3(x):
    a = x.astype(jnp.bfloat16).astype(jnp.float32)
    b = (x - a).astype(jnp.bfloat16).astype(jnp.float32)
    return a, b, x - a - b


def key_side(k2, v2, length):
    keys = k2.shape[0]
    kl = _lanes(keys)
    kbias = jnp.where(lax.broadcasted_iota(jnp.int32, (keys, 128), 0) < length, 0.0, NEG)
    k2, v2 = k2.astype(jnp.float32), v2.astype(jnp.float32)
    heads = []
    for h in range(2):
        mine = (kl // HEAD) == h
        other = HEAD * (1 - h)
        ones = (kl > other) & (kl < other + 4)
        kh = jnp.where(mine, k2, jnp.where(kl == other, kbias, jnp.where(ones, 1.0, 0.0))).astype(jnp.bfloat16)
        vh = jnp.where(mine, v2, jnp.where(ones, 1.0, 0.0)).astype(jnp.bfloat16)
        heads.append((kh, vh, kh.T))
    return heads


def query_block(heads, q2, o2, g2, lse_all, pair, i, last, causal, dka, dva):
    bq = q2.shape[0]
    keys = heads[0][0].shape[0]
    ql = _lanes(bq)
    q2 = q2.astype(jnp.float32) * (HEAD ** -0.5)
    g2 = g2.astype(jnp.float32)
    go = g2 * o2.astype(jnp.float32)
    dqt = []
    for h in range(2):
        kh, vh, kt = heads[h]
        mine = (ql // HEAD) == h
        other = HEAD * (1 - h)
        lse = jnp.sum(jnp.where(ql == 2 * pair + h, lse_all, 0.0), axis=1, keepdims=True)
        delta = jnp.sum(jnp.where(mine, go, 0.0), axis=1, keepdims=True)
        la, lb, lc = split3(-lse)
        da, db, dc = split3(-delta)
        qh = _put(jnp.where(mine, q2, 0.0), ql, ((other, 1.0), (other + 1, la), (other + 2, lb), (other + 3, lc))).astype(jnp.bfloat16)
        gh = _put(jnp.where(mine, g2, 0.0), ql, ((other + 1, da), (other + 2, db), (other + 3, dc))).astype(jnp.bfloat16)
        hi = (i + 1) * bq if causal else keys
        st = _nt(kh[:hi], qh)
        if causal:
            kr = lax.broadcasted_iota(jnp.int32, (hi, bq), 0)
            qc = lax.broadcasted_iota(jnp.int32, (hi, bq), 1) + i * bq
            pt = jnp.where(kr <= qc, jnp.exp(st), 0.0)
        else:
            pt = jnp.exp(st)
        dst = (pt * _nt(vh[:hi], gh)).astype(jnp.bfloat16)
        dvn = _nn(pt.astype(jnp.bfloat16), gh)
        dkn = _nn(dst, qh)
        if last:
            dva[h, :hi] = dvn
            dka[h, :hi] = dkn
        else:
            dva[h, :hi] += dvn
            dka[h, :hi] += dkn
        dqt.append(_nn(kt[:, :hi], dst))
    dq = jnp.concatenate([dqt[0][:HEAD], dqt[1][HEAD:]], axis=0).T
    return (dq * (HEAD ** -0.5)).astype(jnp.bfloat16)


def bwd_kernel(len_ref, q_ref, k_ref, v_ref, o_ref, g_ref, lse_ref, dq_ref, dk_ref, dv_ref, dka, dva, *, causal, bq):
    rows, keys = q_ref.shape[0], k_ref.shape[0]
    heads = key_side(k_ref[...], v_ref[...], len_ref[0])
    blocks = rows // bq
    for i in reversed(range(blocks)):
        at = pl.ds(i * bq, bq)
        dq_ref[at, :] = query_block(heads, q_ref[at, :], o_ref[at, :], g_ref[at, :], lse_ref[at, :], pl.program_id(0), i, i == blocks - 1, causal, dka, dva)
    first = _lanes(keys) < HEAD
    dk_ref[...] = jnp.where(first, dka[0], dka[1]).astype(jnp.bfloat16)
    dv_ref[...] = jnp.where(first, dva[0], dva[1]).astype(jnp.bfloat16)

def attn_bwd(length, q, k, v, o, g, lse, causal, bq=256):
    rows, cols = q.shape
    keys = k.shape[0]
    pairs = cols // 128
    el = pairs * 2 * rows * keys
    qs = pl.BlockSpec((rows, 128), lambda p, n: (0, p))
    ks = pl.BlockSpec((keys, 128), lambda p, n: (0, p))
    return pl.pallas_call(
        functools.partial(bwd_kernel, causal=causal, bq=bq),
        out_shape=(jax.ShapeDtypeStruct((rows, cols), jnp.bfloat16), jax.ShapeDtypeStruct((keys, cols), jnp.bfloat16), jax.ShapeDtypeStruct((keys, cols), jnp.bfloat16)),
        grid_spec=pltpu.PrefetchScalarGridSpec(
            num_scalar_prefetch=1, grid=(pairs,),
            in_specs=[qs, ks, ks, qs, qs, pl.BlockSpec((rows, 128), lambda p, n: (0, 0))],
            out_specs=[qs, ks, ks],
            scratch_shapes=[pltpu.VMEM((2, keys, 128), jnp.float32), pltpu.VMEM((2, keys, 128), jnp.float32)],
        ),
        compiler_params=pltpu.CompilerParams(dimension_semantics=("arbitrary",), vmem_limit_bytes=48 << 20),
        cost_estimate=pl.CostEstimate(flops=40 * el * 64, bytes_accessed=16 * rows * cols, transcendentals=el),
        name="attend_backward",
    )(length, q, k, v, o, g, lse)

CHUNK = 512
LAG = 1
SPAN = 256


class Pipeline:
    AHEAD = 3

    def __init__(self, total, scratch):
        self.spots, self.total, self.step, self.sent, self.loaded = [], total, 0, 0, 0
        (self.held, self.ysum, self.zgot, self.mine, self.load, self.store, self.xs, self.xr, self.ys, self.yr, self.zs, self.zr, self.bs, self.br, self.es, self.er) = scratch
        self.full = self.held
        self.seq, self.ya, za = lax.axis_index("g"), lax.axis_index("y"), lax.axis_index("z")
        self.za = za
        self.peers = {1: za + 1 - 2 * (za % 2), 2: (za + 2) % 4, 3: 3 - za}
        self.stages = (self.to_y, self.to_z, self.back_z, self.back_y, self.finish)

    @staticmethod
    def scratch(total, most):
        dma = pltpu.SemaphoreType.DMA
        return [
            pltpu.VMEM((total, most, SPAN), LOW),
            pltpu.VMEM((total, most // 2, SPAN), LOW),
            pltpu.VMEM((total, 3, most // 8, SPAN), LOW),
            pltpu.VMEM((4, most, SPAN), LOW),
            dma((4,)), dma((total,)),
            dma((total,)), dma((total,)), dma((total,)), dma((total,)),
            dma((total, 3)), dma((total, 3)), dma((total, 3)), dma((total, 3)),
            dma((total,)), dma((total,)),
        ]

    def greet(self, more=()):
        barrier = pltpu.get_barrier_semaphore()
        everyone = [{"g": 1 - self.seq}, {"y": 1 - self.ya}] + [{"z": self.peers[d]} for d in (1, 2, 3)] + list(more)
        for where in everyone:
            pl.semaphore_signal(barrier, inc=1, device_id=where, device_id_type=pl.DeviceIdType.MESH)
        pl.semaphore_wait(barrier, len(everyone))

    def add(self, own, other, out, out_row):
        rows, cols = own.shape
        size = min(CHUNK, rows)
        for r in range(0, rows, size):
            for c in range(0, cols, SPAN):
                self.spots.append((own, other, r, c, size, out, out_row + r))
        self.feed()

    def feed(self):
        while self.sent < min(len(self.spots), self.step + self.AHEAD):
            self.x_copy(self.sent).start()
            self.own_copy(self.sent).start()
            self.sent += 1

    def tick(self, times=1):
        for unused in range(times):
            if self.step >= self.total + LAG * (len(self.stages) - 1):
                return
            for at, stage in enumerate(self.stages):
                if 0 <= self.step - LAG * at < self.total:
                    stage(self.step - LAG * at)
            self.step += 1
            self.feed()

    def drain(self):
        assert len(self.spots) == self.total
        self.tick(self.total + LAG * len(self.stages))
        for k in range(self.total):
            self.x_copy(k).wait_send()
            self.yb_copy(k).wait_send()
            self.out_copy(k).wait()
            for d in (1, 2, 3):
                self.z_copy(k, d).wait_send()
                self.zb_copy(k, d).wait_send()

    @staticmethod
    def remote(src, dst, send, recv, where):
        return pltpu.make_async_remote_copy(src_ref=src, dst_ref=dst, send_sem=send, recv_sem=recv, device_id=where, device_id_type=pl.DeviceIdType.MESH)

    @staticmethod
    def block(at, size):
        return pl.ds(pl.multiple_of(at * size, size), size)

    def x_copy(self, k):
        own, other, r, c, n, o, q = self.spots[k]
        return self.remote(other.at[pl.ds(r, n), pl.ds(c, SPAN)], self.held.at[k, pl.ds(0, n)], self.xs.at[k], self.xr.at[k], {"g": 1 - self.seq})

    def own_copy(self, k):
        own, other, r, c, n, o, q = self.spots[k]
        return pltpu.make_async_copy(own.at[pl.ds(r, n), pl.ds(c, SPAN)], self.mine.at[k % 4, pl.ds(0, n)], self.load.at[k % 4])

    def y_copy(self, k):
        h = self.spots[k][4] // 2
        return self.remote(self.held.at[k, self.block(1 - self.ya, h)], self.ysum.at[k, pl.ds(0, h)], self.ys.at[k], self.yr.at[k], {"y": 1 - self.ya})

    def z_copy(self, k, d):
        p = self.spots[k][4] // 8
        return self.remote(self.ysum.at[k, self.block(self.peers[d], p)], self.zgot.at[k, d - 1, pl.ds(0, p)], self.zs.at[k, d - 1], self.zr.at[k, d - 1], {"z": self.peers[d]})

    def zb_copy(self, k, d):
        rows = self.full.at[k, self.block(self.ya * 4 + self.za, self.spots[k][4] // 8)]
        return self.remote(rows, rows, self.bs.at[k, d - 1], self.br.at[k, d - 1], {"z": self.peers[d]})

    def yb_copy(self, k):
        rows = self.full.at[k, self.block(self.ya, self.spots[k][4] // 2)]
        return self.remote(rows, rows, self.es.at[k], self.er.at[k], {"y": 1 - self.ya})

    def out_copy(self, k):
        own, other, r, c, n, o, q = self.spots[k]
        return pltpu.make_async_copy(self.full.at[k, pl.ds(0, n)], o.at[pl.ds(q, n), pl.ds(c, SPAN)], self.store.at[k])

    def to_y(self, k):
        n = self.spots[k][4]
        self.own_copy(k).wait()
        self.x_copy(k).wait_recv()
        self.held[k, :n] = self.held[k, :n] + self.mine[k % 4, :n]
        self.y_copy(k).start()

    def to_z(self, k):
        h = self.spots[k][4] // 2
        self.y_copy(k).wait()
        self.ysum[k, :h] = self.ysum[k, :h] + self.held[k, self.block(self.ya, h)]
        for d in (1, 2, 3):
            self.z_copy(k, d).start()

    def back_z(self, k):
        p = self.spots[k][4] // 8
        for d in (1, 2, 3):
            self.z_copy(k, d).wait_recv()
        rows = self.ysum[k, self.block(self.za, p)].astype(F32)
        for d in (1, 2, 3):
            rows = rows + self.zgot[k, d - 1, :p].astype(F32)
        self.full[k, self.block(self.ya * 4 + self.za, p)] = rows.astype(LOW)
        for d in (1, 2, 3):
            self.zb_copy(k, d).start()

    def back_y(self, k):
        for d in (1, 2, 3):
            self.zb_copy(k, d).wait_recv()
        self.yb_copy(k).start()

    def finish(self, k):
        self.yb_copy(k).wait_recv()
        self.out_copy(k).start()


def spot_count(shapes):
    return sum((rows // min(CHUNK, rows)) * (cols // SPAN) for rows, cols in shapes)


def attend_back(pipe, shards, length, low, gm, dq, dk, dv, dka, dva, causal, bq):
    rows = low.shape[0]
    blocks = rows // bq
    for s, (q, k, v, o, l, wo) in enumerate(shards):
        for i in range(blocks):
            at = pl.ds(i * bq, bq)
            gm[s, at, :] = _nt(low[at, :], wo[...]).astype(LOW)
    for s, (q, k, v, o, l, wo) in enumerate(shards):
        for p in range(q.shape[1] // 128):
            cols = pl.ds(p * 128, 128)
            heads = key_side(k[:, cols], v[:, cols], length)
            for i in reversed(range(blocks)):
                at = pl.ds(i * bq, bq)
                dq[s, at, cols] = query_block(heads, q[at, cols], o[at, cols], gm[s, at, cols], l[at, :], p, i, i == blocks - 1, causal, dka, dva)
            first = _lanes(k.shape[0]) < HEAD
            dk[s, :, cols] = jnp.where(first, dka[0], dka[1]).astype(LOW)
            dv[s, :, cols] = jnp.where(first, dva[0], dva[1]).astype(LOW)
            pipe.tick()


def back_rows(terms, start, size):
    at = pl.ds(pl.multiple_of(start, size), size)
    both = None
    for grads, s, weight in terms:
        term = _nt(grads[s, at, :], weight)
        both = term if both is None else both + term
    return both


def output_grads(shards, low, outs):
    for (q, k, v, o, l, wo), out in zip(shards, outs):
        for c in range(0, low.shape[1], SPAN):
            out[:, c : c + SPAN] = tn(o[...], low[:, c : c + SPAN]).astype(LOW)


def input_grads(rows_t, grads, out, first, bq):
    for i in range(0, rows_t.shape[0], bq):
        out[pl.ds(first + i, bq), :] = _nn(rows_t[pl.ds(i, bq), :], grads).astype(LOW)


def share_rows(terms, core, part, got, sems, out, bq, pipe):
    half = out.shape[0]
    copy = Pipeline.remote(part, got, sems[0], sems[1], {"c": 1 - core})
    for i in range(0, half, bq):
        part[pl.ds(i, bq), :] = back_rows(terms, (1 - core) * half + i, bq).astype(LOW)
    copy.start()
    pipe.tick()
    for i in range(0, half, bq):
        out[pl.ds(i, bq), :] = back_rows(terms, core * half + i, bq)
    pipe.tick()
    copy.wait()
    for i in range(0, half, bq):
        out[pl.ds(i, bq), :] += got[pl.ds(i, bq), :].astype(F32)


def self_back_kernel(carried, bq, len_ref, low, q0, k0, v0, o0, l0, q1, k1, v1, o1, l1, wo0, wo1, xt, w0, w1, small0, small1, *rest):
    own, other, rest = rest[:carried], rest[carried : 2 * carried], rest[2 * carried :]
    token_out, rest = rest[0], rest[1:]
    outs, rest = rest[: carried + 3], rest[carried + 3 :]
    gm, dq, dk, dv, dka, dva, go_own, go_other, gi_own, gi_other, sm_own, sm_other, part, got, part_send, part_recv = rest[:16]
    core = lax.axis_index("c")
    total = spot_count([ref.shape for ref in own] + [go_own.shape, gi_own.shape, sm_own.shape])
    pipe = Pipeline(total, rest[16:])
    pipe.greet([{"c": 1 - core}])
    for a, b, out in zip(own, other, outs):
        pipe.add(a, b, out, 0)
    shards = ((q0, k0, v0, o0, l0, wo0), (q1, k1, v1, o1, l1, wo1))
    output_grads(shards, low, (go_own, go_other))
    pipe.add(go_own, go_other, outs[carried], 0)
    attend_back(pipe, shards, len_ref[0], low, gm, dq, dk, dv, dka, dva, True, bq)
    for s, (gi, sm, small) in enumerate(((gi_own, sm_own, small0), (gi_other, sm_other, small1))):
        for m, grads in enumerate((dq, dk, dv)):
            input_grads(xt, grads[s], gi, m * xt.shape[0], bq)
        row = lax.broadcasted_iota(jnp.int32, sm.shape, 0)
        sums = [jnp.sum(grads[s].astype(F32), axis=0, keepdims=True) for grads in (dq, dv)]
        sm[...] = jnp.where(row == 9, sums[0], jnp.where(row == 10, sums[1], small[...])).astype(LOW)
    pipe.add(gi_own, gi_other, outs[carried + 1], 0)
    pipe.add(sm_own, sm_other, outs[carried + 2], 0)
    terms = [(grads, s, w[m]) for s, w in ((0, w0), (1, w1)) for m, grads in enumerate((dq, dk, dv))]
    share_rows(terms, core, part, got, (part_send, part_recv), token_out, bq, pipe)
    pipe.drain()


def cross_back_kernel(carried, bq, len_ref, low, q0, k0, v0, o0, l0, q1, k1, v1, o1, l1, wo0, wo1, xt, mt, wq0, wq1, wm0, wm1, *rest):
    own, other, rest = rest[:carried], rest[carried : 2 * carried], rest[2 * carried :]
    row_out, memory_out, sums_out, go_own, go_other, gq_own, gq_other, gm_own, gm_other = rest[:9]
    outs, rest = rest[9 : 9 + carried], rest[9 + carried :]
    gm, dq, dk, dv, dka, dva, part, got, part_send, part_recv, full_part, full_got, full_send, full_recv = rest[:14]
    core = lax.axis_index("c")
    pipe = Pipeline(spot_count([ref.shape for ref in own]), rest[14:])
    pipe.greet([{"c": 1 - core}])
    for a, b, out in zip(own, other, outs):
        pipe.add(a, b, out, 0)
    shards = ((q0, k0, v0, o0, l0, wo0), (q1, k1, v1, o1, l1, wo1))
    attend_back(pipe, shards, len_ref[0], low, gm, dq, dk, dv, dka, dva, False, bq)
    rows = low.shape[0]
    terms = [(dq, 0, wq0[...]), (dq, 1, wq1[...])]
    for i in range(0, rows, bq):
        full_part[pl.ds(i, bq), :] = back_rows(terms, i, bq).astype(LOW)
    exchange = Pipeline.remote(full_part, full_got, full_send, full_recv, {"c": 1 - core})
    exchange.start()
    pipe.tick()
    terms = [(grads, s, w[m]) for s, w in ((0, wm0), (1, wm1)) for m, grads in enumerate((dk, dv))]
    share_rows(terms, core, part, got, (part_send, part_recv), memory_out, bq, pipe)
    output_grads(shards, low, (go_own, go_other))
    pipe.tick()
    for s, (gq, gkv) in enumerate(((gq_own, gm_own), (gq_other, gm_other))):
        input_grads(xt, dq[s], gq, 0, bq)
        input_grads(mt, dk[s], gkv, 0, bq)
        input_grads(mt, dv[s], gkv, mt.shape[0], bq)
        sums_out[s, 0:1] = jnp.sum(dq[s].astype(F32), axis=0, keepdims=True)
        sums_out[s, 1:2] = jnp.sum(dv[s].astype(F32), axis=0, keepdims=True)
        pipe.tick()
    exchange.wait()
    for i in range(0, rows, bq):
        at = pl.ds(i, bq)
        row_out[at, :] = full_part[at, :].astype(F32) + full_got[at, :].astype(F32)
    pipe.drain()


def low_ram(*shape):
    return pltpu.VMEM(shape, LOW)


def back_scratch(rows, width):
    return [low_ram(2, rows, width) for unused in range(4)] + [pltpu.VMEM((2, rows, 128), F32), pltpu.VMEM((2, rows, 128), F32)]


def self_back(length, low, first, second, wo, xt, w, smalls, pairs, bq=256):
    rows, model = low.shape
    width = wo[0].shape[0]
    carried = len(pairs)
    any_space = pl.BlockSpec(memory_space=pl.ANY)
    vmem = pl.BlockSpec(memory_space=pltpu.VMEM)
    dma = pltpu.SemaphoreType.DMA
    ends = [(width, model), (3 * rows, width), smalls[0].shape]
    total = spot_count([own.shape for own, unused in pairs] + ends)
    return pl.pallas_call(
        functools.partial(self_back_kernel, carried, bq),
        out_shape=[jax.ShapeDtypeStruct((rows // 2, model), F32)] + [jax.ShapeDtypeStruct(own.shape, LOW) for own, unused in pairs] + [jax.ShapeDtypeStruct(shape, LOW) for shape in ends],
        in_specs=[pl.BlockSpec(memory_space=pltpu.SMEM)] + [vmem] * 18 + [any_space] * (2 * carried),
        out_specs=[vmem] + [any_space] * (carried + 3),
        scratch_shapes=back_scratch(rows, width)
        + [low_ram(width, model), low_ram(width, model), low_ram(3 * rows, width), low_ram(3 * rows, width), low_ram(*smalls[0].shape), low_ram(*smalls[0].shape)]
        + [low_ram(rows // 2, model), low_ram(rows // 2, model), dma, dma]
        + Pipeline.scratch(total, CHUNK),
        compiler_params=pltpu.CompilerParams(collective_id=0, has_side_effects=True, vmem_limit_bytes=58 << 20),
        cost_estimate=pl.CostEstimate(flops=20 * rows * model * width, bytes_accessed=300 << 20, transcendentals=8 * rows * rows),
        name="self_backward",
    )(length, low, *first, *second, *wo, xt, *w, *smalls, *[p[0] for p in pairs], *[p[1] for p in pairs])


def cross_back(length, low, first, second, wo, xt, mt, wq, wm, pairs, bq=256):
    rows, model = low.shape
    width = wo[0].shape[0]
    carried = len(pairs)
    any_space = pl.BlockSpec(memory_space=pl.ANY)
    vmem = pl.BlockSpec(memory_space=pltpu.VMEM)
    dma = pltpu.SemaphoreType.DMA
    total = spot_count([own.shape for own, unused in pairs])
    shape = jax.ShapeDtypeStruct
    return pl.pallas_call(
        functools.partial(cross_back_kernel, carried, bq),
        out_shape=[shape((rows, model), F32), shape((rows // 2, model), F32), shape((2, 8, width), F32)]
        + [shape((width, model), LOW)] * 2 + [shape((rows, width), LOW)] * 2 + [shape((2 * rows, width), LOW)] * 2
        + [shape(own.shape, LOW) for own, unused in pairs],
        in_specs=[pl.BlockSpec(memory_space=pltpu.SMEM)] + [vmem] * 19 + [any_space] * (2 * carried),
        out_specs=[vmem] * 9 + [any_space] * carried,
        scratch_shapes=back_scratch(rows, width)
        + [low_ram(rows // 2, model), low_ram(rows // 2, model), dma, dma]
        + [low_ram(rows, model), low_ram(rows, model), dma, dma]
        + Pipeline.scratch(total, CHUNK),
        compiler_params=pltpu.CompilerParams(collective_id=1, has_side_effects=True, vmem_limit_bytes=58 << 20),
        cost_estimate=pl.CostEstimate(flops=20 * rows * model * width, bytes_accessed=300 << 20, transcendentals=8 * rows * rows),
        name="cross_backward",
    )(length, low, *first, *second, *wo, xt, mt, *wq, *wm, *[p[0] for p in pairs], *[p[1] for p in pairs])


residual_scale = 300.0**0.25
norm_epsilon = 1e-05
LOW = jnp.bfloat16
F32 = jnp.float32


def tn(rows, grads):
    return lax.dot_general(rows, grads, (((0,), (0,)), ((), ())), preferred_element_type=F32)


def gelu_exact(pre_rows):
    return jax.nn.gelu(pre_rows, approximate=False)


def gelu_backward(pre_rows, grad_rows):
    unused, pullback = jax.vjp(gelu_exact, pre_rows)
    return pullback(grad_rows)[0]


def norm_forward(summed, gain_row, shift_row):
    row_mean = jnp.mean(summed, axis=-1, keepdims=True)
    centred = summed - row_mean
    variance = jnp.mean(centred * centred, axis=-1, keepdims=True)
    inverse = lax.rsqrt(variance + norm_epsilon)
    unit_rows = centred * inverse
    return unit_rows * gain_row + shift_row, unit_rows, inverse


def norm_backward(grad_out, unit_rows, inverse, gain_row):
    grad_unit = grad_out * gain_row
    first_mean = jnp.mean(grad_unit, axis=-1, keepdims=True)
    second_mean = jnp.mean(grad_unit * unit_rows, axis=-1, keepdims=True)
    return inverse * (grad_unit - first_mean - unit_rows * second_mean)


def layer(sizes, tokens, memory, cotangent, target_lengths, memory_lengths, self_inputs, self_output, cross_query, cross_memory, cross_output, feed_in, feed_out, proj_bias, feed_bias, branch_bias, norm_gain, norm_shift):
    zn, yn, gn, cn = sizes
    seq = lax.axis_index("g")
    core = lax.axis_index("c")
    width = self_output.shape[0]
    joined = width % 128 != 0

    def swap(rows):
        return lax.ppermute(rows, "c", [(0, 1), (1, 0)])

    def gather_rows(rows):
        if cn != 2:
            return lax.all_gather(rows, "c", axis=0, tiled=True)
        got = swap(rows)
        return jnp.where(core == 0, jnp.concatenate([rows, got]), jnp.concatenate([got, rows]))

    def sum_all(part):
        part = part.astype(LOW)
        if cn != 2:
            return lax.psum(part, "c").astype(F32)
        return part.astype(F32) + swap(part).astype(F32)

    def own_rows(rows):
        size = rows.shape[0] // cn
        return lax.dynamic_slice_in_dim(rows, core * size, size, 0)

    def sum_own(part):
        if cn != 2:
            return lax.psum_scatter(part.astype(LOW), "c", scatter_dimension=0, tiled=True).astype(F32)
        size = part.shape[0] // 2
        got = swap(lax.dynamic_slice_in_dim(part, (1 - core) * size, size, 0).astype(LOW))
        return lax.dynamic_slice_in_dim(part, core * size, size, 0) + got.astype(F32)

    def spread(shard, axis):
        every = [shard] + [lax.ppermute(shard, "g", [((i + k) % gn, i) for i in range(gn)]) for k in range(1, gn)]
        return [jnp.concatenate(every, axis=axis)] if joined else every

    def send_home(parts):
        total = parts[0]
        for k in range(1, gn):
            total = total + lax.ppermute(parts[k].astype(LOW), "g", [(i, (i + k) % gn) for i in range(gn)]).astype(F32)
        return total

    steps = [("y", 1, lax.axis_index("y"), yn)] if yn == 2 else []
    steps += [("z", 1 << b, lax.axis_index("z"), zn) for b in range((zn - 1).bit_length())]

    def pairwise(rows, axis, far, size):
        return lax.ppermute(rows, axis, [(i, i ^ far) for i in range(size)])

    def sum_groups(total):
        for axis, far, at, size in steps:
            half = total.shape[0] // 2
            bit = (at // far) % 2
            away = lax.dynamic_slice_in_dim(total, (1 - bit) * half, half, 0).astype(LOW)
            keep = lax.dynamic_slice_in_dim(total, bit * half, half, 0)
            total = keep + pairwise(away, axis, far, size).astype(F32)
        total = total.astype(LOW)
        for axis, far, at, size in reversed(steps):
            got = pairwise(total, axis, far, size)
            total = jnp.where((at // far) % 2 == 0, jnp.concatenate([total, got]), jnp.concatenate([got, total]))
        return total.astype(F32)

    def fetch_slices(shards):
        at = lax.axis_index("z") * yn + lax.axis_index("y")
        pieces = [lax.dynamic_slice_in_dim(shard, at * (shard.shape[0] // (zn * yn)), shard.shape[0] // (zn * yn), 0) for shard in shards]
        pieces = [jnp.stack(pieces)] if pieces[0].shape == pieces[1].shape else [piece[None] for piece in pieces]
        return [[lax.ppermute(piece, "g", [((i + k) % gn, i) for i in range(gn)]) for piece in pieces] for k in range(1, gn)]

    def spread_wide(shards, slices):
        every = [[shard] for shard in shards]
        for got in slices:
            whole = [rows for piece in got for rows in lax.all_gather(piece, ("z", "y"), axis=1, tiled=True)]
            for at, rows in enumerate(whole):
                every[at].append(rows)
        return [[jnp.concatenate(part, axis=1 - at)] if joined else part for at, part in enumerate(every)]

    def parts_of(values, axis):
        return jnp.split(values[0], gn, axis=axis) if joined else values

    target_length = lax.dynamic_slice_in_dim(target_lengths, seq, 1, 0)
    memory_length = lax.dynamic_slice_in_dim(memory_lengths, seq, 1, 0)

    def after(value, *needed):
        return lax.optimization_barrier((value,) + needed)[0]

    token_all = gather_rows(tokens)
    biases = spread(jnp.concatenate([proj_bias, feed_bias.reshape(-1, width)]), 1)
    feed_rows = feed_bias.shape[0] // width
    if joined:
        halves = jnp.split(biases[0], gn, axis=1)
        b_in = [jnp.concatenate([part[4:].reshape(-1) for part in halves])]
    else:
        b_in = [part[4:].reshape(-1) for part in biases]
    b_proj = [part[:4] for part in biases]
    slices = fetch_slices((feed_in, feed_out))
    w_self = spread(after(self_inputs, token_all, biases[-1], slices[-1][0]), 2)
    w_in, w_out = spread_wide((feed_in, feed_out), slices)
    self_q, self_k, self_v, self_mixed, self_lse = [], [], [], [], []
    shards = range(len(w_self))
    for s in shards:
        self_q.append((_nn(token_all, w_self[s][0]) + b_proj[s][0]).astype(LOW))
        self_k.append(_nn(token_all, w_self[s][1]).astype(LOW))
        self_v.append((_nn(token_all, w_self[s][2]) + b_proj[s][1]).astype(LOW))
        mixed, lse = attn_fwd(target_length, self_q[s], self_k[s], self_v[s], True)
        self_mixed.append(mixed)
        self_lse.append(lse)
    first = self_mixed[0]
    w_self_out = spread(after(self_output, first), 0)
    memory_all = gather_rows(after(memory, first))
    w_cross_mem = spread(after(cross_memory, first), 2)
    w_cross_q = spread(after(cross_query, first), 1)
    w_cross_out = spread(after(cross_output, first), 0)
    cot_all = gather_rows(after(cotangent, self_mixed[-1]))

    cross_k = [_nn(memory_all, w_cross_mem[s][0]).astype(LOW) for s in shards]
    cross_v = [(_nn(memory_all, w_cross_mem[s][1]) + b_proj[s][3]).astype(LOW) for s in shards]
    branch_one = sum_all(sum(_nn(self_mixed[s], w_self_out[s]) for s in shards)) + branch_bias[0]
    normed_one, unit_one, inverse_one = norm_forward(residual_scale * token_all.astype(F32) + branch_one, norm_gain[0], norm_shift[0])
    second = normed_one.astype(LOW)
    cross_q = [(_nn(second, w_cross_q[s]) + b_proj[s][2]).astype(LOW) for s in shards]
    cross_mixed, cross_lse = zip(*[attn_fwd(memory_length, cross_q[s], cross_k[s], cross_v[s], False) for s in shards])
    branch_two = sum_all(sum(_nn(cross_mixed[s], w_cross_out[s]) for s in shards)) + branch_bias[1]
    normed_two, unit_two, inverse_two = norm_forward(residual_scale * normed_one + branch_two, norm_gain[1], norm_shift[1])
    third = normed_two.astype(LOW)
    hidden_pre = [_nn(third, w_in[s]) + b_in[s].astype(F32) for s in shards]
    hidden = [gelu_exact(hidden_pre[s]).astype(LOW) for s in shards]
    branch_three = sum_all(sum(_nn(hidden[s], w_out[s]) for s in shards)) + branch_bias[2]
    normed_three, unit_three, inverse_three = norm_forward(residual_scale * normed_two + branch_three, norm_gain[2], norm_shift[2])
    block_out = own_rows(normed_three.astype(LOW))

    cot = cot_all.astype(F32)
    grad_three = norm_backward(cot, unit_three, inverse_three, norm_gain[2])
    low_three = grad_three.astype(LOW)
    grad_hidden = [_nt(low_three, w_out[s]) for s in shards]
    feed_out_parts = parts_of([tn(hidden[s], low_three) for s in shards], 0)
    grad_pre = [gelu_backward(hidden_pre[s], grad_hidden[s]).astype(LOW) for s in shards]
    feed_in_parts = parts_of([tn(third, grad_pre[s]) for s in shards], 1)
    grad_normed_two = residual_scale * grad_three + sum_all(sum(_nt(grad_pre[s], w_in[s]) for s in shards))
    grad_two = norm_backward(grad_normed_two, unit_two, inverse_two, norm_gain[1])
    low_two = grad_two.astype(LOW)

    def sums(rows):
        return jnp.sum(rows.astype(F32), axis=0)

    def low_pairs(*parts):
        return [(part[0].astype(LOW), part[1].astype(LOW)) for part in parts]

    in_kernel = (zn, yn, gn, cn, width, joined) == (4, 2, 2, 2, SPAN, False)
    if in_kernel:
        per_shard = [(cross_q[s], cross_k[s], cross_v[s], cross_mixed[s], cross_lse[s]) for s in shards]
        row_part, memory_part, cross_sums, go_own, go_other, gq_own, gq_other, gm_own, gm_other, feed_out_sum, feed_in_sum = cross_back(
            memory_length, low_two, per_shard[0], per_shard[1], w_cross_out, second.T, memory_all.T, w_cross_q, w_cross_mem, low_pairs(feed_out_parts, feed_in_parts))
        cross_sums = [cross_sums[0, :2], cross_sums[1, :2]]
        grad_memory = memory_part.astype(LOW)
        grad_normed_one = residual_scale * grad_two + row_part
    else:
        feed_out_sum, feed_in_sum = [sum_groups(send_home(part)) for part in (feed_out_parts, feed_in_parts)]
        grad_cross_mixed = [_nt(low_two, w_cross_out[s]).astype(LOW) for s in shards]
        cross_out_parts = parts_of([tn(cross_mixed[s], low_two) for s in shards], 0)
        cross_dq, cross_dk, cross_dv = zip(*[attn_bwd(memory_length, cross_q[s], cross_k[s], cross_v[s], cross_mixed[s], grad_cross_mixed[s], cross_lse[s], False) for s in shards])
        grad_normed_one = residual_scale * grad_two + sum_all(sum(_nt(cross_dq[s], w_cross_q[s]) for s in shards))
        cross_parts = [parts_of([tn(rows, grads[s]) for s in shards], 1) for rows, grads in ((second, cross_dq), (memory_all, cross_dk), (memory_all, cross_dv))]
        grad_memory = sum_own(sum(_nt(cross_dk[s], w_cross_mem[s][0]) + _nt(cross_dv[s], w_cross_mem[s][1]) for s in shards)).astype(LOW)
        cross_sums = parts_of([jnp.stack([sums(cross_dq[s]), sums(cross_dv[s])]) for s in shards], 1)
    grad_one = norm_backward(grad_normed_one, unit_one, inverse_one, norm_gain[0])
    low_one = grad_one.astype(LOW)

    model = tokens.shape[1]
    terms = jnp.stack([sums(low_one), sums(low_two), sums(low_three), sums(grad_normed_one * unit_one), sums(grad_normed_two * unit_two), sums(cot * unit_three), sums(grad_normed_one), sums(grad_normed_two), sums(cot)])
    feed_sums = parts_of([sums(grad_pre[s]) for s in shards], 0)
    if not in_kernel:
        grad_self_mixed = [_nt(low_one, w_self_out[s]).astype(LOW) for s in shards]
        self_out_parts = parts_of([tn(self_mixed[s], low_one) for s in shards], 0)
        self_dq, self_dk, self_dv = zip(*[attn_bwd(target_length, self_q[s], self_k[s], self_v[s], self_mixed[s], grad_self_mixed[s], self_lse[s], True) for s in shards])
        token_part = sum_own(sum(_nt(self_dq[s], w_self[s][0]) + _nt(self_dk[s], w_self[s][1]) + _nt(self_dv[s], w_self[s][2]) for s in shards))
        self_sums = parts_of([jnp.stack([sums(self_dq[s]), sums(self_dv[s])]) for s in shards], 1)
    else:
        self_sums = [jnp.zeros((2, width), F32)] * gn
    smalls = []
    for k in range(gn):
        small = lax.dynamic_slice_in_dim(terms, ((seq + k) % gn * cn + core) * width, width, 1)
        small = jnp.concatenate([small, self_sums[k], cross_sums[k], feed_sums[k].reshape(-1, width)])
        smalls.append(jnp.pad(small, ((0, 16 * zn * yn - small.shape[0]), (0, 0))))
    if in_kernel:
        per_shard = [(self_q[s], self_k[s], self_v[s], self_mixed[s], self_lse[s]) for s in shards]
        pairs = [(go_own, go_other), (gq_own, gq_other), (gm_own, gm_other)]
        token_part, *sums_low = self_back(target_length, low_one, per_shard[0], per_shard[1], w_self_out, token_all.T, w_self, smalls, pairs)
    else:
        groups = [[cross_out_parts], cross_parts[:1], cross_parts[1:], [self_out_parts], [parts_of([tn(token_all, grads[s]) for s in shards], 1) for grads in (self_dq, self_dk, self_dv)], [smalls]]
        sums_low = [sum_groups(send_home([jnp.concatenate([part[k] for part in group]) for k in range(gn)])) for group in groups]
    cross_out_sum, cross_q_sum, cross_mem_sum, self_out_sum, self_in_sum, small = [rows.astype(F32) for rows in sums_low]
    feed_out_sum, feed_in_sum = feed_out_sum.astype(F32), feed_in_sum.astype(F32)
    grad_tokens = (residual_scale * own_rows(grad_one) + token_part).astype(LOW)
    return (block_out, grad_tokens, grad_memory, self_in_sum.reshape(3, model, width), self_out_sum, cross_q_sum, cross_mem_sum.reshape(2, model, width), cross_out_sum, feed_in_sum, feed_out_sum, small[9:13], small[13:13 + feed_rows].reshape(-1), small[0:3], small[3:6], small[6:9])


def solution(mesh):
    dp, mp = mesh.shape["dp"], mesh.shape["mp"]

    def whole(*args):
        yn = 2 if dp % 2 == 0 else 1
        gn = args[3].shape[0] // dp
        sizes = (dp // yn, yn, gn, mp // gn)
        fine = Mesh(mesh.devices.reshape(sizes), ("z", "y", "g", "c"))
        d, m = ("z", "y"), ("g", "c")
        rows, wide, tall = P(d + m, None), P(None, m), P(m, None)
        stack = P(None, None, m)
        in_specs = (rows, rows, rows, P(d), P(d), stack, tall, wide, stack, tall, wide, tall, wide, P(m), P(), P(), P())
        out_specs = (rows, rows, rows, stack, tall, wide, stack, tall, wide, tall, wide, P(m), wide, wide, wide)
        return jax.shard_map(functools.partial(layer, sizes), mesh=fine, in_specs=in_specs, out_specs=out_specs, check_vma=False)(*args)

    return whole
```

```python
import functools
import math

import jax, jax.numpy as jnp
from jax import lax
from jax.experimental import pallas as pl
from jax.experimental.pallas import tpu as pltpu
from jax.sharding import Mesh
from jax.sharding import PartitionSpec as P

HEAD = 64
NEG = -1e30

def _nt(a, b):
    return lax.dot_general(a, b, (((1,), (1,)), ((), ())), preferred_element_type=jnp.float32)

def _nn(a, b):
    return lax.dot_general(a, b, (((1,), (0,)), ((), ())), preferred_element_type=jnp.float32)

def _lanes(rows):
    return lax.broadcasted_iota(jnp.int32, (rows, 128), 1)

def _put(base, lane, pairs):
    for at, val in pairs:
        base = jnp.where(lane == at, val, base)
    return base

def fwd_kernel(len_ref, q_ref, k_ref, v_ref, o_ref, lse_ref, *, causal, bq):
    p = pl.program_id(0)
    rows, keys = q_ref.shape[0], k_ref.shape[0]
    length = len_ref[0]
    kl = _lanes(keys)
    kpos = lax.broadcasted_iota(jnp.int32, (keys, 128), 0)
    kbias = jnp.where(kpos < length, 0.0, NEG)
    k2 = k_ref[...].astype(jnp.float32)
    v2 = v_ref[...].astype(jnp.float32)
    ql = _lanes(bq)
    heads = []
    for h in range(2):
        mine = (kl // HEAD) == h
        other = HEAD * (1 - h)
        kh = jnp.where(mine, k2, jnp.where(kl == other, kbias, 0.0)).astype(jnp.bfloat16)
        vh = jnp.where(mine, v2, jnp.where(kl == other, 1.0, 0.0)).astype(jnp.bfloat16)
        heads.append((kh, vh))
    for i in range(rows // bq):
        q2 = q_ref[pl.ds(i * bq, bq), :].astype(jnp.float32) * (HEAD ** -0.5)
        out = jnp.zeros((bq, 128), jnp.float32)
        lse_all = lse_ref[pl.ds(i * bq, bq), :]
        for h in range(2):
            kh, vh = heads[h]
            mine = (ql // HEAD) == h
            other = HEAD * (1 - h)
            qh = jnp.where(mine, q2, jnp.where(ql == other, 1.0, 0.0)).astype(jnp.bfloat16)
            if causal:
                lo = i * bq
                sd = _nt(qh, kh[lo:lo + bq])
                r = lax.broadcasted_iota(jnp.int32, (bq, bq), 0)
                c = lax.broadcasted_iota(jnp.int32, (bq, bq), 1)
                sd = jnp.where(c <= r, sd, NEG)
                m = jnp.max(sd, axis=1, keepdims=True)
                if lo:
                    sl = _nt(qh, kh[:lo])
                    m = jnp.maximum(m, jnp.max(sl, axis=1, keepdims=True))
                    acc = _nn(jnp.exp(sl - m).astype(jnp.bfloat16), vh[:lo])
                    acc += _nn(jnp.exp(sd - m).astype(jnp.bfloat16), vh[lo:lo + bq])
                else:
                    acc = _nn(jnp.exp(sd - m).astype(jnp.bfloat16), vh[:bq])
            else:
                s = _nt(qh, kh)
                m = jnp.max(s, axis=1, keepdims=True)
                acc = _nn(jnp.exp(s - m).astype(jnp.bfloat16), vh)
            total = jnp.sum(jnp.where(ql == other, acc, 0.0), axis=1, keepdims=True)
            out = jnp.where(mine, acc / total, out)
            lse_all = jnp.where(ql == 2 * p + h, m + jnp.log(total), lse_all)
        o_ref[pl.ds(i * bq, bq), :] = out.astype(jnp.bfloat16)
        lse_ref[pl.ds(i * bq, bq), :] = lse_all

def attn_fwd(length, q, k, v, causal, bq=256):
    rows, cols = q.shape
    keys = k.shape[0]
    pairs = cols // 128
    el = pairs * 2 * rows * keys
    return pl.pallas_call(
        functools.partial(fwd_kernel, causal=causal, bq=bq),
        out_shape=(jax.ShapeDtypeStruct((rows, cols), jnp.bfloat16), jax.ShapeDtypeStruct((rows, 128), jnp.float32)),
        grid_spec=pltpu.PrefetchScalarGridSpec(
            num_scalar_prefetch=1, grid=(pairs,),
            in_specs=[pl.BlockSpec((rows, 128), lambda p, n: (0, p)), pl.BlockSpec((keys, 128), lambda p, n: (0, p)), pl.BlockSpec((keys, 128), lambda p, n: (0, p))],
            out_specs=[pl.BlockSpec((rows, 128), lambda p, n: (0, p)), pl.BlockSpec((rows, 128), lambda p, n: (0, 0))],
        ),
        compiler_params=pltpu.CompilerParams(dimension_semantics=("arbitrary",), vmem_limit_bytes=40 << 20),
        cost_estimate=pl.CostEstimate(flops=16 * el * 64, bytes_accessed=8 * rows * cols, transcendentals=el),
        name="attend_forward",
    )(length, q, k, v)

def split3(x):
    a = x.astype(jnp.bfloat16).astype(jnp.float32)
    b = (x - a).astype(jnp.bfloat16).astype(jnp.float32)
    return a, b, x - a - b


def key_side(k2, v2, length):
    keys = k2.shape[0]
    kl = _lanes(keys)
    kbias = jnp.where(lax.broadcasted_iota(jnp.int32, (keys, 128), 0) < length, 0.0, NEG)
    k2, v2 = k2.astype(jnp.float32), v2.astype(jnp.float32)
    heads = []
    for h in range(2):
        mine = (kl // HEAD) == h
        other = HEAD * (1 - h)
        ones = (kl > other) & (kl < other + 4)
        kh = jnp.where(mine, k2, jnp.where(kl == other, kbias, jnp.where(ones, 1.0, 0.0))).astype(jnp.bfloat16)
        vh = jnp.where(mine, v2, jnp.where(ones, 1.0, 0.0)).astype(jnp.bfloat16)
        heads.append((kh, vh, kh.T))
    return heads


def query_block(heads, q2, o2, g2, lse_all, pair, i, last, causal, dka, dva):
    bq = q2.shape[0]
    keys = heads[0][0].shape[0]
    ql = _lanes(bq)
    q2 = q2.astype(jnp.float32) * (HEAD ** -0.5)
    g2 = g2.astype(jnp.float32)
    go = g2 * o2.astype(jnp.float32)
    dqt = []
    for h in range(2):
        kh, vh, kt = heads[h]
        mine = (ql // HEAD) == h
        other = HEAD * (1 - h)
        lse = jnp.sum(jnp.where(ql == 2 * pair + h, lse_all, 0.0), axis=1, keepdims=True)
        delta = jnp.sum(jnp.where(mine, go, 0.0), axis=1, keepdims=True)
        la, lb, lc = split3(-lse)
        da, db, dc = split3(-delta)
        qh = _put(jnp.where(mine, q2, 0.0), ql, ((other, 1.0), (other + 1, la), (other + 2, lb), (other + 3, lc))).astype(jnp.bfloat16)
        gh = _put(jnp.where(mine, g2, 0.0), ql, ((other + 1, da), (other + 2, db), (other + 3, dc))).astype(jnp.bfloat16)
        hi = (i + 1) * bq if causal else keys
        st = _nt(kh[:hi], qh)
        if causal:
            kr = lax.broadcasted_iota(jnp.int32, (hi, bq), 0)
            qc = lax.broadcasted_iota(jnp.int32, (hi, bq), 1) + i * bq
            pt = jnp.where(kr <= qc, jnp.exp(st), 0.0)
        else:
            pt = jnp.exp(st)
        dst = (pt * _nt(vh[:hi], gh)).astype(jnp.bfloat16)
        dvn = _nn(pt.astype(jnp.bfloat16), gh)
        dkn = _nn(dst, qh)
        if last:
            dva[h, :hi] = dvn
            dka[h, :hi] = dkn
        else:
            dva[h, :hi] += dvn
            dka[h, :hi] += dkn
        dqt.append(_nn(kt[:, :hi], dst))
    dq = jnp.concatenate([dqt[0][:HEAD], dqt[1][HEAD:]], axis=0).T
    return (dq * (HEAD ** -0.5)).astype(jnp.bfloat16)


def bwd_kernel(len_ref, q_ref, k_ref, v_ref, o_ref, g_ref, lse_ref, dq_ref, dk_ref, dv_ref, dka, dva, *, causal, bq):
    rows, keys = q_ref.shape[0], k_ref.shape[0]
    heads = key_side(k_ref[...], v_ref[...], len_ref[0])
    blocks = rows // bq
    for i in reversed(range(blocks)):
        at = pl.ds(i * bq, bq)
        dq_ref[at, :] = query_block(heads, q_ref[at, :], o_ref[at, :], g_ref[at, :], lse_ref[at, :], pl.program_id(0), i, i == blocks - 1, causal, dka, dva)
    first = _lanes(keys) < HEAD
    dk_ref[...] = jnp.where(first, dka[0], dka[1]).astype(jnp.bfloat16)
    dv_ref[...] = jnp.where(first, dva[0], dva[1]).astype(jnp.bfloat16)

def attn_bwd(length, q, k, v, o, g, lse, causal, bq=256):
    rows, cols = q.shape
    keys = k.shape[0]
    pairs = cols // 128
    el = pairs * 2 * rows * keys
    qs = pl.BlockSpec((rows, 128), lambda p, n: (0, p))
    ks = pl.BlockSpec((keys, 128), lambda p, n: (0, p))
    return pl.pallas_call(
        functools.partial(bwd_kernel, causal=causal, bq=bq),
        out_shape=(jax.ShapeDtypeStruct((rows, cols), jnp.bfloat16), jax.ShapeDtypeStruct((keys, cols), jnp.bfloat16), jax.ShapeDtypeStruct((keys, cols), jnp.bfloat16)),
        grid_spec=pltpu.PrefetchScalarGridSpec(
            num_scalar_prefetch=1, grid=(pairs,),
            in_specs=[qs, ks, ks, qs, qs, pl.BlockSpec((rows, 128), lambda p, n: (0, 0))],
            out_specs=[qs, ks, ks],
            scratch_shapes=[pltpu.VMEM((2, keys, 128), jnp.float32), pltpu.VMEM((2, keys, 128), jnp.float32)],
        ),
        compiler_params=pltpu.CompilerParams(dimension_semantics=("arbitrary",), vmem_limit_bytes=48 << 20),
        cost_estimate=pl.CostEstimate(flops=40 * el * 64, bytes_accessed=16 * rows * cols, transcendentals=el),
        name="attend_backward",
    )(length, q, k, v, o, g, lse)

CHUNK = 512
LAG = 1
SPAN = 256


class Pipeline:
    AHEAD = 3

    def __init__(self, total, scratch):
        self.spots, self.total, self.step, self.sent, self.loaded = [], total, 0, 0, 0
        (self.held, self.ysum, self.zgot, self.mine, self.load, self.store, self.xs, self.xr, self.ys, self.yr, self.zs, self.zr, self.bs, self.br, self.es, self.er) = scratch
        self.full = self.held
        self.seq, self.ya, za = lax.axis_index("g"), lax.axis_index("y"), lax.axis_index("z")
        self.za = za
        self.peers = {1: za + 1 - 2 * (za % 2), 2: (za + 2) % 4, 3: 3 - za}
        self.stages = (self.to_y, self.to_z, self.back_z, self.back_y, self.finish)

    @staticmethod
    def scratch(total, most):
        dma = pltpu.SemaphoreType.DMA
        return [
            pltpu.VMEM((total, most, SPAN), LOW),
            pltpu.VMEM((total, most // 2, SPAN), LOW),
            pltpu.VMEM((total, 3, most // 8, SPAN), LOW),
            pltpu.VMEM((4, most, SPAN), LOW),
            dma((4,)), dma((total,)),
            dma((total,)), dma((total,)), dma((total,)), dma((total,)),
            dma((total, 3)), dma((total, 3)), dma((total, 3)), dma((total, 3)),
            dma((total,)), dma((total,)),
        ]

    def greet(self, more=()):
        barrier = pltpu.get_barrier_semaphore()
        everyone = [{"g": 1 - self.seq}, {"y": 1 - self.ya}] + [{"z": self.peers[d]} for d in (1, 2, 3)] + list(more)
        for where in everyone:
            pl.semaphore_signal(barrier, inc=1, device_id=where, device_id_type=pl.DeviceIdType.MESH)
        pl.semaphore_wait(barrier, len(everyone))

    def add(self, own, other, out, taper=False):
        for r, size in row_chunks(own.shape[0], taper):
            for c in range(0, own.shape[1], SPAN):
                self.spots.append((own, other, r, c, size, out, r))
        self.feed()

    def feed(self):
        while self.sent < min(len(self.spots), self.step + self.AHEAD):
            self.x_copy(self.sent).start()
            self.own_copy(self.sent).start()
            self.sent += 1

    def tick(self, times=1):
        for unused in range(times):
            if self.step >= self.total + LAG * (len(self.stages) - 1):
                return
            for at, stage in enumerate(self.stages):
                if 0 <= self.step - LAG * at < self.total:
                    stage(self.step - LAG * at)
            self.step += 1
            self.feed()

    def drain(self):
        assert len(self.spots) == self.total
        self.tick(self.total + LAG * len(self.stages))
        for k in range(self.total):
            self.x_copy(k).wait_send()
            self.yb_copy(k).wait_send()
            self.out_copy(k).wait()
            for d in (1, 2, 3):
                self.z_copy(k, d).wait_send()
                self.zb_copy(k, d).wait_send()

    @staticmethod
    def remote(src, dst, send, recv, where):
        return pltpu.make_async_remote_copy(src_ref=src, dst_ref=dst, send_sem=send, recv_sem=recv, device_id=where, device_id_type=pl.DeviceIdType.MESH)

    @staticmethod
    def block(at, size):
        return pl.ds(pl.multiple_of(at * size, size), size)

    def x_copy(self, k):
        own, other, r, c, n, o, q = self.spots[k]
        return self.remote(other.at[pl.ds(r, n), pl.ds(c, SPAN)], self.held.at[k, pl.ds(0, n)], self.xs.at[k], self.xr.at[k], {"g": 1 - self.seq})

    def own_copy(self, k):
        own, other, r, c, n, o, q = self.spots[k]
        return pltpu.make_async_copy(own.at[pl.ds(r, n), pl.ds(c, SPAN)], self.mine.at[k % 4, pl.ds(0, n)], self.load.at[k % 4])

    def y_copy(self, k):
        h = self.spots[k][4] // 2
        return self.remote(self.held.at[k, self.block(1 - self.ya, h)], self.ysum.at[k, pl.ds(0, h)], self.ys.at[k], self.yr.at[k], {"y": 1 - self.ya})

    def z_copy(self, k, d):
        p = self.spots[k][4] // 8
        return self.remote(self.ysum.at[k, self.block(self.peers[d], p)], self.zgot.at[k, d - 1, pl.ds(0, p)], self.zs.at[k, d - 1], self.zr.at[k, d - 1], {"z": self.peers[d]})

    def zb_copy(self, k, d):
        rows = self.full.at[k, self.block(self.ya * 4 + self.za, self.spots[k][4] // 8)]
        return self.remote(rows, rows, self.bs.at[k, d - 1], self.br.at[k, d - 1], {"z": self.peers[d]})

    def yb_copy(self, k):
        rows = self.full.at[k, self.block(self.ya, self.spots[k][4] // 2)]
        return self.remote(rows, rows, self.es.at[k], self.er.at[k], {"y": 1 - self.ya})

    def out_copy(self, k):
        own, other, r, c, n, o, q = self.spots[k]
        return pltpu.make_async_copy(self.full.at[k, pl.ds(0, n)], o.at[pl.ds(q, n), pl.ds(c, SPAN)], self.store.at[k])

    def to_y(self, k):
        n = self.spots[k][4]
        self.own_copy(k).wait()
        self.x_copy(k).wait_recv()
        self.held[k, :n] = self.held[k, :n] + self.mine[k % 4, :n]
        self.y_copy(k).start()

    def to_z(self, k):
        h = self.spots[k][4] // 2
        self.y_copy(k).wait()
        self.ysum[k, :h] = self.ysum[k, :h] + self.held[k, self.block(self.ya, h)]
        for d in (1, 2, 3):
            self.z_copy(k, d).start()

    def back_z(self, k):
        p = self.spots[k][4] // 8
        for d in (1, 2, 3):
            self.z_copy(k, d).wait_recv()
        rows = self.ysum[k, self.block(self.za, p)].astype(F32)
        for d in (1, 2, 3):
            rows = rows + self.zgot[k, d - 1, :p].astype(F32)
        self.full[k, self.block(self.ya * 4 + self.za, p)] = rows.astype(LOW)
        for d in (1, 2, 3):
            self.zb_copy(k, d).start()

    def back_y(self, k):
        for d in (1, 2, 3):
            self.zb_copy(k, d).wait_recv()
        self.yb_copy(k).start()

    def finish(self, k):
        self.yb_copy(k).wait_recv()
        self.out_copy(k).start()


def row_chunks(rows, taper=False):
    size = min(CHUNK, rows)
    sizes = [size] * (rows // size)
    if taper:
        sizes[-1:] = [size // 2, size // 4, size // 4]
    return [(sum(sizes[:i]), n) for i, n in enumerate(sizes)]


def spot_count(shapes, taper=()):
    return sum(len(row_chunks(rows, at in taper)) * (cols // SPAN) for at, (rows, cols) in enumerate(shapes))


def attend_back(pipe, shards, length, low, gm, dq, dk, dv, dka, dva, causal, bq):
    rows = low.shape[0]
    blocks = rows // bq
    for s, (q, k, v, o, l, wo) in enumerate(shards):
        for i in range(blocks):
            at = pl.ds(i * bq, bq)
            gm[s, at, :] = _nt(low[at, :], wo[...]).astype(LOW)
    for s, (q, k, v, o, l, wo) in enumerate(shards):
        for p in range(q.shape[1] // 128):
            cols = pl.ds(p * 128, 128)
            heads = key_side(k[:, cols], v[:, cols], length)
            for i in reversed(range(blocks)):
                at = pl.ds(i * bq, bq)
                dq[s, at, cols] = query_block(heads, q[at, cols], o[at, cols], gm[s, at, cols], l[at, :], p, i, i == blocks - 1, causal, dka, dva)
            first = _lanes(k.shape[0]) < HEAD
            dk[s, :, cols] = jnp.where(first, dka[0], dka[1]).astype(LOW)
            dv[s, :, cols] = jnp.where(first, dva[0], dva[1]).astype(LOW)
            pipe.tick()


def back_rows(terms, start, size):
    at = pl.ds(pl.multiple_of(start, size), size)
    both = None
    for grads, s, weight in terms:
        term = _nt(grads[s, at, :], weight)
        both = term if both is None else both + term
    return both


def output_grads(shards, low, outs):
    for (q, k, v, o, l, wo), out in zip(shards, outs):
        for c in range(0, low.shape[1], SPAN):
            out[:, c : c + SPAN] = tn(o[...], low[:, c : c + SPAN]).astype(LOW)


def input_grads(rows_in, grads, out, first, bq):
    for i in range(0, rows_in.shape[1], bq):
        out[pl.ds(first + i, bq), :] = tn(rows_in[:, i : i + bq], grads).astype(LOW)


def share_rows(terms, core, part, got, sems, out, bq, pipe):
    half = out.shape[0]
    copy = Pipeline.remote(part, got, sems[0], sems[1], {"c": 1 - core})
    for i in range(0, half, bq):
        part[pl.ds(i, bq), :] = back_rows(terms, (1 - core) * half + i, bq).astype(LOW)
    copy.start()
    pipe.tick()
    mine = [back_rows(terms, core * half + i, bq) for i in range(0, half, bq)]
    pipe.tick()
    copy.wait()
    for i in range(0, half, bq):
        out[pl.ds(i, bq), :] = (mine[i // bq] + got[pl.ds(i, bq), :].astype(F32)).astype(out.dtype)


def self_back_kernel(carried, bq, len_ref, low, q0, k0, v0, o0, l0, q1, k1, v1, o1, l1, wo0, wo1, x_in, w0, w1, small0, small1, *rest):
    own, other, rest = rest[:carried], rest[carried : 2 * carried], rest[2 * carried :]
    token_out, rest = rest[0], rest[1:]
    outs, rest = rest[: carried + 3], rest[carried + 3 :]
    gm, dq, dk, dv, dka, dva, go_own, go_other, gi_own, gi_other, sm_own, sm_other, part, got, part_send, part_recv = rest[:16]
    core = lax.axis_index("c")
    total = spot_count([ref.shape for ref in own] + [go_own.shape, sm_own.shape, gi_own.shape], (carried + 2,))
    pipe = Pipeline(total, rest[16:])
    pipe.greet([{"c": 1 - core}])
    for a, b, out in zip(own, other, outs):
        pipe.add(a, b, out)
    shards = ((q0, k0, v0, o0, l0, wo0), (q1, k1, v1, o1, l1, wo1))
    output_grads(shards, low, (go_own, go_other))
    pipe.add(go_own, go_other, outs[carried])
    attend_back(pipe, shards, len_ref[0], low, gm, dq, dk, dv, dka, dva, True, bq)
    for s, (gi, sm, small) in enumerate(((gi_own, sm_own, small0), (gi_other, sm_other, small1))):
        for m, grads in enumerate((dq, dk, dv)):
            input_grads(x_in, grads[s], gi, m * x_in.shape[1], bq)
        row = lax.broadcasted_iota(jnp.int32, sm.shape, 0)
        sums = [jnp.sum(grads[s].astype(F32), axis=0, keepdims=True) for grads in (dq, dv)]
        sm[...] = jnp.where(row == 9, sums[0], jnp.where(row == 10, sums[1], small[...])).astype(LOW)
    pipe.add(sm_own, sm_other, outs[carried + 2])
    pipe.add(gi_own, gi_other, outs[carried + 1], True)
    terms = [(grads, s, w[m]) for s, w in ((0, w0), (1, w1)) for m, grads in enumerate((dq, dk, dv))]
    share_rows(terms, core, part, got, (part_send, part_recv), token_out, bq, pipe)
    pipe.drain()


def cross_back_kernel(carried, bq, len_ref, low, q0, k0, v0, o0, l0, q1, k1, v1, o1, l1, wo0, wo1, x_in, m_in, wq0, wq1, wm0, wm1, *rest):
    own, other, rest = rest[:carried], rest[carried : 2 * carried], rest[2 * carried :]
    row_out, memory_out, sums_out, go_own, go_other, gq_own, gq_other, gm_own, gm_other = rest[:9]
    outs, rest = rest[9 : 9 + carried], rest[9 + carried :]
    gm, dq, dk, dv, dka, dva, part, got, part_send, part_recv, full_part, full_got, full_send, full_recv = rest[:14]
    core = lax.axis_index("c")
    pipe = Pipeline(spot_count([ref.shape for ref in own], (carried - 1,)), rest[14:])
    pipe.greet([{"c": 1 - core}])
    for at, (a, b, out) in enumerate(zip(own, other, outs)):
        pipe.add(a, b, out, at == carried - 1)
    shards = ((q0, k0, v0, o0, l0, wo0), (q1, k1, v1, o1, l1, wo1))
    attend_back(pipe, shards, len_ref[0], low, gm, dq, dk, dv, dka, dva, False, bq)
    rows = low.shape[0]
    terms = [(dq, 0, wq0[...]), (dq, 1, wq1[...])]
    for i in range(0, rows, bq):
        full_part[pl.ds(i, bq), :] = back_rows(terms, i, bq).astype(LOW)
    exchange = Pipeline.remote(full_part, full_got, full_send, full_recv, {"c": 1 - core})
    exchange.start()
    pipe.tick()
    terms = [(grads, s, w[m]) for s, w in ((0, wm0), (1, wm1)) for m, grads in enumerate((dk, dv))]
    share_rows(terms, core, part, got, (part_send, part_recv), memory_out, bq, pipe)
    output_grads(shards, low, (go_own, go_other))
    pipe.tick()
    for s, (gq, gkv) in enumerate(((gq_own, gm_own), (gq_other, gm_other))):
        input_grads(x_in, dq[s], gq, 0, bq)
        input_grads(m_in, dk[s], gkv, 0, bq)
        input_grads(m_in, dv[s], gkv, m_in.shape[1], bq)
        sums_out[s, 0:1] = jnp.sum(dq[s].astype(F32), axis=0, keepdims=True)
        sums_out[s, 1:2] = jnp.sum(dv[s].astype(F32), axis=0, keepdims=True)
        pipe.tick()
    exchange.wait()
    for i in range(0, rows, bq):
        at = pl.ds(i, bq)
        row_out[at, :] = (full_part[at, :].astype(F32) + full_got[at, :].astype(F32)).astype(LOW)
    pipe.drain()


def low_ram(*shape):
    return pltpu.VMEM(shape, LOW)


def back_scratch(rows, width):
    return [low_ram(2, rows, width) for unused in range(4)] + [pltpu.VMEM((2, rows, 128), F32), pltpu.VMEM((2, rows, 128), F32)]


def self_back(length, low, first, second, wo, x_in, w, smalls, pairs, bq=256):
    rows, model = low.shape
    width = wo[0].shape[0]
    carried = len(pairs)
    any_space = pl.BlockSpec(memory_space=pl.ANY)
    vmem = pl.BlockSpec(memory_space=pltpu.VMEM)
    dma = pltpu.SemaphoreType.DMA
    ends = [(width, model), (3 * rows, width), smalls[0].shape]
    total = spot_count([own.shape for own, unused in pairs] + [ends[0], ends[2], ends[1]], (carried + 2,))
    return pl.pallas_call(
        functools.partial(self_back_kernel, carried, bq),
        out_shape=[jax.ShapeDtypeStruct((rows // 2, model), F32)] + [jax.ShapeDtypeStruct(own.shape, LOW) for own, unused in pairs] + [jax.ShapeDtypeStruct(shape, LOW) for shape in ends],
        in_specs=[pl.BlockSpec(memory_space=pltpu.SMEM)] + [vmem] * 18 + [any_space] * (2 * carried),
        out_specs=[vmem] + [any_space] * (carried + 3),
        scratch_shapes=back_scratch(rows, width)
        + [low_ram(width, model), low_ram(width, model), low_ram(3 * rows, width), low_ram(3 * rows, width), low_ram(*smalls[0].shape), low_ram(*smalls[0].shape)]
        + [low_ram(rows // 2, model), low_ram(rows // 2, model), dma, dma]
        + Pipeline.scratch(total, CHUNK),
        compiler_params=pltpu.CompilerParams(collective_id=0, has_side_effects=True, vmem_limit_bytes=58 << 20),
        cost_estimate=pl.CostEstimate(flops=20 * rows * model * width, bytes_accessed=300 << 20, transcendentals=8 * rows * rows),
        name="self_backward",
    )(length, low, *first, *second, *wo, x_in, *w, *smalls, *[p[0] for p in pairs], *[p[1] for p in pairs])


def cross_back(length, low, first, second, wo, x_in, m_in, wq, wm, pairs, bq=256):
    rows, model = low.shape
    width = wo[0].shape[0]
    carried = len(pairs)
    any_space = pl.BlockSpec(memory_space=pl.ANY)
    vmem = pl.BlockSpec(memory_space=pltpu.VMEM)
    dma = pltpu.SemaphoreType.DMA
    total = spot_count([own.shape for own, unused in pairs], (carried - 1,))
    shape = jax.ShapeDtypeStruct
    return pl.pallas_call(
        functools.partial(cross_back_kernel, carried, bq),
        out_shape=[shape((rows, model), LOW), shape((rows // 2, model), LOW), shape((2, 8, width), F32)]
        + [shape((width, model), LOW)] * 2 + [shape((rows, width), LOW)] * 2 + [shape((2 * rows, width), LOW)] * 2
        + [shape(own.shape, LOW) for own, unused in pairs],
        in_specs=[pl.BlockSpec(memory_space=pltpu.SMEM)] + [vmem] * 19 + [any_space] * (2 * carried),
        out_specs=[vmem] * 9 + [any_space] * carried,
        scratch_shapes=back_scratch(rows, width)
        + [low_ram(rows // 2, model), low_ram(rows // 2, model), dma, dma]
        + [low_ram(rows, model), low_ram(rows, model), dma, dma]
        + Pipeline.scratch(total, CHUNK),
        compiler_params=pltpu.CompilerParams(collective_id=1, has_side_effects=True, vmem_limit_bytes=58 << 20),
        cost_estimate=pl.CostEstimate(flops=20 * rows * model * width, bytes_accessed=300 << 20, transcendentals=8 * rows * rows),
        name="cross_backward",
    )(length, low, *first, *second, *wo, x_in, m_in, *wq, *wm, *[p[0] for p in pairs], *[p[1] for p in pairs])


def feed_kernel(count, rows_in, *refs):
    w_in, b_in, w_out, part, hidden, slope = refs[:count], refs[count : 2 * count], refs[2 * count : 3 * count], refs[3 * count], refs[3 * count + 1 : 4 * count + 1], refs[4 * count + 1 :]
    branch = None
    for s in range(count):
        pre = _nn(rows_in[...], w_in[s][...]) + b_in[s][...].astype(F32)
        spread_to = 0.5 + 0.5 * lax.erf(pre * 0.5**0.5)
        hidden[s][...] = (pre * spread_to).astype(LOW)
        slope[s][...] = (spread_to + pre * (jnp.exp(-0.5 * pre * pre) * (2.0 * math.pi) ** -0.5)).astype(LOW)
        term = _nn(hidden[s][...], w_out[s][...])
        branch = term if branch is None else branch + term
    part[...] = branch.astype(LOW)


def feed_forward(rows_in, w_in, b_in, w_out, bq=256):
    count = len(w_in)
    rows, model = rows_in.shape
    units = w_in[0].shape[1]
    wide = pl.BlockSpec((bq, units), lambda i: (i, 0))
    block = pl.BlockSpec((bq, model), lambda i: (i, 0))
    held = lambda array: pl.BlockSpec(array.shape, lambda i: (0, 0))
    out = pl.pallas_call(
        functools.partial(feed_kernel, count),
        grid=(rows // bq,),
        out_shape=[jax.ShapeDtypeStruct((rows, model), LOW)] + [jax.ShapeDtypeStruct((rows, units), LOW)] * (2 * count),
        in_specs=[block] + [held(array) for array in (*w_in, *b_in, *w_out)],
        out_specs=[block] + [wide] * (2 * count),
        compiler_params=pltpu.CompilerParams(dimension_semantics=("arbitrary",), vmem_limit_bytes=50 << 20),
        cost_estimate=pl.CostEstimate(flops=4 * count * rows * model * units, bytes_accessed=16 << 20, transcendentals=2 * count * rows * units),
        name="feed_forward",
    )(rows_in, *w_in, *b_in, *w_out)
    return out[0], out[1 : 1 + count], out[1 + count :]


residual_scale = 300.0**0.25
norm_epsilon = 1e-05
LOW = jnp.bfloat16
F32 = jnp.float32


def tn(rows, grads):
    return lax.dot_general(rows, grads, (((0,), (0,)), ((), ())), preferred_element_type=F32)


def norm_forward(summed, gain_row, shift_row):
    row_mean = jnp.mean(summed, axis=-1, keepdims=True)
    centred = summed - row_mean
    variance = jnp.mean(centred * centred, axis=-1, keepdims=True)
    inverse = lax.rsqrt(variance + norm_epsilon)
    unit_rows = centred * inverse
    return unit_rows * gain_row + shift_row, unit_rows, inverse


def norm_backward(grad_out, unit_rows, inverse, gain_row):
    grad_unit = grad_out * gain_row
    first_mean = jnp.mean(grad_unit, axis=-1, keepdims=True)
    second_mean = jnp.mean(grad_unit * unit_rows, axis=-1, keepdims=True)
    return inverse * (grad_unit - first_mean - unit_rows * second_mean)


def layer(sizes, tokens, memory, cotangent, target_lengths, memory_lengths, self_inputs, self_output, cross_query, cross_memory, cross_output, feed_in, feed_out, proj_bias, feed_bias, branch_bias, norm_gain, norm_shift):
    zn, yn, gn, cn = sizes
    seq = lax.axis_index("g")
    core = lax.axis_index("c")
    width = self_output.shape[0]
    joined = width % 128 != 0

    def swap(rows):
        return lax.ppermute(rows, "c", [(0, 1), (1, 0)])

    def gather_rows(rows):
        if cn != 2:
            return lax.all_gather(rows, "c", axis=0, tiled=True)
        got = swap(rows)
        return jnp.where(core == 0, jnp.concatenate([rows, got]), jnp.concatenate([got, rows]))

    def sum_all(part):
        part = part.astype(LOW)
        if cn != 2:
            return lax.psum(part, "c").astype(F32)
        return part.astype(F32) + swap(part).astype(F32)

    def own_rows(rows):
        size = rows.shape[0] // cn
        return lax.dynamic_slice_in_dim(rows, core * size, size, 0)

    def sum_own(part):
        if cn != 2:
            return lax.psum_scatter(part.astype(LOW), "c", scatter_dimension=0, tiled=True).astype(F32)
        size = part.shape[0] // 2
        got = swap(lax.dynamic_slice_in_dim(part, (1 - core) * size, size, 0).astype(LOW))
        return lax.dynamic_slice_in_dim(part, core * size, size, 0) + got.astype(F32)

    def spread(shard, axis):
        every = [shard] + [lax.ppermute(shard, "g", [((i + k) % gn, i) for i in range(gn)]) for k in range(1, gn)]
        return [jnp.concatenate(every, axis=axis)] if joined else every

    def send_home(parts):
        total = parts[0]
        for k in range(1, gn):
            total = total + lax.ppermute(parts[k].astype(LOW), "g", [(i, (i + k) % gn) for i in range(gn)]).astype(F32)
        return total

    steps = [("y", 1, lax.axis_index("y"), yn)] if yn == 2 else []
    steps += [("z", 1 << b, lax.axis_index("z"), zn) for b in range((zn - 1).bit_length())]

    def pairwise(rows, axis, far, size):
        return lax.ppermute(rows, axis, [(i, i ^ far) for i in range(size)])

    def sum_groups(total):
        for axis, far, at, size in steps:
            half = total.shape[0] // 2
            bit = (at // far) % 2
            away = lax.dynamic_slice_in_dim(total, (1 - bit) * half, half, 0).astype(LOW)
            keep = lax.dynamic_slice_in_dim(total, bit * half, half, 0)
            total = keep + pairwise(away, axis, far, size).astype(F32)
        total = total.astype(LOW)
        for axis, far, at, size in reversed(steps):
            got = pairwise(total, axis, far, size)
            total = jnp.where((at // far) % 2 == 0, jnp.concatenate([total, got]), jnp.concatenate([got, total]))
        return total.astype(F32)

    def fetch_slices(shards):
        at = lax.axis_index("z") * yn + lax.axis_index("y")
        pieces = [lax.dynamic_slice_in_dim(shard, at * (shard.shape[0] // (zn * yn)), shard.shape[0] // (zn * yn), 0) for shard in shards]
        pieces = [jnp.stack(pieces)] if pieces[0].shape == pieces[1].shape else [piece[None] for piece in pieces]
        return [[lax.ppermute(piece, "g", [((i + k) % gn, i) for i in range(gn)]) for piece in pieces] for k in range(1, gn)]

    def spread_wide(shards, slices):
        every = [[shard] for shard in shards]
        for got in slices:
            whole = [rows for piece in got for rows in lax.all_gather(piece, ("z", "y"), axis=1, tiled=True)]
            for at, rows in enumerate(whole):
                every[at].append(rows)
        return [[jnp.concatenate(part, axis=1 - at)] if joined else part for at, part in enumerate(every)]

    def parts_of(values, axis):
        return jnp.split(values[0], gn, axis=axis) if joined else values

    target_length = lax.dynamic_slice_in_dim(target_lengths, seq, 1, 0)
    memory_length = lax.dynamic_slice_in_dim(memory_lengths, seq, 1, 0)

    def after(value, *needed):
        return lax.optimization_barrier((value,) + needed)[0]

    token_all = gather_rows(tokens)
    biases = spread(jnp.concatenate([proj_bias, feed_bias.reshape(-1, width)]), 1)
    feed_rows = feed_bias.shape[0] // width
    if joined:
        halves = jnp.split(biases[0], gn, axis=1)
        b_in = [jnp.concatenate([part[4:].reshape(-1) for part in halves])]
    else:
        b_in = [part[4:].reshape(-1) for part in biases]
    b_proj = [part[:4] for part in biases]
    slices = fetch_slices((feed_in, feed_out))
    w_self = spread(after(self_inputs, token_all, biases[-1], slices[-1][0]), 2)
    w_in, w_out = spread_wide((feed_in, feed_out), slices)
    self_q, self_k, self_v, self_mixed, self_lse = [], [], [], [], []
    shards = range(len(w_self))
    for s in shards:
        self_q.append((_nn(token_all, w_self[s][0]) + b_proj[s][0]).astype(LOW))
        self_k.append(_nn(token_all, w_self[s][1]).astype(LOW))
        self_v.append((_nn(token_all, w_self[s][2]) + b_proj[s][1]).astype(LOW))
        mixed, lse = attn_fwd(target_length, self_q[s], self_k[s], self_v[s], True)
        self_mixed.append(mixed)
        self_lse.append(lse)
    first = self_mixed[0]
    w_self_out = spread(after(self_output, self_q[0]), 0)
    memory_all = gather_rows(after(memory, first))
    w_cross_mem = spread(after(cross_memory, first), 2)
    w_cross_q = spread(after(cross_query, first), 1)
    w_cross_out = spread(after(cross_output, first), 0)
    cot_all = gather_rows(after(cotangent, self_mixed[-1]))

    cross_k = [_nn(memory_all, w_cross_mem[s][0]).astype(LOW) for s in shards]
    cross_v = [(_nn(memory_all, w_cross_mem[s][1]) + b_proj[s][3]).astype(LOW) for s in shards]
    branch_one = sum_all(sum(_nn(self_mixed[s], w_self_out[s]) for s in shards)) + branch_bias[0]
    normed_one, unit_one, inverse_one = norm_forward(residual_scale * token_all.astype(F32) + branch_one, norm_gain[0], norm_shift[0])
    second = after(normed_one.astype(LOW), w_in[-1], w_out[-1])
    cross_q = [(_nn(second, w_cross_q[s]) + b_proj[s][2]).astype(LOW) for s in shards]
    cross_mixed, cross_lse = zip(*[attn_fwd(memory_length, cross_q[s], cross_k[s], cross_v[s], False) for s in shards])
    branch_two = sum_all(sum(_nn(cross_mixed[s], w_cross_out[s]) for s in shards)) + branch_bias[1]
    normed_two, unit_two, inverse_two = norm_forward(residual_scale * normed_one + branch_two, norm_gain[1], norm_shift[1])
    third = normed_two.astype(LOW)
    feed_part, hidden, slope = feed_forward(third, w_in, [b_in[s].reshape(1, -1) for s in shards], w_out)
    branch_three = sum_all(feed_part) + branch_bias[2]
    normed_three, unit_three, inverse_three = norm_forward(residual_scale * normed_two + branch_three, norm_gain[2], norm_shift[2])
    block_out = own_rows(normed_three.astype(LOW))

    cot = cot_all.astype(F32)
    grad_three = norm_backward(cot, unit_three, inverse_three, norm_gain[2])
    low_three = grad_three.astype(LOW)
    grad_hidden = [_nt(low_three, w_out[s]) for s in shards]
    feed_out_parts = parts_of([tn(hidden[s], low_three) for s in shards], 0)
    grad_pre = [(grad_hidden[s] * slope[s].astype(F32)).astype(LOW) for s in shards]
    feed_in_parts = parts_of([tn(third, grad_pre[s]) for s in shards], 1)
    grad_normed_two = residual_scale * grad_three + sum_all(sum(_nt(grad_pre[s], w_in[s]) for s in shards))
    grad_two = norm_backward(grad_normed_two, unit_two, inverse_two, norm_gain[1])
    low_two = grad_two.astype(LOW)

    def sums(rows):
        return jnp.sum(rows.astype(F32), axis=0)

    def low_pairs(*parts):
        return [(part[0].astype(LOW), part[1].astype(LOW)) for part in parts]

    in_kernel = (zn, yn, gn, cn, width, joined) == (4, 2, 2, 2, SPAN, False)
    if in_kernel:
        per_shard = [(cross_q[s], cross_k[s], cross_v[s], cross_mixed[s], cross_lse[s]) for s in shards]
        row_part, memory_part, cross_sums, go_own, go_other, gq_own, gq_other, gm_own, gm_other, feed_out_sum, feed_in_sum = cross_back(
            memory_length, low_two, per_shard[0], per_shard[1], w_cross_out, second, memory_all, w_cross_q, w_cross_mem, low_pairs(feed_out_parts, feed_in_parts))
        cross_sums = [cross_sums[0, :2], cross_sums[1, :2]]
        grad_memory = memory_part
        grad_normed_one = residual_scale * grad_two + row_part.astype(F32)
    else:
        feed_out_sum, feed_in_sum = [sum_groups(send_home(part)) for part in (feed_out_parts, feed_in_parts)]
        grad_cross_mixed = [_nt(low_two, w_cross_out[s]).astype(LOW) for s in shards]
        cross_out_parts = parts_of([tn(cross_mixed[s], low_two) for s in shards], 0)
        cross_dq, cross_dk, cross_dv = zip(*[attn_bwd(memory_length, cross_q[s], cross_k[s], cross_v[s], cross_mixed[s], grad_cross_mixed[s], cross_lse[s], False) for s in shards])
        grad_normed_one = residual_scale * grad_two + sum_all(sum(_nt(cross_dq[s], w_cross_q[s]) for s in shards))
        cross_parts = [parts_of([tn(rows, grads[s]) for s in shards], 1) for rows, grads in ((second, cross_dq), (memory_all, cross_dk), (memory_all, cross_dv))]
        grad_memory = sum_own(sum(_nt(cross_dk[s], w_cross_mem[s][0]) + _nt(cross_dv[s], w_cross_mem[s][1]) for s in shards)).astype(LOW)
        cross_sums = parts_of([jnp.stack([sums(cross_dq[s]), sums(cross_dv[s])]) for s in shards], 1)
    grad_one = norm_backward(grad_normed_one, unit_one, inverse_one, norm_gain[0])
    low_one = grad_one.astype(LOW)

    model = tokens.shape[1]
    terms = jnp.stack([sums(low_one), sums(low_two), sums(low_three), sums(grad_normed_one * unit_one), sums(grad_normed_two * unit_two), sums(cot * unit_three), sums(grad_normed_one), sums(grad_normed_two), sums(cot)])
    feed_sums = parts_of([sums(grad_pre[s]) for s in shards], 0)
    if not in_kernel:
        grad_self_mixed = [_nt(low_one, w_self_out[s]).astype(LOW) for s in shards]
        self_out_parts = parts_of([tn(self_mixed[s], low_one) for s in shards], 0)
        self_dq, self_dk, self_dv = zip(*[attn_bwd(target_length, self_q[s], self_k[s], self_v[s], self_mixed[s], grad_self_mixed[s], self_lse[s], True) for s in shards])
        token_part = sum_own(sum(_nt(self_dq[s], w_self[s][0]) + _nt(self_dk[s], w_self[s][1]) + _nt(self_dv[s], w_self[s][2]) for s in shards))
        self_sums = parts_of([jnp.stack([sums(self_dq[s]), sums(self_dv[s])]) for s in shards], 1)
    else:
        self_sums = [jnp.zeros((2, width), F32)] * gn
    smalls = []
    for k in range(gn):
        small = lax.dynamic_slice_in_dim(terms, ((seq + k) % gn * cn + core) * width, width, 1)
        small = jnp.concatenate([small, self_sums[k], cross_sums[k], feed_sums[k].reshape(-1, width)])
        smalls.append(jnp.pad(small, ((0, 16 * zn * yn - small.shape[0]), (0, 0))))
    if in_kernel:
        per_shard = [(self_q[s], self_k[s], self_v[s], self_mixed[s], self_lse[s]) for s in shards]
        pairs = [(go_own, go_other), (gq_own, gq_other), (gm_own, gm_other)]
        token_part, *sums_low = self_back(target_length, low_one, per_shard[0], per_shard[1], w_self_out, token_all, w_self, smalls, pairs)
    else:
        groups = [[cross_out_parts], cross_parts[:1], cross_parts[1:], [self_out_parts], [parts_of([tn(token_all, grads[s]) for s in shards], 1) for grads in (self_dq, self_dk, self_dv)], [smalls]]
        sums_low = [sum_groups(send_home([jnp.concatenate([part[k] for part in group]) for k in range(gn)])) for group in groups]
    cross_out_sum, cross_q_sum, cross_mem_sum, self_out_sum, self_in_sum, small = [rows.astype(F32) for rows in sums_low]
    feed_out_sum, feed_in_sum = feed_out_sum.astype(F32), feed_in_sum.astype(F32)
    grad_tokens = (residual_scale * own_rows(grad_one) + token_part).astype(LOW)
    return (block_out, grad_tokens, grad_memory, self_in_sum.reshape(3, model, width), self_out_sum, cross_q_sum, cross_mem_sum.reshape(2, model, width), cross_out_sum, feed_in_sum, feed_out_sum, small[9:13], small[13:13 + feed_rows].reshape(-1), small[0:3], small[3:6], small[6:9])


def solution(mesh):
    dp, mp = mesh.shape["dp"], mesh.shape["mp"]

    def whole(*args):
        yn = 2 if dp % 2 == 0 else 1
        gn = args[3].shape[0] // dp
        sizes = (dp // yn, yn, gn, mp // gn)
        fine = Mesh(mesh.devices.reshape(sizes), ("z", "y", "g", "c"))
        d, m = ("z", "y"), ("g", "c")
        rows, wide, tall = P(d + m, None), P(None, m), P(m, None)
        stack = P(None, None, m)
        in_specs = (rows, rows, rows, P(d), P(d), stack, tall, wide, stack, tall, wide, tall, wide, P(m), P(), P(), P())
        out_specs = (rows, rows, rows, stack, tall, wide, stack, tall, wide, tall, wide, P(m), wide, wide, wide)
        return jax.shard_map(functools.partial(layer, sizes), mesh=fine, in_specs=in_specs, out_specs=out_specs, check_vma=False)(*args)

    return whole
```

```python
import functools
import math

import jax, jax.numpy as jnp
from jax import lax
from jax.experimental import pallas as pl
from jax.experimental.pallas import tpu as pltpu
from jax.sharding import Mesh
from jax.sharding import PartitionSpec as P

HEAD = 64
NEG = -1e30

def _nt(a, b):
    return lax.dot_general(a, b, (((1,), (1,)), ((), ())), preferred_element_type=jnp.float32)

def _nn(a, b):
    return lax.dot_general(a, b, (((1,), (0,)), ((), ())), preferred_element_type=jnp.float32)

def _lanes(rows):
    return lax.broadcasted_iota(jnp.int32, (rows, 128), 1)

def _put(base, lane, pairs):
    for at, val in pairs:
        base = jnp.where(lane == at, val, base)
    return base

def fwd_kernel(len_ref, q_ref, k_ref, v_ref, o_ref, lse_ref, *, causal, bq):
    p = pl.program_id(0)
    rows, keys = q_ref.shape[0], k_ref.shape[0]
    length = len_ref[0]
    kl = _lanes(keys)
    kpos = lax.broadcasted_iota(jnp.int32, (keys, 128), 0)
    kbias = jnp.where(kpos < length, 0.0, NEG)
    k2 = k_ref[...].astype(jnp.float32)
    v2 = v_ref[...].astype(jnp.float32)
    ql = _lanes(bq)
    heads = []
    for h in range(2):
        mine = (kl // HEAD) == h
        other = HEAD * (1 - h)
        kh = jnp.where(mine, k2, jnp.where(kl == other, kbias, 0.0)).astype(jnp.bfloat16)
        vh = jnp.where(mine, v2, jnp.where(kl == other, 1.0, 0.0)).astype(jnp.bfloat16)
        heads.append((kh, vh))
    for i in range(rows // bq):
        q2 = q_ref[pl.ds(i * bq, bq), :].astype(jnp.float32) * (HEAD ** -0.5)
        out = jnp.zeros((bq, 128), jnp.float32)
        lse_all = lse_ref[pl.ds(i * bq, bq), :]
        for h in range(2):
            kh, vh = heads[h]
            mine = (ql // HEAD) == h
            other = HEAD * (1 - h)
            qh = jnp.where(mine, q2, jnp.where(ql == other, 1.0, 0.0)).astype(jnp.bfloat16)
            if causal:
                lo = i * bq
                sd = _nt(qh, kh[lo:lo + bq])
                r = lax.broadcasted_iota(jnp.int32, (bq, bq), 0)
                c = lax.broadcasted_iota(jnp.int32, (bq, bq), 1)
                sd = jnp.where(c <= r, sd, NEG)
                m = jnp.max(sd, axis=1, keepdims=True)
                if lo:
                    sl = _nt(qh, kh[:lo])
                    m = jnp.maximum(m, jnp.max(sl, axis=1, keepdims=True))
                    acc = _nn(jnp.exp(sl - m).astype(jnp.bfloat16), vh[:lo])
                    acc += _nn(jnp.exp(sd - m).astype(jnp.bfloat16), vh[lo:lo + bq])
                else:
                    acc = _nn(jnp.exp(sd - m).astype(jnp.bfloat16), vh[:bq])
            else:
                s = _nt(qh, kh)
                m = jnp.max(s, axis=1, keepdims=True)
                acc = _nn(jnp.exp(s - m).astype(jnp.bfloat16), vh)
            total = jnp.sum(jnp.where(ql == other, acc, 0.0), axis=1, keepdims=True)
            out = jnp.where(mine, acc / total, out)
            lse_all = jnp.where(ql == 2 * p + h, m + jnp.log(total), lse_all)
        o_ref[pl.ds(i * bq, bq), :] = out.astype(jnp.bfloat16)
        lse_ref[pl.ds(i * bq, bq), :] = lse_all

def attn_fwd(length, q, k, v, causal, bq=256):
    rows, cols = q.shape
    keys = k.shape[0]
    pairs = cols // 128
    el = pairs * 2 * rows * keys
    return pl.pallas_call(
        functools.partial(fwd_kernel, causal=causal, bq=bq),
        out_shape=(jax.ShapeDtypeStruct((rows, cols), jnp.bfloat16), jax.ShapeDtypeStruct((rows, 128), jnp.float32)),
        grid_spec=pltpu.PrefetchScalarGridSpec(
            num_scalar_prefetch=1, grid=(pairs,),
            in_specs=[pl.BlockSpec((rows, 128), lambda p, n: (0, p)), pl.BlockSpec((keys, 128), lambda p, n: (0, p)), pl.BlockSpec((keys, 128), lambda p, n: (0, p))],
            out_specs=[pl.BlockSpec((rows, 128), lambda p, n: (0, p)), pl.BlockSpec((rows, 128), lambda p, n: (0, 0))],
        ),
        compiler_params=pltpu.CompilerParams(dimension_semantics=("arbitrary",), vmem_limit_bytes=40 << 20),
        cost_estimate=pl.CostEstimate(flops=16 * el * 64, bytes_accessed=8 * rows * cols, transcendentals=el),
        name="attend_forward",
    )(length, q, k, v)

def split3(x):
    a = x.astype(jnp.bfloat16).astype(jnp.float32)
    b = (x - a).astype(jnp.bfloat16).astype(jnp.float32)
    return a, b, x - a - b


def key_side(k2, v2, length):
    keys = k2.shape[0]
    kl = _lanes(keys)
    kbias = jnp.where(lax.broadcasted_iota(jnp.int32, (keys, 128), 0) < length, 0.0, NEG)
    k2, v2 = k2.astype(jnp.float32), v2.astype(jnp.float32)
    heads = []
    for h in range(2):
        mine = (kl // HEAD) == h
        other = HEAD * (1 - h)
        ones = (kl > other) & (kl < other + 4)
        kh = jnp.where(mine, k2, jnp.where(kl == other, kbias, jnp.where(ones, 1.0, 0.0))).astype(jnp.bfloat16)
        vh = jnp.where(mine, v2, jnp.where(ones, 1.0, 0.0)).astype(jnp.bfloat16)
        heads.append((kh, vh, kh.T))
    return heads


def query_block(heads, q2, o2, g2, lse_all, pair, i, last, causal, dka, dva):
    bq = q2.shape[0]
    keys = heads[0][0].shape[0]
    ql = _lanes(bq)
    q2 = q2.astype(jnp.float32) * (HEAD ** -0.5)
    g2 = g2.astype(jnp.float32)
    go = g2 * o2.astype(jnp.float32)
    dqt = []
    for h in range(2):
        kh, vh, kt = heads[h]
        mine = (ql // HEAD) == h
        other = HEAD * (1 - h)
        lse = jnp.sum(jnp.where(ql == 2 * pair + h, lse_all, 0.0), axis=1, keepdims=True)
        delta = jnp.sum(jnp.where(mine, go, 0.0), axis=1, keepdims=True)
        la, lb, lc = split3(-lse)
        da, db, dc = split3(-delta)
        qh = _put(jnp.where(mine, q2, 0.0), ql, ((other, 1.0), (other + 1, la), (other + 2, lb), (other + 3, lc))).astype(jnp.bfloat16)
        gh = _put(jnp.where(mine, g2, 0.0), ql, ((other + 1, da), (other + 2, db), (other + 3, dc))).astype(jnp.bfloat16)
        hi = (i + 1) * bq if causal else keys
        st = _nt(kh[:hi], qh)
        if causal:
            kr = lax.broadcasted_iota(jnp.int32, (hi, bq), 0)
            qc = lax.broadcasted_iota(jnp.int32, (hi, bq), 1) + i * bq
            pt = jnp.where(kr <= qc, jnp.exp(st), 0.0)
        else:
            pt = jnp.exp(st)
        dst = (pt * _nt(vh[:hi], gh)).astype(jnp.bfloat16)
        dvn = _nn(pt.astype(jnp.bfloat16), gh)
        dkn = _nn(dst, qh)
        if last:
            dva[h, :hi] = dvn
            dka[h, :hi] = dkn
        else:
            dva[h, :hi] += dvn
            dka[h, :hi] += dkn
        dqt.append(_nn(kt[:, :hi], dst))
    dq = jnp.concatenate([dqt[0][:HEAD], dqt[1][HEAD:]], axis=0).T
    return (dq * (HEAD ** -0.5)).astype(jnp.bfloat16)


def bwd_kernel(len_ref, q_ref, k_ref, v_ref, o_ref, g_ref, lse_ref, dq_ref, dk_ref, dv_ref, dka, dva, *, causal, bq):
    rows, keys = q_ref.shape[0], k_ref.shape[0]
    heads = key_side(k_ref[...], v_ref[...], len_ref[0])
    blocks = rows // bq
    for i in reversed(range(blocks)):
        at = pl.ds(i * bq, bq)
        dq_ref[at, :] = query_block(heads, q_ref[at, :], o_ref[at, :], g_ref[at, :], lse_ref[at, :], pl.program_id(0), i, i == blocks - 1, causal, dka, dva)
    first = _lanes(keys) < HEAD
    dk_ref[...] = jnp.where(first, dka[0], dka[1]).astype(jnp.bfloat16)
    dv_ref[...] = jnp.where(first, dva[0], dva[1]).astype(jnp.bfloat16)

def attn_bwd(length, q, k, v, o, g, lse, causal, bq=256):
    rows, cols = q.shape
    keys = k.shape[0]
    pairs = cols // 128
    el = pairs * 2 * rows * keys
    qs = pl.BlockSpec((rows, 128), lambda p, n: (0, p))
    ks = pl.BlockSpec((keys, 128), lambda p, n: (0, p))
    return pl.pallas_call(
        functools.partial(bwd_kernel, causal=causal, bq=bq),
        out_shape=(jax.ShapeDtypeStruct((rows, cols), jnp.bfloat16), jax.ShapeDtypeStruct((keys, cols), jnp.bfloat16), jax.ShapeDtypeStruct((keys, cols), jnp.bfloat16)),
        grid_spec=pltpu.PrefetchScalarGridSpec(
            num_scalar_prefetch=1, grid=(pairs,),
            in_specs=[qs, ks, ks, qs, qs, pl.BlockSpec((rows, 128), lambda p, n: (0, 0))],
            out_specs=[qs, ks, ks],
            scratch_shapes=[pltpu.VMEM((2, keys, 128), jnp.float32), pltpu.VMEM((2, keys, 128), jnp.float32)],
        ),
        compiler_params=pltpu.CompilerParams(dimension_semantics=("arbitrary",), vmem_limit_bytes=48 << 20),
        cost_estimate=pl.CostEstimate(flops=40 * el * 64, bytes_accessed=16 * rows * cols, transcendentals=el),
        name="attend_backward",
    )(length, q, k, v, o, g, lse)

CHUNK = 512
LAG = 1
SPAN = 256


class Pipeline:
    AHEAD = 3

    def __init__(self, total, scratch):
        self.spots, self.total, self.step, self.sent, self.loaded = [], total, 0, 0, 0
        (self.held, self.ysum, self.zgot, self.mine, self.load, self.store, self.xs, self.xr, self.ys, self.yr, self.zs, self.zr, self.bs, self.br, self.es, self.er) = scratch
        self.full = self.held
        self.seq, self.ya, za = lax.axis_index("g"), lax.axis_index("y"), lax.axis_index("z")
        self.za = za
        self.peers = {1: za + 1 - 2 * (za % 2), 2: (za + 2) % 4, 3: 3 - za}
        self.stages = (self.to_y, self.to_z, self.back_z, self.back_y, self.finish)

    @staticmethod
    def scratch(total, most):
        dma = pltpu.SemaphoreType.DMA
        return [
            pltpu.VMEM((total, most, SPAN), LOW),
            pltpu.VMEM((total, most // 2, SPAN), LOW),
            pltpu.VMEM((total, 3, most // 8, SPAN), LOW),
            pltpu.VMEM((4, most, SPAN), LOW),
            dma((4,)), dma((total,)),
            dma((total,)), dma((total,)), dma((total,)), dma((total,)),
            dma((total, 3)), dma((total, 3)), dma((total, 3)), dma((total, 3)),
            dma((total,)), dma((total,)),
        ]

    def greet(self, more=()):
        barrier = pltpu.get_barrier_semaphore()
        everyone = [{"g": 1 - self.seq}, {"y": 1 - self.ya}] + [{"z": self.peers[d]} for d in (1, 2, 3)] + list(more)
        for where in everyone:
            pl.semaphore_signal(barrier, inc=1, device_id=where, device_id_type=pl.DeviceIdType.MESH)
        pl.semaphore_wait(barrier, len(everyone))

    def add(self, own, other, out, taper=False, first=0, count=None):
        for r, size, c in cut(own.shape[0] if count is None else count, own.shape[1], taper):
            self.spots.append((own, other, first + r, c, size, out, first + r))
        self.feed()

    def feed(self):
        while self.sent < min(len(self.spots), self.step + self.AHEAD):
            self.x_copy(self.sent).start()
            self.own_copy(self.sent).start()
            self.sent += 1

    def tick(self, times=1):
        for unused in range(times):
            if self.step >= self.total + LAG * (len(self.stages) - 1) or len(self.spots) <= self.step < self.total:
                return
            for at, stage in enumerate(self.stages):
                if 0 <= self.step - LAG * at < self.total:
                    stage(self.step - LAG * at)
            self.step += 1
            self.feed()

    def drain(self):
        assert len(self.spots) == self.total
        self.tick(self.total + LAG * len(self.stages))
        for k in range(self.total):
            self.x_copy(k).wait_send()
            self.yb_copy(k).wait_send()
            self.out_copy(k).wait()
            for d in (1, 2, 3):
                self.z_copy(k, d).wait_send()
                self.zb_copy(k, d).wait_send()

    @staticmethod
    def remote(src, dst, send, recv, where):
        return pltpu.make_async_remote_copy(src_ref=src, dst_ref=dst, send_sem=send, recv_sem=recv, device_id=where, device_id_type=pl.DeviceIdType.MESH)

    @staticmethod
    def block(at, size):
        return pl.ds(pl.multiple_of(at * size, size), size)

    def x_copy(self, k):
        own, other, r, c, n, o, q = self.spots[k]
        return self.remote(other.at[pl.ds(r, n), pl.ds(c, SPAN)], self.held.at[k, pl.ds(0, n)], self.xs.at[k], self.xr.at[k], {"g": 1 - self.seq})

    def own_copy(self, k):
        own, other, r, c, n, o, q = self.spots[k]
        return pltpu.make_async_copy(own.at[pl.ds(r, n), pl.ds(c, SPAN)], self.mine.at[k % 4, pl.ds(0, n)], self.load.at[k % 4])

    def y_copy(self, k):
        h = self.spots[k][4] // 2
        return self.remote(self.held.at[k, self.block(1 - self.ya, h)], self.ysum.at[k, pl.ds(0, h)], self.ys.at[k], self.yr.at[k], {"y": 1 - self.ya})

    def z_copy(self, k, d):
        p = self.spots[k][4] // 8
        return self.remote(self.ysum.at[k, self.block(self.peers[d], p)], self.zgot.at[k, d - 1, pl.ds(0, p)], self.zs.at[k, d - 1], self.zr.at[k, d - 1], {"z": self.peers[d]})

    def zb_copy(self, k, d):
        rows = self.full.at[k, self.block(self.ya * 4 + self.za, self.spots[k][4] // 8)]
        return self.remote(rows, rows, self.bs.at[k, d - 1], self.br.at[k, d - 1], {"z": self.peers[d]})

    def yb_copy(self, k):
        rows = self.full.at[k, self.block(self.ya, self.spots[k][4] // 2)]
        return self.remote(rows, rows, self.es.at[k], self.er.at[k], {"y": 1 - self.ya})

    def out_copy(self, k):
        own, other, r, c, n, o, q = self.spots[k]
        return pltpu.make_async_copy(self.full.at[k, pl.ds(0, n)], o.at[pl.ds(q, n), pl.ds(c, SPAN)], self.store.at[k])

    def to_y(self, k):
        n = self.spots[k][4]
        self.own_copy(k).wait()
        self.x_copy(k).wait_recv()
        self.held[k, :n] = self.held[k, :n] + self.mine[k % 4, :n]
        self.y_copy(k).start()

    def to_z(self, k):
        h = self.spots[k][4] // 2
        self.y_copy(k).wait()
        self.ysum[k, :h] = self.ysum[k, :h] + self.held[k, self.block(self.ya, h)]
        for d in (1, 2, 3):
            self.z_copy(k, d).start()

    def back_z(self, k):
        p = self.spots[k][4] // 8
        for d in (1, 2, 3):
            self.z_copy(k, d).wait_recv()
        rows = self.ysum[k, self.block(self.za, p)].astype(F32)
        for d in (1, 2, 3):
            rows = rows + self.zgot[k, d - 1, :p].astype(F32)
        self.full[k, self.block(self.ya * 4 + self.za, p)] = rows.astype(LOW)
        for d in (1, 2, 3):
            self.zb_copy(k, d).start()

    def back_y(self, k):
        for d in (1, 2, 3):
            self.zb_copy(k, d).wait_recv()
        self.yb_copy(k).start()

    def finish(self, k):
        self.yb_copy(k).wait_recv()
        self.out_copy(k).start()


def cut(rows, cols, taper=False):
    size = min(CHUNK, rows)
    chunks = [(r, size, c) for r in range(0, rows, size) for c in range(0, cols, SPAN)]
    if taper:
        r, unused, c = chunks.pop()
        chunks += [(r, size // 2, c), (r + size // 2, size // 4, c), (r + size - size // 4, size // 4, c)]
    return chunks


def spot_count(shapes, taper=()):
    return sum(len(cut(rows, cols, at in taper)) for at, (rows, cols) in enumerate(shapes))


def attend_back(pipe, shards, length, low, gm, dq, dk, dv, dka, dva, causal, bq, every):
    rows = low.shape[0]
    blocks = rows // bq
    for s, (q, k, v, o, l, wo) in enumerate(shards):
        for i in range(blocks):
            at = pl.ds(i * bq, bq)
            gm[s, at, :] = _nt(low[at, :], wo[...]).astype(LOW)
    for s, (q, k, v, o, l, wo) in enumerate(shards):
        for p in range(q.shape[1] // 128):
            cols = pl.ds(p * 128, 128)
            heads = key_side(k[:, cols], v[:, cols], length)
            for i in reversed(range(blocks)):
                at = pl.ds(i * bq, bq)
                dq[s, at, cols] = query_block(heads, q[at, cols], o[at, cols], gm[s, at, cols], l[at, :], p, i, i == blocks - 1, causal, dka, dva)
                if i % every == 0:
                    pipe.tick()
            first = _lanes(k.shape[0]) < HEAD
            dk[s, :, cols] = jnp.where(first, dka[0], dka[1]).astype(LOW)
            dv[s, :, cols] = jnp.where(first, dva[0], dva[1]).astype(LOW)


def back_rows(terms, start, size):
    at = pl.ds(pl.multiple_of(start, size), size)
    both = None
    for grads, s, weight in terms:
        term = _nt(grads[s, at, :], weight)
        both = term if both is None else both + term
    return both


def output_grads(shards, low, outs):
    for (q, k, v, o, l, wo), out in zip(shards, outs):
        for c in range(0, low.shape[1], SPAN):
            out[:, c : c + SPAN] = tn(o[...], low[:, c : c + SPAN]).astype(LOW)


def input_grads(rows_in, grads, out, first, bq):
    for i in range(0, rows_in.shape[1], bq):
        out[pl.ds(first + i, bq), :] = tn(rows_in[:, i : i + bq], grads).astype(LOW)


def share_rows(terms, core, part, got, sems, out, bq, pipe):
    half = out.shape[0]
    copy = Pipeline.remote(part, got, sems[0], sems[1], {"c": 1 - core})
    for i in range(0, half, bq):
        part[pl.ds(i, bq), :] = back_rows(terms, (1 - core) * half + i, bq).astype(LOW)
    copy.start()
    pipe.tick()
    mine = [back_rows(terms, core * half + i, bq) for i in range(0, half, bq)]
    pipe.tick()
    copy.wait()
    for i in range(0, half, bq):
        out[pl.ds(i, bq), :] = (mine[i // bq] + got[pl.ds(i, bq), :].astype(F32)).astype(out.dtype)


def self_back_kernel(carried, bq, len_ref, low, q0, k0, v0, o0, l0, q1, k1, v1, o1, l1, wo0, wo1, x_in, w0, w1, small0, small1, *rest):
    own, other, rest = rest[:carried], rest[carried : 2 * carried], rest[2 * carried :]
    token_out, rest = rest[0], rest[1:]
    outs, rest = rest[: carried + 3], rest[carried + 3 :]
    gm, dq, dk, dv, dka, dva, go_own, go_other, gi_own, gi_other, sm_own, sm_other, part, got, part_send, part_recv = rest[:16]
    core = lax.axis_index("c")
    total = spot_count([ref.shape for ref in own] + [go_own.shape, sm_own.shape] + [(low.shape[1], gi_own.shape[1])] * 3, (carried + 4,))
    pipe = Pipeline(total, rest[16:])
    pipe.greet([{"c": 1 - core}])
    for a, b, out in zip(own, other, outs):
        pipe.add(a, b, out)
    shards = ((q0, k0, v0, o0, l0, wo0), (q1, k1, v1, o1, l1, wo1))
    output_grads(shards, low, (go_own, go_other))
    pipe.add(go_own, go_other, outs[carried])
    attend_back(pipe, shards, len_ref[0], low, gm, dq, dk, dv, dka, dva, True, bq, 2)
    for s, (sm, small) in enumerate(((sm_own, small0), (sm_other, small1))):
        row = lax.broadcasted_iota(jnp.int32, sm.shape, 0)
        sums = [jnp.sum(grads[s].astype(F32), axis=0, keepdims=True) for grads in (dq, dv)]
        sm[...] = jnp.where(row == 9, sums[0], jnp.where(row == 10, sums[1], small[...])).astype(LOW)
    pipe.add(sm_own, sm_other, outs[carried + 2])
    model = x_in.shape[1]
    for m, grads in enumerate((dq, dk, dv)):
        for s, gi in enumerate((gi_own, gi_other)):
            input_grads(x_in, grads[s], gi, m * model, bq)
            pipe.tick()
        pipe.add(gi_own, gi_other, outs[carried + 1], m == 2, m * model, model)
    terms = [(grads, s, w[m]) for s, w in ((0, w0), (1, w1)) for m, grads in enumerate((dq, dk, dv))]
    share_rows(terms, core, part, got, (part_send, part_recv), token_out, bq, pipe)
    pipe.drain()


def cross_back_kernel(carried, bq, len_ref, low, q0, k0, v0, o0, l0, q1, k1, v1, o1, l1, wo0, wo1, x_in, m_in, wq0, wq1, wm0, wm1, *rest):
    own, other, rest = rest[:carried], rest[carried : 2 * carried], rest[2 * carried :]
    row_out, memory_out, sums_out, go_own, go_other, gq_own, gq_other, gm_own, gm_other = rest[:9]
    outs, rest = rest[9 : 9 + carried], rest[9 + carried :]
    gm, dq, dk, dv, dka, dva, part, got, part_send, part_recv, full_part, full_got, full_send, full_recv = rest[:14]
    core = lax.axis_index("c")
    pipe = Pipeline(spot_count([ref.shape for ref in own], (carried - 1,)), rest[14:])
    pipe.greet([{"c": 1 - core}])
    for at, (a, b, out) in enumerate(zip(own, other, outs)):
        pipe.add(a, b, out, at == carried - 1)
    shards = ((q0, k0, v0, o0, l0, wo0), (q1, k1, v1, o1, l1, wo1))
    attend_back(pipe, shards, len_ref[0], low, gm, dq, dk, dv, dka, dva, False, bq, 1)
    rows = low.shape[0]
    terms = [(dq, 0, wq0[...]), (dq, 1, wq1[...])]
    for i in range(0, rows, bq):
        full_part[pl.ds(i, bq), :] = back_rows(terms, i, bq).astype(LOW)
        if i % (2 * bq):
            pipe.tick()
    exchange = Pipeline.remote(full_part, full_got, full_send, full_recv, {"c": 1 - core})
    exchange.start()
    pipe.tick()
    terms = [(grads, s, w[m]) for s, w in ((0, wm0), (1, wm1)) for m, grads in enumerate((dk, dv))]
    share_rows(terms, core, part, got, (part_send, part_recv), memory_out, bq, pipe)
    output_grads(shards, low, (go_own, go_other))
    pipe.tick()
    for s, (gq, gkv) in enumerate(((gq_own, gm_own), (gq_other, gm_other))):
        input_grads(x_in, dq[s], gq, 0, bq)
        pipe.tick()
        input_grads(m_in, dk[s], gkv, 0, bq)
        pipe.tick()
        input_grads(m_in, dv[s], gkv, m_in.shape[1], bq)
        sums_out[s, 0:1] = jnp.sum(dq[s].astype(F32), axis=0, keepdims=True)
        sums_out[s, 1:2] = jnp.sum(dv[s].astype(F32), axis=0, keepdims=True)
        pipe.tick()
    exchange.wait()
    for i in range(0, rows, bq):
        at = pl.ds(i, bq)
        row_out[at, :] = (full_part[at, :].astype(F32) + full_got[at, :].astype(F32)).astype(LOW)
    pipe.drain()


def low_ram(*shape):
    return pltpu.VMEM(shape, LOW)


def back_scratch(rows, width):
    return [low_ram(2, rows, width) for unused in range(4)] + [pltpu.VMEM((2, rows, 128), F32), pltpu.VMEM((2, rows, 128), F32)]


def self_back(length, low, first, second, wo, x_in, w, smalls, pairs, bq=256):
    rows, model = low.shape
    width = wo[0].shape[0]
    carried = len(pairs)
    any_space = pl.BlockSpec(memory_space=pl.ANY)
    vmem = pl.BlockSpec(memory_space=pltpu.VMEM)
    dma = pltpu.SemaphoreType.DMA
    ends = [(width, model), (3 * rows, width), smalls[0].shape]
    total = spot_count([own.shape for own, unused in pairs] + [ends[0], ends[2]] + [(model, width)] * 3, (carried + 4,))
    return pl.pallas_call(
        functools.partial(self_back_kernel, carried, bq),
        out_shape=[jax.ShapeDtypeStruct((rows // 2, model), F32)] + [jax.ShapeDtypeStruct(own.shape, LOW) for own, unused in pairs] + [jax.ShapeDtypeStruct(shape, LOW) for shape in ends],
        in_specs=[pl.BlockSpec(memory_space=pltpu.SMEM)] + [vmem] * 18 + [any_space] * (2 * carried),
        out_specs=[vmem] + [any_space] * (carried + 3),
        scratch_shapes=back_scratch(rows, width)
        + [low_ram(width, model), low_ram(width, model), low_ram(3 * rows, width), low_ram(3 * rows, width), low_ram(*smalls[0].shape), low_ram(*smalls[0].shape)]
        + [low_ram(rows // 2, model), low_ram(rows // 2, model), dma, dma]
        + Pipeline.scratch(total, CHUNK),
        compiler_params=pltpu.CompilerParams(collective_id=0, has_side_effects=True, vmem_limit_bytes=58 << 20),
        cost_estimate=pl.CostEstimate(flops=20 * rows * model * width, bytes_accessed=300 << 20, transcendentals=8 * rows * rows),
        name="self_backward",
    )(length, low, *first, *second, *wo, x_in, *w, *smalls, *[p[0] for p in pairs], *[p[1] for p in pairs])


def cross_back(length, low, first, second, wo, x_in, m_in, wq, wm, pairs, bq=256):
    rows, model = low.shape
    width = wo[0].shape[0]
    carried = len(pairs)
    any_space = pl.BlockSpec(memory_space=pl.ANY)
    vmem = pl.BlockSpec(memory_space=pltpu.VMEM)
    dma = pltpu.SemaphoreType.DMA
    total = spot_count([own.shape for own, unused in pairs], (carried - 1,))
    shape = jax.ShapeDtypeStruct
    return pl.pallas_call(
        functools.partial(cross_back_kernel, carried, bq),
        out_shape=[shape((rows, model), LOW), shape((rows // 2, model), LOW), shape((2, 8, width), F32)]
        + [shape((width, model), LOW)] * 2 + [shape((rows, width), LOW)] * 2 + [shape((2 * rows, width), LOW)] * 2
        + [shape(own.shape, LOW) for own, unused in pairs],
        in_specs=[pl.BlockSpec(memory_space=pltpu.SMEM)] + [vmem] * 19 + [any_space] * (2 * carried),
        out_specs=[vmem] * 9 + [any_space] * carried,
        scratch_shapes=back_scratch(rows, width)
        + [low_ram(rows // 2, model), low_ram(rows // 2, model), dma, dma]
        + [low_ram(rows, model), low_ram(rows, model), dma, dma]
        + Pipeline.scratch(total, CHUNK),
        compiler_params=pltpu.CompilerParams(collective_id=1, has_side_effects=True, vmem_limit_bytes=58 << 20),
        cost_estimate=pl.CostEstimate(flops=20 * rows * model * width, bytes_accessed=300 << 20, transcendentals=8 * rows * rows),
        name="cross_backward",
    )(length, low, *first, *second, *wo, x_in, m_in, *wq, *wm, *[p[0] for p in pairs], *[p[1] for p in pairs])


def feed_kernel(count, rows_in, *refs):
    w_in, b_in, w_out, part, hidden, slope = refs[:count], refs[count : 2 * count], refs[2 * count : 3 * count], refs[3 * count], refs[3 * count + 1 : 4 * count + 1], refs[4 * count + 1 :]
    branch = None
    for s in range(count):
        pre = _nn(rows_in[...], w_in[s][...]) + b_in[s][...].astype(F32)
        spread_to = 0.5 + 0.5 * lax.erf(pre * 0.5**0.5)
        hidden[s][...] = (pre * spread_to).astype(LOW)
        slope[s][...] = (spread_to + pre * (jnp.exp(-0.5 * pre * pre) * (2.0 * math.pi) ** -0.5)).astype(LOW)
        term = _nn(hidden[s][...], w_out[s][...])
        branch = term if branch is None else branch + term
    part[...] = branch.astype(LOW)


def feed_forward(rows_in, w_in, b_in, w_out, bq=256):
    count = len(w_in)
    rows, model = rows_in.shape
    units = w_in[0].shape[1]
    wide = pl.BlockSpec((bq, units), lambda i: (i, 0))
    block = pl.BlockSpec((bq, model), lambda i: (i, 0))
    held = lambda array: pl.BlockSpec(array.shape, lambda i: (0, 0))
    out = pl.pallas_call(
        functools.partial(feed_kernel, count),
        grid=(rows // bq,),
        out_shape=[jax.ShapeDtypeStruct((rows, model), LOW)] + [jax.ShapeDtypeStruct((rows, units), LOW)] * (2 * count),
        in_specs=[block] + [held(array) for array in (*w_in, *b_in, *w_out)],
        out_specs=[block] + [wide] * (2 * count),
        compiler_params=pltpu.CompilerParams(dimension_semantics=("arbitrary",), vmem_limit_bytes=50 << 20),
        cost_estimate=pl.CostEstimate(flops=4 * count * rows * model * units, bytes_accessed=16 << 20, transcendentals=2 * count * rows * units),
        name="feed_forward",
    )(rows_in, *w_in, *b_in, *w_out)
    return out[0], out[1 : 1 + count], out[1 + count :]


def feed_back_kernel(count, scale, core_ref, part, got, normed, cot_ref, vectors, *refs):
    slope, w_in, w_out, refs = refs[:count], refs[count : 2 * count], refs[2 * count : 3 * count], refs[3 * count :]
    out, low, grad, row_part, sums, refs = refs[0], refs[1], refs[2], refs[3], refs[4], refs[5:]
    pre_grads, pre_sums = refs[:count], refs[count:]
    step = pl.program_id(0)
    bias, gain, shift = vectors[0:1], vectors[1:2], vectors[2:3]
    summed = scale * normed[...] + (part[...].astype(F32) + got[...].astype(F32) + bias)
    rows, unit, inverse = norm_forward(summed, gain, shift)
    half = pl.num_programs(0) // 2

    @pl.when(step // half == core_ref[0])
    def mine():
        out[...] = rows.astype(LOW)

    cot = cot_ref[...].astype(F32)
    grads = norm_backward(cot, unit, inverse, gain)
    grad[...] = grads
    low_rows = grads.astype(LOW)
    low[...] = low_rows
    totals = [jnp.sum(v, axis=0, keepdims=True) for v in (low_rows.astype(F32), cot * unit, cot)]
    branch = None
    for s in range(count):
        pre = (_nt(low_rows, w_out[s][...]) * slope[s][...].astype(F32)).astype(LOW)
        pre_grads[s][...] = pre
        term = _nt(pre, w_in[s][...])
        branch = term if branch is None else branch + term
        totals.append(jnp.sum(pre.astype(F32), axis=0, keepdims=True))
    row_part[...] = branch.astype(LOW)

    @pl.when(step == 0)
    def clear():
        sums[...] = jnp.zeros_like(sums)
        for s in range(count):
            pre_sums[s][...] = jnp.zeros_like(pre_sums[s])

    for at in range(3):
        sums[at : at + 1] += totals[at]
    for s in range(count):
        pre_sums[s][...] += totals[3 + s]


def feed_backward(core, part, got, normed, cot, vectors, slope, w_in, w_out, bq=256):
    count = len(w_in)
    rows, model = part.shape
    units = w_in[0].shape[1]
    half = rows // bq // 2
    wide = pl.BlockSpec((bq, units), lambda i, c: (i, 0))
    block = pl.BlockSpec((bq, model), lambda i, c: (i, 0))
    held = lambda shape: pl.BlockSpec(shape, lambda i, c: (0, 0))
    shape = jax.ShapeDtypeStruct
    out = pl.pallas_call(
        functools.partial(feed_back_kernel, count, residual_scale),
        out_shape=[shape((rows // 2, model), LOW), shape((rows, model), LOW), shape((rows, model), F32), shape((rows, model), LOW), shape((8, model), F32)]
        + [shape((rows, units), LOW)] * count + [shape((1, units), F32)] * count,
        grid_spec=pltpu.PrefetchScalarGridSpec(
            num_scalar_prefetch=1,
            grid=(rows // bq,),
            in_specs=[block, block, block, block, held((3, model))] + [wide] * count + [held(array.shape) for array in (*w_in, *w_out)],
            out_specs=[pl.BlockSpec((bq, model), lambda i, c: (jnp.clip(i - half * c[0], 0, half - 1), 0)), block, block, block, held((8, model))] + [wide] * count + [held((1, units))] * count,
        ),
        compiler_params=pltpu.CompilerParams(dimension_semantics=("arbitrary",), vmem_limit_bytes=54 << 20),
        cost_estimate=pl.CostEstimate(flops=4 * count * rows * model * units, bytes_accessed=30 << 20, transcendentals=0),
        name="feed_backward",
    )(core, part, got, normed, cot, vectors, *slope, *w_in, *w_out)
    return out[0], out[1], out[2], out[3], out[4][:3], out[5 : 5 + count], out[5 + count :]


residual_scale = 300.0**0.25
norm_epsilon = 1e-05
LOW = jnp.bfloat16
F32 = jnp.float32


def tn(rows, grads):
    return lax.dot_general(rows, grads, (((0,), (0,)), ((), ())), preferred_element_type=F32)


def norm_forward(summed, gain_row, shift_row):
    row_mean = jnp.mean(summed, axis=-1, keepdims=True)
    centred = summed - row_mean
    variance = jnp.mean(centred * centred, axis=-1, keepdims=True)
    inverse = lax.rsqrt(variance + norm_epsilon)
    unit_rows = centred * inverse
    return unit_rows * gain_row + shift_row, unit_rows, inverse


def norm_backward(grad_out, unit_rows, inverse, gain_row):
    grad_unit = grad_out * gain_row
    first_mean = jnp.mean(grad_unit, axis=-1, keepdims=True)
    second_mean = jnp.mean(grad_unit * unit_rows, axis=-1, keepdims=True)
    return inverse * (grad_unit - first_mean - unit_rows * second_mean)


def layer(sizes, tokens, memory, cotangent, target_lengths, memory_lengths, self_inputs, self_output, cross_query, cross_memory, cross_output, feed_in, feed_out, proj_bias, feed_bias, branch_bias, norm_gain, norm_shift):
    zn, yn, gn, cn = sizes
    seq = lax.axis_index("g")
    core = lax.axis_index("c")
    width = self_output.shape[0]
    joined = width % 128 != 0

    def swap(rows):
        return lax.ppermute(rows, "c", [(0, 1), (1, 0)])

    def gather_rows(rows):
        if cn != 2:
            return lax.all_gather(rows, "c", axis=0, tiled=True)
        got = swap(rows)
        return jnp.where(core == 0, jnp.concatenate([rows, got]), jnp.concatenate([got, rows]))

    def sum_all(part):
        part = part.astype(LOW)
        if cn != 2:
            return lax.psum(part, "c").astype(F32)
        return part.astype(F32) + swap(part).astype(F32)

    def own_rows(rows):
        size = rows.shape[0] // cn
        return lax.dynamic_slice_in_dim(rows, core * size, size, 0)

    def sum_own(part):
        if cn != 2:
            return lax.psum_scatter(part.astype(LOW), "c", scatter_dimension=0, tiled=True).astype(F32)
        size = part.shape[0] // 2
        got = swap(lax.dynamic_slice_in_dim(part, (1 - core) * size, size, 0).astype(LOW))
        return lax.dynamic_slice_in_dim(part, core * size, size, 0) + got.astype(F32)

    def spread(shard, axis):
        every = [shard] + [lax.ppermute(shard, "g", [((i + k) % gn, i) for i in range(gn)]) for k in range(1, gn)]
        return [jnp.concatenate(every, axis=axis)] if joined else every

    def send_home(parts):
        total = parts[0]
        for k in range(1, gn):
            total = total + lax.ppermute(parts[k].astype(LOW), "g", [(i, (i + k) % gn) for i in range(gn)]).astype(F32)
        return total

    steps = [("y", 1, lax.axis_index("y"), yn)] if yn == 2 else []
    steps += [("z", 1 << b, lax.axis_index("z"), zn) for b in range((zn - 1).bit_length())]

    def pairwise(rows, axis, far, size):
        return lax.ppermute(rows, axis, [(i, i ^ far) for i in range(size)])

    def sum_groups(total):
        for axis, far, at, size in steps:
            half = total.shape[0] // 2
            bit = (at // far) % 2
            away = lax.dynamic_slice_in_dim(total, (1 - bit) * half, half, 0).astype(LOW)
            keep = lax.dynamic_slice_in_dim(total, bit * half, half, 0)
            total = keep + pairwise(away, axis, far, size).astype(F32)
        total = total.astype(LOW)
        for axis, far, at, size in reversed(steps):
            got = pairwise(total, axis, far, size)
            total = jnp.where((at // far) % 2 == 0, jnp.concatenate([total, got]), jnp.concatenate([got, total]))
        return total.astype(F32)

    def fetch_slices(shards):
        at = lax.axis_index("z") * yn + lax.axis_index("y")
        pieces = [lax.dynamic_slice_in_dim(shard, at * (shard.shape[0] // (zn * yn)), shard.shape[0] // (zn * yn), 0) for shard in shards]
        pieces = [jnp.stack(pieces)] if pieces[0].shape == pieces[1].shape else [piece[None] for piece in pieces]
        return [[lax.ppermute(piece, "g", [((i + k) % gn, i) for i in range(gn)]) for piece in pieces] for k in range(1, gn)]

    def spread_wide(shards, slices):
        every = [[shard] for shard in shards]
        for got in slices:
            whole = [rows for piece in got for rows in lax.all_gather(piece, ("z", "y"), axis=1, tiled=True)]
            for at, rows in enumerate(whole):
                every[at].append(rows)
        return [[jnp.concatenate(part, axis=1 - at)] if joined else part for at, part in enumerate(every)]

    def parts_of(values, axis):
        return jnp.split(values[0], gn, axis=axis) if joined else values

    target_length = lax.dynamic_slice_in_dim(target_lengths, seq, 1, 0)
    memory_length = lax.dynamic_slice_in_dim(memory_lengths, seq, 1, 0)

    def after(value, *needed):
        return lax.optimization_barrier((value,) + needed)[0]

    token_all = gather_rows(tokens)
    biases = spread(jnp.concatenate([proj_bias, feed_bias.reshape(-1, width)]), 1)
    feed_rows = feed_bias.shape[0] // width
    if joined:
        halves = jnp.split(biases[0], gn, axis=1)
        b_in = [jnp.concatenate([part[4:].reshape(-1) for part in halves])]
    else:
        b_in = [part[4:].reshape(-1) for part in biases]
    b_proj = [part[:4] for part in biases]
    w_self = spread(self_inputs, 2)
    w_self_out = spread(after(self_output, token_all), 0)
    self_q, self_k, self_v, self_mixed, self_lse = [], [], [], [], []
    shards = range(len(w_self))
    for s in shards:
        self_q.append((_nn(token_all, w_self[s][0]) + b_proj[s][0]).astype(LOW))
        self_k.append(_nn(token_all, w_self[s][1]).astype(LOW))
        self_v.append((_nn(token_all, w_self[s][2]) + b_proj[s][1]).astype(LOW))
        mixed, lse = attn_fwd(target_length, self_q[s], self_k[s], self_v[s], True)
        self_mixed.append(mixed)
        self_lse.append(lse)
    first = self_mixed[0]
    slices = fetch_slices([after(feed_in, first), after(feed_out, first)])
    w_in, w_out = spread_wide((feed_in, feed_out), [[after(piece, self_mixed[-1]) for piece in got] for got in slices])
    memory_all = gather_rows(after(memory, first))
    w_cross_mem = spread(after(cross_memory, self_q[-1]), 2)
    w_cross_q = spread(after(cross_query, self_q[-1]), 1)
    w_cross_out = spread(after(cross_output, self_q[-1]), 0)
    cot_all = gather_rows(after(cotangent, self_mixed[-1]))

    cross_k = [_nn(memory_all, w_cross_mem[s][0]).astype(LOW) for s in shards]
    cross_v = [(_nn(memory_all, w_cross_mem[s][1]) + b_proj[s][3]).astype(LOW) for s in shards]
    branch_one = sum_all(sum(_nn(self_mixed[s], w_self_out[s]) for s in shards)) + branch_bias[0]
    normed_one, unit_one, inverse_one = norm_forward(residual_scale * token_all.astype(F32) + branch_one, norm_gain[0], norm_shift[0])
    second = normed_one.astype(LOW)
    cross_q, cross_mixed, cross_lse = [], [], []
    for s in shards:
        rows_in = second if s == 0 else after(second, w_in[-1], w_out[-1])
        cross_q.append((_nn(rows_in, w_cross_q[s]) + b_proj[s][2]).astype(LOW))
        mixed, lse = attn_fwd(memory_length, cross_q[s], cross_k[s], cross_v[s], False)
        cross_mixed.append(mixed)
        cross_lse.append(lse)
    branch_two = sum_all(sum(_nn(cross_mixed[s], w_cross_out[s]) for s in shards)) + branch_bias[1]
    normed_two, unit_two, inverse_two = norm_forward(residual_scale * normed_one + branch_two, norm_gain[1], norm_shift[1])
    third = normed_two.astype(LOW)
    feed_part, hidden, slope = feed_forward(third, w_in, [b_in[s].reshape(1, -1) for s in shards], w_out)
    if cn == 2:
        vectors = jnp.stack([branch_bias[2], norm_gain[2], norm_shift[2]])
        block_out, low_three, grad_three, row_part, sums_three, grad_pre, feed_sums = feed_backward(core.reshape(1), feed_part, swap(feed_part), normed_two, cot_all, vectors, slope, w_in, w_out)
        feed_sums = [part.reshape(-1) for part in feed_sums]
    else:
        branch_three = sum_all(feed_part) + branch_bias[2]
        normed_three, unit_three, inverse_three = norm_forward(residual_scale * normed_two + branch_three, norm_gain[2], norm_shift[2])
        block_out = own_rows(normed_three.astype(LOW))
        cot = cot_all.astype(F32)
        grad_three = norm_backward(cot, unit_three, inverse_three, norm_gain[2])
        low_three = grad_three.astype(LOW)
        grad_pre = [(_nt(low_three, w_out[s]) * slope[s].astype(F32)).astype(LOW) for s in shards]
        row_part = sum(_nt(grad_pre[s], w_in[s]) for s in shards)
        sums_three = [jnp.sum(rows.astype(F32), axis=0) for rows in (low_three, cot * unit_three, cot)]
        feed_sums = [jnp.sum(grad_pre[s].astype(F32), axis=0) for s in shards]
    feed_out_parts = parts_of([tn(hidden[s], low_three) for s in shards], 0)
    feed_in_parts = parts_of([tn(third, grad_pre[s]) for s in shards], 1)
    grad_normed_two = residual_scale * grad_three + sum_all(row_part)
    grad_two = norm_backward(grad_normed_two, unit_two, inverse_two, norm_gain[1])
    low_two = grad_two.astype(LOW)

    def sums(rows):
        return jnp.sum(rows.astype(F32), axis=0)

    def low_pairs(*parts):
        return [(part[0].astype(LOW), part[1].astype(LOW)) for part in parts]

    in_kernel = (zn, yn, gn, cn, width, joined) == (4, 2, 2, 2, SPAN, False)
    if in_kernel:
        per_shard = [(cross_q[s], cross_k[s], cross_v[s], cross_mixed[s], cross_lse[s]) for s in shards]
        row_part, memory_part, cross_sums, go_own, go_other, gq_own, gq_other, gm_own, gm_other, feed_out_sum, feed_in_sum = cross_back(
            memory_length, low_two, per_shard[0], per_shard[1], w_cross_out, second, memory_all, w_cross_q, w_cross_mem, low_pairs(feed_out_parts, feed_in_parts))
        cross_sums = [cross_sums[0, :2], cross_sums[1, :2]]
        grad_memory = memory_part
        grad_normed_one = residual_scale * grad_two + row_part.astype(F32)
    else:
        feed_out_sum, feed_in_sum = [sum_groups(send_home(part)) for part in (feed_out_parts, feed_in_parts)]
        grad_cross_mixed = [_nt(low_two, w_cross_out[s]).astype(LOW) for s in shards]
        cross_out_parts = parts_of([tn(cross_mixed[s], low_two) for s in shards], 0)
        cross_dq, cross_dk, cross_dv = zip(*[attn_bwd(memory_length, cross_q[s], cross_k[s], cross_v[s], cross_mixed[s], grad_cross_mixed[s], cross_lse[s], False) for s in shards])
        grad_normed_one = residual_scale * grad_two + sum_all(sum(_nt(cross_dq[s], w_cross_q[s]) for s in shards))
        cross_parts = [parts_of([tn(rows, grads[s]) for s in shards], 1) for rows, grads in ((second, cross_dq), (memory_all, cross_dk), (memory_all, cross_dv))]
        grad_memory = sum_own(sum(_nt(cross_dk[s], w_cross_mem[s][0]) + _nt(cross_dv[s], w_cross_mem[s][1]) for s in shards)).astype(LOW)
        cross_sums = parts_of([jnp.stack([sums(cross_dq[s]), sums(cross_dv[s])]) for s in shards], 1)
    grad_one = norm_backward(grad_normed_one, unit_one, inverse_one, norm_gain[0])
    low_one = grad_one.astype(LOW)

    model = tokens.shape[1]
    terms = jnp.stack([sums(low_one), sums(low_two), sums_three[0], sums(grad_normed_one * unit_one), sums(grad_normed_two * unit_two), sums_three[1], sums(grad_normed_one), sums(grad_normed_two), sums_three[2]])
    feed_sums = parts_of(feed_sums, 0)
    if not in_kernel:
        grad_self_mixed = [_nt(low_one, w_self_out[s]).astype(LOW) for s in shards]
        self_out_parts = parts_of([tn(self_mixed[s], low_one) for s in shards], 0)
        self_dq, self_dk, self_dv = zip(*[attn_bwd(target_length, self_q[s], self_k[s], self_v[s], self_mixed[s], grad_self_mixed[s], self_lse[s], True) for s in shards])
        token_part = sum_own(sum(_nt(self_dq[s], w_self[s][0]) + _nt(self_dk[s], w_self[s][1]) + _nt(self_dv[s], w_self[s][2]) for s in shards))
        self_sums = parts_of([jnp.stack([sums(self_dq[s]), sums(self_dv[s])]) for s in shards], 1)
    else:
        self_sums = [jnp.zeros((2, width), F32)] * gn
    smalls = []
    for k in range(gn):
        small = lax.dynamic_slice_in_dim(terms, ((seq + k) % gn * cn + core) * width, width, 1)
        small = jnp.concatenate([small, self_sums[k], cross_sums[k], feed_sums[k].reshape(-1, width)])
        smalls.append(jnp.pad(small, ((0, 16 * zn * yn - small.shape[0]), (0, 0))))
    if in_kernel:
        per_shard = [(self_q[s], self_k[s], self_v[s], self_mixed[s], self_lse[s]) for s in shards]
        pairs = [(go_own, go_other), (gq_own, gq_other), (gm_own, gm_other)]
        token_part, *sums_low = self_back(target_length, low_one, per_shard[0], per_shard[1], w_self_out, token_all, w_self, smalls, pairs)
    else:
        groups = [[cross_out_parts], cross_parts[:1], cross_parts[1:], [self_out_parts], [parts_of([tn(token_all, grads[s]) for s in shards], 1) for grads in (self_dq, self_dk, self_dv)], [smalls]]
        sums_low = [sum_groups(send_home([jnp.concatenate([part[k] for part in group]) for k in range(gn)])) for group in groups]
    cross_out_sum, cross_q_sum, cross_mem_sum, self_out_sum, self_in_sum, small = [rows.astype(F32) for rows in sums_low]
    feed_out_sum, feed_in_sum = feed_out_sum.astype(F32), feed_in_sum.astype(F32)
    grad_tokens = (residual_scale * own_rows(grad_one) + token_part).astype(LOW)
    return (block_out, grad_tokens, grad_memory, self_in_sum.reshape(3, model, width), self_out_sum, cross_q_sum, cross_mem_sum.reshape(2, model, width), cross_out_sum, feed_in_sum, feed_out_sum, small[9:13], small[13:13 + feed_rows].reshape(-1), small[0:3], small[3:6], small[6:9])


def solution(mesh):
    dp, mp = mesh.shape["dp"], mesh.shape["mp"]

    def whole(*args):
        yn = 2 if dp % 2 == 0 else 1
        gn = args[3].shape[0] // dp
        sizes = (dp // yn, yn, gn, mp // gn)
        fine = Mesh(mesh.devices.reshape(sizes), ("z", "y", "g", "c"))
        d, m = ("z", "y"), ("g", "c")
        rows, wide, tall = P(d + m, None), P(None, m), P(m, None)
        stack = P(None, None, m)
        in_specs = (rows, rows, rows, P(d), P(d), stack, tall, wide, stack, tall, wide, tall, wide, P(m), P(), P(), P())
        out_specs = (rows, rows, rows, stack, tall, wide, stack, tall, wide, tall, wide, P(m), wide, wide, wide)
        return jax.shard_map(functools.partial(layer, sizes), mesh=fine, in_specs=in_specs, out_specs=out_specs, check_vma=False)(*args)

    return whole
```

```python
import functools
import math

import jax, jax.numpy as jnp
from jax import lax
from jax.experimental import pallas as pl
from jax.experimental.pallas import tpu as pltpu
from jax.sharding import Mesh
from jax.sharding import PartitionSpec as P

HEAD = 64
NEG = -1e30

def _nt(a, b):
    return lax.dot_general(a, b, (((1,), (1,)), ((), ())), preferred_element_type=jnp.float32)

def _nn(a, b):
    return lax.dot_general(a, b, (((1,), (0,)), ((), ())), preferred_element_type=jnp.float32)

def _lanes(rows):
    return lax.broadcasted_iota(jnp.int32, (rows, 128), 1)

def _put(base, lane, pairs):
    for at, val in pairs:
        base = jnp.where(lane == at, val, base)
    return base

def fwd_kernel(len_ref, q_ref, k_ref, v_ref, o_ref, lse_ref, *, causal, bq):
    p = pl.program_id(0)
    rows, keys = q_ref.shape[0], k_ref.shape[0]
    length = len_ref[0]
    kl = _lanes(keys)
    kpos = lax.broadcasted_iota(jnp.int32, (keys, 128), 0)
    kbias = jnp.where(kpos < length, 0.0, NEG)
    k2 = k_ref[...].astype(jnp.float32)
    v2 = v_ref[...].astype(jnp.float32)
    ql = _lanes(bq)
    heads = []
    for h in range(2):
        mine = (kl // HEAD) == h
        other = HEAD * (1 - h)
        kh = jnp.where(mine, k2, jnp.where(kl == other, kbias, 0.0)).astype(jnp.bfloat16)
        vh = jnp.where(mine, v2, jnp.where(kl == other, 1.0, 0.0)).astype(jnp.bfloat16)
        heads.append((kh, vh))
    for i in range(rows // bq):
        q2 = q_ref[pl.ds(i * bq, bq), :].astype(jnp.float32) * (HEAD ** -0.5)
        out = jnp.zeros((bq, 128), jnp.float32)
        lse_all = lse_ref[pl.ds(i * bq, bq), :]
        for h in range(2):
            kh, vh = heads[h]
            mine = (ql // HEAD) == h
            other = HEAD * (1 - h)
            qh = jnp.where(mine, q2, jnp.where(ql == other, 1.0, 0.0)).astype(jnp.bfloat16)
            if causal:
                lo = i * bq
                sd = _nt(qh, kh[lo:lo + bq])
                r = lax.broadcasted_iota(jnp.int32, (bq, bq), 0)
                c = lax.broadcasted_iota(jnp.int32, (bq, bq), 1)
                sd = jnp.where(c <= r, sd, NEG)
                m = jnp.max(sd, axis=1, keepdims=True)
                if lo:
                    sl = _nt(qh, kh[:lo])
                    m = jnp.maximum(m, jnp.max(sl, axis=1, keepdims=True))
                    acc = _nn(jnp.exp(sl - m).astype(jnp.bfloat16), vh[:lo])
                    acc += _nn(jnp.exp(sd - m).astype(jnp.bfloat16), vh[lo:lo + bq])
                else:
                    acc = _nn(jnp.exp(sd - m).astype(jnp.bfloat16), vh[:bq])
            else:
                s = _nt(qh, kh)
                m = jnp.max(s, axis=1, keepdims=True)
                acc = _nn(jnp.exp(s - m).astype(jnp.bfloat16), vh)
            total = jnp.sum(jnp.where(ql == other, acc, 0.0), axis=1, keepdims=True)
            out = jnp.where(mine, acc / total, out)
            lse_all = jnp.where(ql == 2 * p + h, m + jnp.log(total), lse_all)
        o_ref[pl.ds(i * bq, bq), :] = out.astype(jnp.bfloat16)
        lse_ref[pl.ds(i * bq, bq), :] = lse_all

def attn_fwd(length, q, k, v, causal, bq=256):
    rows, cols = q.shape
    keys = k.shape[0]
    pairs = cols // 128
    el = pairs * 2 * rows * keys
    return pl.pallas_call(
        functools.partial(fwd_kernel, causal=causal, bq=bq),
        out_shape=(jax.ShapeDtypeStruct((rows, cols), jnp.bfloat16), jax.ShapeDtypeStruct((rows, 128), jnp.float32)),
        grid_spec=pltpu.PrefetchScalarGridSpec(
            num_scalar_prefetch=1, grid=(pairs,),
            in_specs=[pl.BlockSpec((rows, 128), lambda p, n: (0, p)), pl.BlockSpec((keys, 128), lambda p, n: (0, p)), pl.BlockSpec((keys, 128), lambda p, n: (0, p))],
            out_specs=[pl.BlockSpec((rows, 128), lambda p, n: (0, p)), pl.BlockSpec((rows, 128), lambda p, n: (0, 0))],
        ),
        compiler_params=pltpu.CompilerParams(dimension_semantics=("arbitrary",), vmem_limit_bytes=40 << 20),
        cost_estimate=pl.CostEstimate(flops=16 * el * 64, bytes_accessed=8 * rows * cols, transcendentals=el),
        name="attend_forward",
    )(length, q, k, v)

def split3(x):
    a = x.astype(jnp.bfloat16).astype(jnp.float32)
    b = (x - a).astype(jnp.bfloat16).astype(jnp.float32)
    return a, b, x - a - b


def key_side(k2, v2, length):
    keys = k2.shape[0]
    kl = _lanes(keys)
    kbias = jnp.where(lax.broadcasted_iota(jnp.int32, (keys, 128), 0) < length, 0.0, NEG)
    k2, v2 = k2.astype(jnp.float32), v2.astype(jnp.float32)
    heads = []
    for h in range(2):
        mine = (kl // HEAD) == h
        other = HEAD * (1 - h)
        ones = (kl > other) & (kl < other + 4)
        kh = jnp.where(mine, k2, jnp.where(kl == other, kbias, jnp.where(ones, 1.0, 0.0))).astype(jnp.bfloat16)
        vh = jnp.where(mine, v2, jnp.where(ones, 1.0, 0.0)).astype(jnp.bfloat16)
        heads.append((kh, vh, kh.T))
    return heads


def query_block(heads, q2, o2, g2, lse_all, pair, i, last, causal, dka, dva):
    bq = q2.shape[0]
    keys = heads[0][0].shape[0]
    ql = _lanes(bq)
    q2 = q2.astype(jnp.float32) * (HEAD ** -0.5)
    g2 = g2.astype(jnp.float32)
    go = g2 * o2.astype(jnp.float32)
    dqt = []
    for h in range(2):
        kh, vh, kt = heads[h]
        mine = (ql // HEAD) == h
        other = HEAD * (1 - h)
        lse = jnp.sum(jnp.where(ql == 2 * pair + h, lse_all, 0.0), axis=1, keepdims=True)
        delta = jnp.sum(jnp.where(mine, go, 0.0), axis=1, keepdims=True)
        la, lb, lc = split3(-lse)
        da, db, dc = split3(-delta)
        qh = _put(jnp.where(mine, q2, 0.0), ql, ((other, 1.0), (other + 1, la), (other + 2, lb), (other + 3, lc))).astype(jnp.bfloat16)
        gh = _put(jnp.where(mine, g2, 0.0), ql, ((other + 1, da), (other + 2, db), (other + 3, dc))).astype(jnp.bfloat16)
        hi = (i + 1) * bq if causal else keys
        st = _nt(kh[:hi], qh)
        if causal:
            kr = lax.broadcasted_iota(jnp.int32, (hi, bq), 0)
            qc = lax.broadcasted_iota(jnp.int32, (hi, bq), 1) + i * bq
            pt = jnp.where(kr <= qc, jnp.exp(st), 0.0)
        else:
            pt = jnp.exp(st)
        dst = (pt * _nt(vh[:hi], gh)).astype(jnp.bfloat16)
        dvn = _nn(pt.astype(jnp.bfloat16), gh)
        dkn = _nn(dst, qh)
        if last:
            dva[h, :hi] = dvn
            dka[h, :hi] = dkn
        else:
            dva[h, :hi] += dvn
            dka[h, :hi] += dkn
        dqt.append(_nn(kt[:, :hi], dst))
    dq = jnp.concatenate([dqt[0][:HEAD], dqt[1][HEAD:]], axis=0).T
    return (dq * (HEAD ** -0.5)).astype(jnp.bfloat16)


def bwd_kernel(len_ref, q_ref, k_ref, v_ref, o_ref, g_ref, lse_ref, dq_ref, dk_ref, dv_ref, dka, dva, *, causal, bq):
    rows, keys = q_ref.shape[0], k_ref.shape[0]
    heads = key_side(k_ref[...], v_ref[...], len_ref[0])
    blocks = rows // bq
    for i in reversed(range(blocks)):
        at = pl.ds(i * bq, bq)
        dq_ref[at, :] = query_block(heads, q_ref[at, :], o_ref[at, :], g_ref[at, :], lse_ref[at, :], pl.program_id(0), i, i == blocks - 1, causal, dka, dva)
    first = _lanes(keys) < HEAD
    dk_ref[...] = jnp.where(first, dka[0], dka[1]).astype(jnp.bfloat16)
    dv_ref[...] = jnp.where(first, dva[0], dva[1]).astype(jnp.bfloat16)

def attn_bwd(length, q, k, v, o, g, lse, causal, bq=256):
    rows, cols = q.shape
    keys = k.shape[0]
    pairs = cols // 128
    el = pairs * 2 * rows * keys
    qs = pl.BlockSpec((rows, 128), lambda p, n: (0, p))
    ks = pl.BlockSpec((keys, 128), lambda p, n: (0, p))
    return pl.pallas_call(
        functools.partial(bwd_kernel, causal=causal, bq=bq),
        out_shape=(jax.ShapeDtypeStruct((rows, cols), jnp.bfloat16), jax.ShapeDtypeStruct((keys, cols), jnp.bfloat16), jax.ShapeDtypeStruct((keys, cols), jnp.bfloat16)),
        grid_spec=pltpu.PrefetchScalarGridSpec(
            num_scalar_prefetch=1, grid=(pairs,),
            in_specs=[qs, ks, ks, qs, qs, pl.BlockSpec((rows, 128), lambda p, n: (0, 0))],
            out_specs=[qs, ks, ks],
            scratch_shapes=[pltpu.VMEM((2, keys, 128), jnp.float32), pltpu.VMEM((2, keys, 128), jnp.float32)],
        ),
        compiler_params=pltpu.CompilerParams(dimension_semantics=("arbitrary",), vmem_limit_bytes=48 << 20),
        cost_estimate=pl.CostEstimate(flops=40 * el * 64, bytes_accessed=16 * rows * cols, transcendentals=el),
        name="attend_backward",
    )(length, q, k, v, o, g, lse)

CHUNK = 512
LAG = 1
SPAN = 256


class Pipeline:
    AHEAD = 3

    def __init__(self, total, scratch):
        self.spots, self.total, self.step, self.sent, self.loaded = [], total, 0, 0, 0
        (self.held, self.ysum, self.zgot, self.mine, self.load, self.store, self.xs, self.xr, self.ys, self.yr, self.zs, self.zr, self.bs, self.br, self.es, self.er) = scratch
        self.full = self.held
        self.seq, self.ya, za = lax.axis_index("g"), lax.axis_index("y"), lax.axis_index("z")
        self.za = za
        self.peers = {1: za + 1 - 2 * (za % 2), 2: (za + 2) % 4, 3: 3 - za}
        self.stages = (self.to_y, self.to_z, self.back_z, self.back_y, self.finish)

    @staticmethod
    def scratch(total, most):
        dma = pltpu.SemaphoreType.DMA
        return [
            pltpu.VMEM((total, most, SPAN), LOW),
            pltpu.VMEM((total, most // 2, SPAN), LOW),
            pltpu.VMEM((total, 3, most // 8, SPAN), LOW),
            pltpu.VMEM((4, most, SPAN), LOW),
            dma((4,)), dma((total,)),
            dma((total,)), dma((total,)), dma((total,)), dma((total,)),
            dma((total, 3)), dma((total, 3)), dma((total, 3)), dma((total, 3)),
            dma((total,)), dma((total,)),
        ]

    def greet(self, more=()):
        barrier = pltpu.get_barrier_semaphore()
        everyone = [{"g": 1 - self.seq}, {"y": 1 - self.ya}] + [{"z": self.peers[d]} for d in (1, 2, 3)] + list(more)
        for where in everyone:
            pl.semaphore_signal(barrier, inc=1, device_id=where, device_id_type=pl.DeviceIdType.MESH)
        pl.semaphore_wait(barrier, len(everyone))

    def add(self, own, other, out, taper=False, first=0, count=None):
        for r, size, c in cut(own.shape[0] if count is None else count, own.shape[1], taper):
            self.spots.append((own, other, first + r, c, size, out, first + r))
        self.feed()

    def feed(self):
        while self.sent < min(len(self.spots), self.step + self.AHEAD):
            self.x_copy(self.sent).start()
            self.own_copy(self.sent).start()
            self.sent += 1

    def tick(self, times=1):
        for unused in range(times):
            if self.step >= self.total + LAG * (len(self.stages) - 1) or len(self.spots) <= self.step < self.total:
                return
            for at, stage in enumerate(self.stages):
                if 0 <= self.step - LAG * at < self.total:
                    stage(self.step - LAG * at)
            self.step += 1
            self.feed()

    def drain(self):
        assert len(self.spots) == self.total
        self.tick(self.total + LAG * len(self.stages))
        for k in range(self.total):
            self.x_copy(k).wait_send()
            self.yb_copy(k).wait_send()
            self.out_copy(k).wait()
            for d in (1, 2, 3):
                self.z_copy(k, d).wait_send()
                self.zb_copy(k, d).wait_send()

    @staticmethod
    def remote(src, dst, send, recv, where):
        return pltpu.make_async_remote_copy(src_ref=src, dst_ref=dst, send_sem=send, recv_sem=recv, device_id=where, device_id_type=pl.DeviceIdType.MESH)

    @staticmethod
    def block(at, size):
        return pl.ds(pl.multiple_of(at * size, size), size)

    def x_copy(self, k):
        own, other, r, c, n, o, q = self.spots[k]
        return self.remote(other.at[pl.ds(r, n), pl.ds(c, SPAN)], self.held.at[k, pl.ds(0, n)], self.xs.at[k], self.xr.at[k], {"g": 1 - self.seq})

    def own_copy(self, k):
        own, other, r, c, n, o, q = self.spots[k]
        return pltpu.make_async_copy(own.at[pl.ds(r, n), pl.ds(c, SPAN)], self.mine.at[k % 4, pl.ds(0, n)], self.load.at[k % 4])

    def y_copy(self, k):
        h = self.spots[k][4] // 2
        return self.remote(self.held.at[k, self.block(1 - self.ya, h)], self.ysum.at[k, pl.ds(0, h)], self.ys.at[k], self.yr.at[k], {"y": 1 - self.ya})

    def z_copy(self, k, d):
        p = self.spots[k][4] // 8
        return self.remote(self.ysum.at[k, self.block(self.peers[d], p)], self.zgot.at[k, d - 1, pl.ds(0, p)], self.zs.at[k, d - 1], self.zr.at[k, d - 1], {"z": self.peers[d]})

    def zb_copy(self, k, d):
        rows = self.full.at[k, self.block(self.ya * 4 + self.za, self.spots[k][4] // 8)]
        return self.remote(rows, rows, self.bs.at[k, d - 1], self.br.at[k, d - 1], {"z": self.peers[d]})

    def yb_copy(self, k):
        rows = self.full.at[k, self.block(self.ya, self.spots[k][4] // 2)]
        return self.remote(rows, rows, self.es.at[k], self.er.at[k], {"y": 1 - self.ya})

    def out_copy(self, k):
        own, other, r, c, n, o, q = self.spots[k]
        return pltpu.make_async_copy(self.full.at[k, pl.ds(0, n)], o.at[pl.ds(q, n), pl.ds(c, SPAN)], self.store.at[k])

    def to_y(self, k):
        n = self.spots[k][4]
        self.own_copy(k).wait()
        self.x_copy(k).wait_recv()
        self.held[k, :n] = self.held[k, :n] + self.mine[k % 4, :n]
        self.y_copy(k).start()

    def to_z(self, k):
        h = self.spots[k][4] // 2
        self.y_copy(k).wait()
        self.ysum[k, :h] = self.ysum[k, :h] + self.held[k, self.block(self.ya, h)]
        for d in (1, 2, 3):
            self.z_copy(k, d).start()

    def back_z(self, k):
        p = self.spots[k][4] // 8
        for d in (1, 2, 3):
            self.z_copy(k, d).wait_recv()
        rows = self.ysum[k, self.block(self.za, p)].astype(F32)
        for d in (1, 2, 3):
            rows = rows + self.zgot[k, d - 1, :p].astype(F32)
        self.full[k, self.block(self.ya * 4 + self.za, p)] = rows.astype(LOW)
        for d in (1, 2, 3):
            self.zb_copy(k, d).start()

    def back_y(self, k):
        for d in (1, 2, 3):
            self.zb_copy(k, d).wait_recv()
        self.yb_copy(k).start()

    def finish(self, k):
        self.yb_copy(k).wait_recv()
        self.out_copy(k).start()


def cut(rows, cols, taper=False):
    size = min(CHUNK, rows)
    chunks = [(r, size, c) for r in range(0, rows, size) for c in range(0, cols, SPAN)]
    if taper:
        r, unused, c = chunks.pop()
        chunks += [(r, size // 2, c), (r + size // 2, size // 4, c), (r + size - size // 4, size // 4, c)]
    return chunks


def spot_count(shapes, taper=()):
    return sum(len(cut(rows, cols, at in taper)) for at, (rows, cols) in enumerate(shapes))


def attend_back(pipe, shards, length, low, gm, dq, dk, dv, dka, dva, causal, bq, every):
    rows = low.shape[0]
    blocks = rows // bq
    for s, (q, k, v, o, l, wo) in enumerate(shards):
        for i in range(blocks):
            at = pl.ds(i * bq, bq)
            gm[s, at, :] = _nt(low[at, :], wo[...]).astype(LOW)
    for s, (q, k, v, o, l, wo) in enumerate(shards):
        for p in range(q.shape[1] // 128):
            cols = pl.ds(p * 128, 128)
            heads = key_side(k[:, cols], v[:, cols], length)
            for i in reversed(range(blocks)):
                at = pl.ds(i * bq, bq)
                dq[s, at, cols] = query_block(heads, q[at, cols], o[at, cols], gm[s, at, cols], l[at, :], p, i, i == blocks - 1, causal, dka, dva)
                if i % every == 0:
                    pipe.tick()
            first = _lanes(k.shape[0]) < HEAD
            dk[s, :, cols] = jnp.where(first, dka[0], dka[1]).astype(LOW)
            dv[s, :, cols] = jnp.where(first, dva[0], dva[1]).astype(LOW)


def back_rows(terms, start, size):
    at = pl.ds(pl.multiple_of(start, size), size)
    both = None
    for grads, s, weight in terms:
        term = _nt(grads[s, at, :], weight)
        both = term if both is None else both + term
    return both


def output_grads(shards, low, outs):
    for (q, k, v, o, l, wo), out in zip(shards, outs):
        for c in range(0, low.shape[1], SPAN):
            out[:, c : c + SPAN] = tn(o[...], low[:, c : c + SPAN]).astype(LOW)


def input_grads(rows_in, grads, out, first, bq):
    for i in range(0, rows_in.shape[1], bq):
        out[pl.ds(first + i, bq), :] = tn(rows_in[:, i : i + bq], grads).astype(LOW)


def share_rows(terms, core, part, got, sems, out, bq, pipe, more):
    half = out.shape[0]
    copy = Pipeline.remote(part, got, sems[0], sems[1], {"c": 1 - core})
    for i in range(0, half, bq):
        part[pl.ds(i, bq), :] = back_rows(terms, (1 - core) * half + i, bq).astype(LOW)
    copy.start()
    pipe.tick()
    mine = [back_rows(terms, core * half + i, bq) for i in range(0, half, bq)]
    if more is not None:
        mine = [rows + more(pl.ds(pl.multiple_of(core * half + at * bq, bq), bq)) for at, rows in enumerate(mine)]
    pipe.tick()
    copy.wait()
    for i in range(0, half, bq):
        out[pl.ds(i, bq), :] = (mine[i // bq] + got[pl.ds(i, bq), :].astype(F32)).astype(out.dtype)


def norm_back(scale, grad_above, terms, unit_rows, inverse, gain, blocks, keep, low, sums, bq):
    above, unit, sem = blocks
    totals = None
    for i in range(low.shape[0] // bq):
        at = pl.ds(i * bq, bq)
        loads = [pltpu.make_async_copy(grad_above.at[at, :], above, sem.at[0]), pltpu.make_async_copy(unit_rows.at[at, :], unit, sem.at[1])]
        for load in loads:
            load.start()
        for load in loads:
            load.wait()
        incoming = scale * above[...] + terms(at)
        grads = norm_backward(incoming, unit[...], inverse[at, :], gain[...])
        low_rows = grads.astype(LOW)
        low[at, :] = low_rows
        keep(i, at, grads)
        new = [jnp.sum(v, axis=0, keepdims=True) for v in (low_rows.astype(F32), incoming * unit[...], incoming)]
        totals = new if totals is None else [x + y for x, y in zip(totals, new)]
    for at, total in enumerate(totals):
        sums[at : at + 1] = total


def self_back_kernel(carried, bq, scale, len_ref, above_in, row_in, unit_in, inverse, gain, q0, k0, v0, o0, l0, q1, k1, v1, o1, l1, wo0, wo1, x_in, w0, w1, small0, small1, *rest):
    own, other, rest = rest[:carried], rest[carried : 2 * carried], rest[2 * carried :]
    token_out, rest = rest[0], rest[1:]
    outs, rest = rest[: carried + 3], rest[carried + 3 :]
    gm, dq, dk, dv, dka, dva, go_own, go_other, gi_own, gi_other, sm_own, sm_other, part, got, part_send, part_recv, low, kept, sums, above, unit, loads = rest[:22]
    core = lax.axis_index("c")
    total = spot_count([ref.shape for ref in own] + [go_own.shape, sm_own.shape] + [(low.shape[1], gi_own.shape[1])] * 3, (carried + 4,))
    pipe = Pipeline(total, rest[22:])
    pipe.greet([{"c": 1 - core}])
    for a, b, out in zip(own, other, outs):
        pipe.add(a, b, out)
    shards = ((q0, k0, v0, o0, l0, wo0), (q1, k1, v1, o1, l1, wo1))

    def keep(i, at, grads):
        kept[at, :] = grads
        pipe.tick()

    norm_back(scale, above_in, lambda at: row_in[at, :].astype(F32), unit_in, inverse, gain, (above, unit, loads), keep, low, sums, bq)
    output_grads(shards, low, (go_own, go_other))
    pipe.add(go_own, go_other, outs[carried])
    attend_back(pipe, shards, len_ref[0], low, gm, dq, dk, dv, dka, dva, True, bq, 2)
    for s, (sm, small) in enumerate(((sm_own, small0), (sm_other, small1))):
        row = lax.broadcasted_iota(jnp.int32, sm.shape, 0)
        shard = (pipe.seq + s) % 2 * 2 + core
        mine = pl.ds(pl.multiple_of(shard * sm.shape[1], sm.shape[1]), sm.shape[1])
        filled = small[...]
        for at, value in ((0, sums[0:1, mine]), (3, sums[1:2, mine]), (6, sums[2:3, mine]), (9, jnp.sum(dq[s].astype(F32), axis=0, keepdims=True)), (10, jnp.sum(dv[s].astype(F32), axis=0, keepdims=True))):
            filled = jnp.where(row == at, value, filled)
        sm[...] = filled.astype(LOW)
    pipe.add(sm_own, sm_other, outs[carried + 2])
    model = x_in.shape[1]
    for m, grads in enumerate((dq, dk, dv)):
        for s, gi in enumerate((gi_own, gi_other)):
            input_grads(x_in, grads[s], gi, m * model, bq)
            pipe.tick()
        pipe.add(gi_own, gi_other, outs[carried + 1], m == 2, m * model, model)
    terms = [(grads, s, w[m]) for s, w in ((0, w0), (1, w1)) for m, grads in enumerate((dq, dk, dv))]
    share_rows(terms, core, part, got, (part_send, part_recv), token_out, bq, pipe, lambda at: scale * kept[at, :])
    pipe.drain()


def cross_back_kernel(carried, bq, scale, len_ref, above_in, row_in, unit_in, inverse, gain, q0, k0, v0, o0, l0, q1, k1, v1, o1, l1, wo0, wo1, x_in, m_in, wq0, wq1, wm0, wm1, *rest):
    own, other, rest = rest[:carried], rest[carried : 2 * carried], rest[2 * carried :]
    row_out, memory_out, sums_out, go_own, go_other, gq_own, gq_other, gm_own, gm_other, norm_sums, grad_out = rest[:11]
    outs, rest = rest[11 : 11 + carried], rest[11 + carried :]
    gm, dq, dk, dv, dka, dva, part, got, part_send, part_recv, full_part, full_got, full_send, full_recv, low, row_got, row_send, row_recv, above, unit, loads, stored = rest[:22]
    core = lax.axis_index("c")
    pipe = Pipeline(spot_count([ref.shape for ref in own], (carried - 1,)), rest[22:])
    pipe.greet([{"c": 1 - core}])
    rows_over = Pipeline.remote(row_in, row_got, row_send, row_recv, {"c": 1 - core})
    rows_over.start()
    for at, (a, b, out) in enumerate(zip(own, other, outs)):
        pipe.add(a, b, out, at == carried - 1)
    rows_over.wait()

    def keep(i, at, grads):
        above[...] = grads
        copy = pltpu.make_async_copy(above, grad_out.at[at, :], stored)
        copy.start()
        pipe.tick()
        copy.wait()

    norm_back(scale, above_in, lambda at: row_in[at, :].astype(F32) + row_got[at, :].astype(F32), unit_in, inverse, gain, (above, unit, loads), keep, low, norm_sums, bq)
    shards = ((q0, k0, v0, o0, l0, wo0), (q1, k1, v1, o1, l1, wo1))
    attend_back(pipe, shards, len_ref[0], low, gm, dq, dk, dv, dka, dva, False, bq, 1)
    rows = low.shape[0]
    terms = [(dq, 0, wq0[...]), (dq, 1, wq1[...])]
    for i in range(0, rows, bq):
        full_part[pl.ds(i, bq), :] = back_rows(terms, i, bq).astype(LOW)
        if i % (2 * bq):
            pipe.tick()
    exchange = Pipeline.remote(full_part, full_got, full_send, full_recv, {"c": 1 - core})
    exchange.start()
    pipe.tick()
    terms = [(grads, s, w[m]) for s, w in ((0, wm0), (1, wm1)) for m, grads in enumerate((dk, dv))]
    share_rows(terms, core, part, got, (part_send, part_recv), memory_out, bq, pipe, None)
    output_grads(shards, low, (go_own, go_other))
    pipe.tick()
    for s, (gq, gkv) in enumerate(((gq_own, gm_own), (gq_other, gm_other))):
        input_grads(x_in, dq[s], gq, 0, bq)
        pipe.tick()
        input_grads(m_in, dk[s], gkv, 0, bq)
        pipe.tick()
        input_grads(m_in, dv[s], gkv, m_in.shape[1], bq)
        sums_out[s, 0:1] = jnp.sum(dq[s].astype(F32), axis=0, keepdims=True)
        sums_out[s, 1:2] = jnp.sum(dv[s].astype(F32), axis=0, keepdims=True)
        pipe.tick()
    exchange.wait()
    for i in range(0, rows, bq):
        at = pl.ds(i, bq)
        row_out[at, :] = (full_part[at, :].astype(F32) + full_got[at, :].astype(F32)).astype(LOW)
    pipe.drain()


def low_ram(*shape):
    return pltpu.VMEM(shape, LOW)


def back_scratch(rows, width):
    return [low_ram(2, rows, width) for unused in range(4)] + [pltpu.VMEM((2, rows, 128), F32), pltpu.VMEM((2, rows, 128), F32)]


def self_back(length, above, row_part, unit, inverse, gain, first, second, wo, x_in, w, smalls, pairs, bq=256):
    rows, model = above.shape
    width = wo[0].shape[0]
    carried = len(pairs)
    any_space = pl.BlockSpec(memory_space=pl.ANY)
    vmem = pl.BlockSpec(memory_space=pltpu.VMEM)
    dma = pltpu.SemaphoreType.DMA
    ends = [(width, model), (3 * rows, width), smalls[0].shape]
    total = spot_count([own.shape for own, unused in pairs] + [ends[0], ends[2]] + [(model, width)] * 3, (carried + 4,))
    return pl.pallas_call(
        functools.partial(self_back_kernel, carried, bq, residual_scale),
        out_shape=[jax.ShapeDtypeStruct((rows // 2, model), LOW)] + [jax.ShapeDtypeStruct(own.shape, LOW) for own, unused in pairs] + [jax.ShapeDtypeStruct(shape, LOW) for shape in ends],
        in_specs=[pl.BlockSpec(memory_space=pltpu.SMEM), any_space, vmem, any_space, vmem, vmem] + [vmem] * 17 + [any_space] * (2 * carried),
        out_specs=[vmem] + [any_space] * (carried + 3),
        scratch_shapes=back_scratch(rows, width)
        + [low_ram(width, model), low_ram(width, model), low_ram(3 * rows, width), low_ram(3 * rows, width), low_ram(*smalls[0].shape), low_ram(*smalls[0].shape)]
        + [low_ram(rows // 2, model), low_ram(rows // 2, model), dma, dma]
        + [low_ram(rows, model), pltpu.VMEM((rows, model), F32), pltpu.VMEM((8, model), F32), pltpu.VMEM((bq, model), F32), pltpu.VMEM((bq, model), F32), dma((2,))]
        + Pipeline.scratch(total, CHUNK),
        compiler_params=pltpu.CompilerParams(collective_id=0, has_side_effects=True, vmem_limit_bytes=58 << 20),
        cost_estimate=pl.CostEstimate(flops=20 * rows * model * width, bytes_accessed=300 << 20, transcendentals=8 * rows * rows),
        name="self_backward",
    )(length, above, row_part, unit, inverse, gain, *first, *second, *wo, x_in, *w, *smalls, *[p[0] for p in pairs], *[p[1] for p in pairs])


def cross_back(length, above, row_part, unit, inverse, gain, first, second, wo, x_in, m_in, wq, wm, pairs, bq=256):
    rows, model = above.shape
    width = wo[0].shape[0]
    carried = len(pairs)
    any_space = pl.BlockSpec(memory_space=pl.ANY)
    vmem = pl.BlockSpec(memory_space=pltpu.VMEM)
    dma = pltpu.SemaphoreType.DMA
    total = spot_count([own.shape for own, unused in pairs], (carried - 1,))
    shape = jax.ShapeDtypeStruct
    return pl.pallas_call(
        functools.partial(cross_back_kernel, carried, bq, residual_scale),
        out_shape=[shape((rows, model), LOW), shape((rows // 2, model), LOW), shape((2, 8, width), F32)]
        + [shape((width, model), LOW)] * 2 + [shape((rows, width), LOW)] * 2 + [shape((2 * rows, width), LOW)] * 2 + [shape((8, model), F32), shape((rows, model), F32)]
        + [shape(own.shape, LOW) for own, unused in pairs],
        in_specs=[pl.BlockSpec(memory_space=pltpu.SMEM), any_space, vmem, any_space, vmem, vmem] + [vmem] * 18 + [any_space] * (2 * carried),
        out_specs=[vmem] * 10 + [any_space] * (1 + carried),
        scratch_shapes=back_scratch(rows, width)
        + [low_ram(rows // 2, model), low_ram(rows // 2, model), dma, dma]
        + [low_ram(rows, model), low_ram(rows, model), dma, dma]
        + [low_ram(rows, model), low_ram(rows, model), dma, dma, pltpu.VMEM((bq, model), F32), pltpu.VMEM((bq, model), F32), dma((2,)), dma]
        + Pipeline.scratch(total, CHUNK),
        compiler_params=pltpu.CompilerParams(collective_id=1, has_side_effects=True, vmem_limit_bytes=58 << 20),
        cost_estimate=pl.CostEstimate(flops=20 * rows * model * width, bytes_accessed=300 << 20, transcendentals=8 * rows * rows),
        name="cross_backward",
    )(length, above, row_part, unit, inverse, gain, *first, *second, *wo, x_in, m_in, *wq, *wm, *[p[0] for p in pairs], *[p[1] for p in pairs])


def feed_kernel(count, rows_in, *refs):
    w_in, b_in, w_out, part, hidden, slope = refs[:count], refs[count : 2 * count], refs[2 * count : 3 * count], refs[3 * count], refs[3 * count + 1 : 4 * count + 1], refs[4 * count + 1 :]
    branch = None
    for s in range(count):
        pre = _nn(rows_in[...], w_in[s][...]) + b_in[s][...].astype(F32)
        spread_to = 0.5 + 0.5 * lax.erf(pre * 0.5**0.5)
        hidden[s][...] = (pre * spread_to).astype(LOW)
        slope[s][...] = (spread_to + pre * (jnp.exp(-0.5 * pre * pre) * (2.0 * math.pi) ** -0.5)).astype(LOW)
        term = _nn(hidden[s][...], w_out[s][...])
        branch = term if branch is None else branch + term
    part[...] = branch.astype(LOW)


def feed_forward(rows_in, w_in, b_in, w_out, bq=256):
    count = len(w_in)
    rows, model = rows_in.shape
    units = w_in[0].shape[1]
    wide = pl.BlockSpec((bq, units), lambda i: (i, 0))
    block = pl.BlockSpec((bq, model), lambda i: (i, 0))
    held = lambda array: pl.BlockSpec(array.shape, lambda i: (0, 0))
    out = pl.pallas_call(
        functools.partial(feed_kernel, count),
        grid=(rows // bq,),
        out_shape=[jax.ShapeDtypeStruct((rows, model), LOW)] + [jax.ShapeDtypeStruct((rows, units), LOW)] * (2 * count),
        in_specs=[block] + [held(array) for array in (*w_in, *b_in, *w_out)],
        out_specs=[block] + [wide] * (2 * count),
        compiler_params=pltpu.CompilerParams(dimension_semantics=("arbitrary",), vmem_limit_bytes=50 << 20),
        cost_estimate=pl.CostEstimate(flops=4 * count * rows * model * units, bytes_accessed=16 << 20, transcendentals=2 * count * rows * units),
        name="feed_forward",
    )(rows_in, *w_in, *b_in, *w_out)
    return out[0], out[1 : 1 + count], out[1 + count :]


def feed_back_kernel(count, scale, core_ref, part, got, normed, cot_ref, vectors, *refs):
    slope, w_in, w_out, refs = refs[:count], refs[count : 2 * count], refs[2 * count : 3 * count], refs[3 * count :]
    out, low, grad, row_part, sums, refs = refs[0], refs[1], refs[2], refs[3], refs[4], refs[5:]
    pre_grads, pre_sums = refs[:count], refs[count:]
    step = pl.program_id(0)
    bias, gain, shift = vectors[0:1], vectors[1:2], vectors[2:3]
    summed = scale * normed[...] + (part[...].astype(F32) + got[...].astype(F32) + bias)
    rows, unit, inverse = norm_forward(summed, gain, shift)
    half = pl.num_programs(0) // 2

    @pl.when(step // half == core_ref[0])
    def mine():
        out[...] = rows.astype(LOW)

    cot = cot_ref[...].astype(F32)
    grads = norm_backward(cot, unit, inverse, gain)
    grad[...] = grads
    low_rows = grads.astype(LOW)
    low[...] = low_rows
    totals = [jnp.sum(v, axis=0, keepdims=True) for v in (low_rows.astype(F32), cot * unit, cot)]
    branch = None
    for s in range(count):
        pre = (_nt(low_rows, w_out[s][...]) * slope[s][...].astype(F32)).astype(LOW)
        pre_grads[s][...] = pre
        term = _nt(pre, w_in[s][...])
        branch = term if branch is None else branch + term
        totals.append(jnp.sum(pre.astype(F32), axis=0, keepdims=True))
    row_part[...] = branch.astype(LOW)

    @pl.when(step == 0)
    def clear():
        sums[...] = jnp.zeros_like(sums)
        for s in range(count):
            pre_sums[s][...] = jnp.zeros_like(pre_sums[s])

    for at in range(3):
        sums[at : at + 1] += totals[at]
    for s in range(count):
        pre_sums[s][...] += totals[3 + s]


def feed_backward(core, part, got, normed, cot, vectors, slope, w_in, w_out, bq=256):
    count = len(w_in)
    rows, model = part.shape
    units = w_in[0].shape[1]
    half = rows // bq // 2
    wide = pl.BlockSpec((bq, units), lambda i, c: (i, 0))
    block = pl.BlockSpec((bq, model), lambda i, c: (i, 0))
    held = lambda shape: pl.BlockSpec(shape, lambda i, c: (0, 0))
    shape = jax.ShapeDtypeStruct
    out = pl.pallas_call(
        functools.partial(feed_back_kernel, count, residual_scale),
        out_shape=[shape((rows // 2, model), LOW), shape((rows, model), LOW), shape((rows, model), F32), shape((rows, model), LOW), shape((8, model), F32)]
        + [shape((rows, units), LOW)] * count + [shape((1, units), F32)] * count,
        grid_spec=pltpu.PrefetchScalarGridSpec(
            num_scalar_prefetch=1,
            grid=(rows // bq,),
            in_specs=[block, block, block, block, held((3, model))] + [wide] * count + [held(array.shape) for array in (*w_in, *w_out)],
            out_specs=[pl.BlockSpec((bq, model), lambda i, c: (jnp.clip(i - half * c[0], 0, half - 1), 0)), block, block, block, held((8, model))] + [wide] * count + [held((1, units))] * count,
        ),
        compiler_params=pltpu.CompilerParams(dimension_semantics=("arbitrary",), vmem_limit_bytes=54 << 20),
        cost_estimate=pl.CostEstimate(flops=4 * count * rows * model * units, bytes_accessed=30 << 20, transcendentals=0),
        name="feed_backward",
    )(core, part, got, normed, cot, vectors, *slope, *w_in, *w_out)
    return out[0], out[1], out[2], out[3], out[4][:3], out[5 : 5 + count], out[5 + count :]


residual_scale = 300.0**0.25
norm_epsilon = 1e-05
LOW = jnp.bfloat16
F32 = jnp.float32


def tn(rows, grads):
    return lax.dot_general(rows, grads, (((0,), (0,)), ((), ())), preferred_element_type=F32)


def norm_forward(summed, gain_row, shift_row):
    row_mean = jnp.mean(summed, axis=-1, keepdims=True)
    centred = summed - row_mean
    variance = jnp.mean(centred * centred, axis=-1, keepdims=True)
    inverse = lax.rsqrt(variance + norm_epsilon)
    unit_rows = centred * inverse
    return unit_rows * gain_row + shift_row, unit_rows, inverse


def norm_backward(grad_out, unit_rows, inverse, gain_row):
    grad_unit = grad_out * gain_row
    first_mean = jnp.mean(grad_unit, axis=-1, keepdims=True)
    second_mean = jnp.mean(grad_unit * unit_rows, axis=-1, keepdims=True)
    return inverse * (grad_unit - first_mean - unit_rows * second_mean)


def layer(sizes, tokens, memory, cotangent, target_lengths, memory_lengths, self_inputs, self_output, cross_query, cross_memory, cross_output, feed_in, feed_out, proj_bias, feed_bias, branch_bias, norm_gain, norm_shift):
    zn, yn, gn, cn = sizes
    seq = lax.axis_index("g")
    core = lax.axis_index("c")
    width = self_output.shape[0]
    joined = width % 128 != 0

    def swap(rows):
        return lax.ppermute(rows, "c", [(0, 1), (1, 0)])

    def gather_rows(rows):
        if cn != 2:
            return lax.all_gather(rows, "c", axis=0, tiled=True)
        got = swap(rows)
        return jnp.where(core == 0, jnp.concatenate([rows, got]), jnp.concatenate([got, rows]))

    def sum_all(part):
        part = part.astype(LOW)
        if cn != 2:
            return lax.psum(part, "c").astype(F32)
        return part.astype(F32) + swap(part).astype(F32)

    def own_rows(rows):
        size = rows.shape[0] // cn
        return lax.dynamic_slice_in_dim(rows, core * size, size, 0)

    def sum_own(part):
        if cn != 2:
            return lax.psum_scatter(part.astype(LOW), "c", scatter_dimension=0, tiled=True).astype(F32)
        size = part.shape[0] // 2
        got = swap(lax.dynamic_slice_in_dim(part, (1 - core) * size, size, 0).astype(LOW))
        return lax.dynamic_slice_in_dim(part, core * size, size, 0) + got.astype(F32)

    def spread(shard, axis):
        every = [shard] + [lax.ppermute(shard, "g", [((i + k) % gn, i) for i in range(gn)]) for k in range(1, gn)]
        return [jnp.concatenate(every, axis=axis)] if joined else every

    def send_home(parts):
        total = parts[0]
        for k in range(1, gn):
            total = total + lax.ppermute(parts[k].astype(LOW), "g", [(i, (i + k) % gn) for i in range(gn)]).astype(F32)
        return total

    steps = [("y", 1, lax.axis_index("y"), yn)] if yn == 2 else []
    steps += [("z", 1 << b, lax.axis_index("z"), zn) for b in range((zn - 1).bit_length())]

    def pairwise(rows, axis, far, size):
        return lax.ppermute(rows, axis, [(i, i ^ far) for i in range(size)])

    def sum_groups(total):
        for axis, far, at, size in steps:
            half = total.shape[0] // 2
            bit = (at // far) % 2
            away = lax.dynamic_slice_in_dim(total, (1 - bit) * half, half, 0).astype(LOW)
            keep = lax.dynamic_slice_in_dim(total, bit * half, half, 0)
            total = keep + pairwise(away, axis, far, size).astype(F32)
        total = total.astype(LOW)
        for axis, far, at, size in reversed(steps):
            got = pairwise(total, axis, far, size)
            total = jnp.where((at // far) % 2 == 0, jnp.concatenate([total, got]), jnp.concatenate([got, total]))
        return total.astype(F32)

    def fetch_slices(shards):
        at = lax.axis_index("z") * yn + lax.axis_index("y")
        pieces = [lax.dynamic_slice_in_dim(shard, at * (shard.shape[0] // (zn * yn)), shard.shape[0] // (zn * yn), 0) for shard in shards]
        pieces = [jnp.stack(pieces)] if pieces[0].shape == pieces[1].shape else [piece[None] for piece in pieces]
        return [[lax.ppermute(piece, "g", [((i + k) % gn, i) for i in range(gn)]) for piece in pieces] for k in range(1, gn)]

    def spread_wide(shards, slices):
        every = [[shard] for shard in shards]
        for got in slices:
            whole = [rows for piece in got for rows in lax.all_gather(piece, ("z", "y"), axis=1, tiled=True)]
            for at, rows in enumerate(whole):
                every[at].append(rows)
        return [[jnp.concatenate(part, axis=1 - at)] if joined else part for at, part in enumerate(every)]

    def parts_of(values, axis):
        return jnp.split(values[0], gn, axis=axis) if joined else values

    target_length = lax.dynamic_slice_in_dim(target_lengths, seq, 1, 0)
    memory_length = lax.dynamic_slice_in_dim(memory_lengths, seq, 1, 0)

    def after(value, *needed):
        return lax.optimization_barrier((value,) + needed)[0]

    token_all = gather_rows(tokens)
    biases = spread(jnp.concatenate([proj_bias, feed_bias.reshape(-1, width)]), 1)
    feed_rows = feed_bias.shape[0] // width
    if joined:
        halves = jnp.split(biases[0], gn, axis=1)
        b_in = [jnp.concatenate([part[4:].reshape(-1) for part in halves])]
    else:
        b_in = [part[4:].reshape(-1) for part in biases]
    b_proj = [part[:4] for part in biases]
    slices = fetch_slices((feed_in, feed_out))
    w_self = spread(after(self_inputs, token_all), 2)
    self_q, self_k, self_v, self_mixed, self_lse = [], [], [], [], []
    shards = range(len(w_self))
    for s in shards:
        self_q.append((_nn(token_all, w_self[s][0]) + b_proj[s][0]).astype(LOW))
        self_k.append(_nn(token_all, w_self[s][1]).astype(LOW))
        self_v.append((_nn(token_all, w_self[s][2]) + b_proj[s][1]).astype(LOW))
        mixed, lse = attn_fwd(target_length, self_q[s], self_k[s], self_v[s], True)
        self_mixed.append(mixed)
        self_lse.append(lse)
    first = self_mixed[0]
    w_in, w_out = spread_wide((feed_in, feed_out), [[after(piece, first) for piece in got] for got in slices])
    w_self_out = spread(after(self_output, self_q[0]), 0)
    memory_all = gather_rows(after(memory, first))
    w_cross_mem = spread(after(cross_memory, first), 2)
    w_cross_q = spread(after(cross_query, first), 1)
    w_cross_out = spread(after(cross_output, first), 0)
    cot_all = gather_rows(after(cotangent, self_mixed[-1]))

    cross_k = [_nn(memory_all, w_cross_mem[s][0]).astype(LOW) for s in shards]
    cross_v = [(_nn(memory_all, w_cross_mem[s][1]) + b_proj[s][3]).astype(LOW) for s in shards]
    branch_one = sum_all(sum(_nn(self_mixed[s], w_self_out[s]) for s in shards)) + branch_bias[0]
    normed_one, unit_one, inverse_one = norm_forward(residual_scale * token_all.astype(F32) + branch_one, norm_gain[0], norm_shift[0])
    second = normed_one.astype(LOW)
    cross_q, cross_mixed, cross_lse = [], [], []
    for s in shards:
        rows_in = second if s == 0 else after(second, w_in[-1], w_out[-1])
        cross_q.append((_nn(rows_in, w_cross_q[s]) + b_proj[s][2]).astype(LOW))
        mixed, lse = attn_fwd(memory_length, cross_q[s], cross_k[s], cross_v[s], False)
        cross_mixed.append(mixed)
        cross_lse.append(lse)
    branch_two = sum_all(sum(_nn(cross_mixed[s], w_cross_out[s]) for s in shards)) + branch_bias[1]
    normed_two, unit_two, inverse_two = norm_forward(residual_scale * normed_one + branch_two, norm_gain[1], norm_shift[1])
    third = normed_two.astype(LOW)
    feed_part, hidden, slope = feed_forward(third, w_in, [b_in[s].reshape(1, -1) for s in shards], w_out)
    if cn == 2:
        vectors = jnp.stack([branch_bias[2], norm_gain[2], norm_shift[2]])
        block_out, low_three, grad_three, row_part, sums_three, grad_pre, feed_sums = feed_backward(core.reshape(1), feed_part, swap(feed_part), normed_two, cot_all, vectors, slope, w_in, w_out)
        feed_sums = [part.reshape(-1) for part in feed_sums]
    else:
        branch_three = sum_all(feed_part) + branch_bias[2]
        normed_three, unit_three, inverse_three = norm_forward(residual_scale * normed_two + branch_three, norm_gain[2], norm_shift[2])
        block_out = own_rows(normed_three.astype(LOW))
        cot = cot_all.astype(F32)
        grad_three = norm_backward(cot, unit_three, inverse_three, norm_gain[2])
        low_three = grad_three.astype(LOW)
        grad_pre = [(_nt(low_three, w_out[s]) * slope[s].astype(F32)).astype(LOW) for s in shards]
        row_part = sum(_nt(grad_pre[s], w_in[s]) for s in shards)
        sums_three = [jnp.sum(rows.astype(F32), axis=0) for rows in (low_three, cot * unit_three, cot)]
        feed_sums = [jnp.sum(grad_pre[s].astype(F32), axis=0) for s in shards]
    feed_out_parts = parts_of([tn(hidden[s], low_three) for s in shards], 0)
    feed_in_parts = parts_of([tn(third, grad_pre[s]) for s in shards], 1)
    def sums(rows):
        return jnp.sum(rows.astype(F32), axis=0)

    def low_pairs(*parts):
        return [(part[0].astype(LOW), part[1].astype(LOW)) for part in parts]

    in_kernel = (zn, yn, gn, cn, width, joined) == (4, 2, 2, 2, SPAN, False)
    if not in_kernel:
        grad_normed_two = residual_scale * grad_three + sum_all(row_part)
        grad_two = norm_backward(grad_normed_two, unit_two, inverse_two, norm_gain[1])
        low_two = grad_two.astype(LOW)
        sums_two = [sums(low_two), sums(grad_normed_two * unit_two), sums(grad_normed_two)]
    if in_kernel:
        per_shard = [(cross_q[s], cross_k[s], cross_v[s], cross_mixed[s], cross_lse[s]) for s in shards]
        row_part, memory_part, cross_sums, go_own, go_other, gq_own, gq_other, gm_own, gm_other, sums_two, grad_two, feed_out_sum, feed_in_sum = cross_back(
            memory_length, grad_three, row_part, unit_two, inverse_two, norm_gain[1:2], per_shard[0], per_shard[1], w_cross_out, second, memory_all, w_cross_q, w_cross_mem, low_pairs(feed_out_parts, feed_in_parts))
        cross_sums = [cross_sums[0, :2], cross_sums[1, :2]]
        grad_memory = memory_part
        sums_one = [jnp.zeros_like(norm_gain[0])] * 3
    else:
        feed_out_sum, feed_in_sum = [sum_groups(send_home(part)) for part in (feed_out_parts, feed_in_parts)]
        grad_cross_mixed = [_nt(low_two, w_cross_out[s]).astype(LOW) for s in shards]
        cross_out_parts = parts_of([tn(cross_mixed[s], low_two) for s in shards], 0)
        cross_dq, cross_dk, cross_dv = zip(*[attn_bwd(memory_length, cross_q[s], cross_k[s], cross_v[s], cross_mixed[s], grad_cross_mixed[s], cross_lse[s], False) for s in shards])
        grad_normed_one = residual_scale * grad_two + sum_all(sum(_nt(cross_dq[s], w_cross_q[s]) for s in shards))
        cross_parts = [parts_of([tn(rows, grads[s]) for s in shards], 1) for rows, grads in ((second, cross_dq), (memory_all, cross_dk), (memory_all, cross_dv))]
        grad_memory = sum_own(sum(_nt(cross_dk[s], w_cross_mem[s][0]) + _nt(cross_dv[s], w_cross_mem[s][1]) for s in shards)).astype(LOW)
        cross_sums = parts_of([jnp.stack([sums(cross_dq[s]), sums(cross_dv[s])]) for s in shards], 1)
    if not in_kernel:
        grad_one = norm_backward(grad_normed_one, unit_one, inverse_one, norm_gain[0])
        low_one = grad_one.astype(LOW)
        sums_one = [sums(low_one), sums(grad_normed_one * unit_one), sums(grad_normed_one)]
    model = tokens.shape[1]
    terms = jnp.stack([norm_sums[at] for at in range(3) for norm_sums in (sums_one, sums_two, sums_three)])
    feed_sums = parts_of(feed_sums, 0)
    if not in_kernel:
        grad_self_mixed = [_nt(low_one, w_self_out[s]).astype(LOW) for s in shards]
        self_out_parts = parts_of([tn(self_mixed[s], low_one) for s in shards], 0)
        self_dq, self_dk, self_dv = zip(*[attn_bwd(target_length, self_q[s], self_k[s], self_v[s], self_mixed[s], grad_self_mixed[s], self_lse[s], True) for s in shards])
        token_part = sum_own(sum(_nt(self_dq[s], w_self[s][0]) + _nt(self_dk[s], w_self[s][1]) + _nt(self_dv[s], w_self[s][2]) for s in shards))
        self_sums = parts_of([jnp.stack([sums(self_dq[s]), sums(self_dv[s])]) for s in shards], 1)
    else:
        self_sums = [jnp.zeros((2, width), F32)] * gn
    smalls = []
    for k in range(gn):
        small = lax.dynamic_slice_in_dim(terms, ((seq + k) % gn * cn + core) * width, width, 1)
        small = jnp.concatenate([small, self_sums[k], cross_sums[k], feed_sums[k].reshape(-1, width)])
        smalls.append(jnp.pad(small, ((0, 16 * zn * yn - small.shape[0]), (0, 0))))
    if in_kernel:
        per_shard = [(self_q[s], self_k[s], self_v[s], self_mixed[s], self_lse[s]) for s in shards]
        pairs = [(go_own, go_other), (gq_own, gq_other), (gm_own, gm_other)]
        grad_tokens, *sums_low = self_back(target_length, grad_two, row_part, unit_one, inverse_one, norm_gain[0:1], per_shard[0], per_shard[1], w_self_out, token_all, w_self, smalls, pairs)
    else:
        groups = [[cross_out_parts], cross_parts[:1], cross_parts[1:], [self_out_parts], [parts_of([tn(token_all, grads[s]) for s in shards], 1) for grads in (self_dq, self_dk, self_dv)], [smalls]]
        sums_low = [sum_groups(send_home([jnp.concatenate([part[k] for part in group]) for k in range(gn)])) for group in groups]
    cross_out_sum, cross_q_sum, cross_mem_sum, self_out_sum, self_in_sum, small = [rows.astype(F32) for rows in sums_low]
    feed_out_sum, feed_in_sum = feed_out_sum.astype(F32), feed_in_sum.astype(F32)
    if not in_kernel:
        grad_tokens = (residual_scale * own_rows(grad_one) + token_part).astype(LOW)
    return (block_out, grad_tokens, grad_memory, self_in_sum.reshape(3, model, width), self_out_sum, cross_q_sum, cross_mem_sum.reshape(2, model, width), cross_out_sum, feed_in_sum, feed_out_sum, small[9:13], small[13:13 + feed_rows].reshape(-1), small[0:3], small[3:6], small[6:9])


def solution(mesh):
    dp, mp = mesh.shape["dp"], mesh.shape["mp"]

    def whole(*args):
        yn = 2 if dp % 2 == 0 else 1
        gn = args[3].shape[0] // dp
        sizes = (dp // yn, yn, gn, mp // gn)
        fine = Mesh(mesh.devices.reshape(sizes), ("z", "y", "g", "c"))
        d, m = ("z", "y"), ("g", "c")
        rows, wide, tall = P(d + m, None), P(None, m), P(m, None)
        stack = P(None, None, m)
        in_specs = (rows, rows, rows, P(d), P(d), stack, tall, wide, stack, tall, wide, tall, wide, P(m), P(), P(), P())
        out_specs = (rows, rows, rows, stack, tall, wide, stack, tall, wide, tall, wide, P(m), wide, wide, wide)
        return jax.shard_map(functools.partial(layer, sizes), mesh=fine, in_specs=in_specs, out_specs=out_specs, check_vma=False)(*args)

    return whole
```
